32 devices in a mesh: dp: 4 (over y, x), fsdp: 8 (over z, core).
Axes of the slice: x: 2, y: 2, z: 4, core: 2. Of those that a mesh axis runs over, the one named last changes fastest.
Arguments:
- tokens_in: bfloat16 [32, 1024, 768], P(('dp', 'fsdp')), may hold values from -6 to 6
- ln1_gain: bfloat16 [768], P('fsdp'), may hold values from 0.5 to 1.5
- ln1_bias: bfloat16 [768], P('fsdp'), may hold values from -3 to 3
- ln2_gain: bfloat16 [768], P('fsdp'), may hold values from 0.5 to 1.5
- ln2_bias: bfloat16 [768], P('fsdp'), may hold values from -3 to 3
- qkv_weight: bfloat16 [768, 2304], P('fsdp'), may hold values from -0.21875 to 0.21875
- qkv_bias: bfloat16 [2304], P('fsdp'), may hold values from -2 to 2
- out_weight: bfloat16 [768, 768], P('fsdp'), may hold values from -0.625 to 0.625
- out_bias: bfloat16 [768], P('fsdp'), may hold values from -2 to 2
- up_weight: bfloat16 [768, 3072], P('fsdp'), may hold values from -0.21875 to 0.21875
- up_bias: bfloat16 [3072], P('fsdp'), may hold values from -2 to 2
- down_weight: bfloat16 [3072, 768], P('fsdp'), may hold values from -0.15625 to 0.15625
- down_bias: bfloat16 [768], P('fsdp'), may hold values from -2 to 2
- cotangent: bfloat16 [32, 1024, 768], P(('dp', 'fsdp')), may hold values from -6 to 6
- lengths: int32 [32], P(('dp', 'fsdp')), may hold values from 128 to 1024, as said below
- assignment: int32 [32], P(('dp', 'fsdp')), may hold values from 0 to 31, each once
- clip_bound: int32 [1], replicated, may hold values from 6 to 10
Outputs:
- mixed: bfloat16 [32, 1024, 768], P(('dp', 'fsdp'))
- tokens_grad: bfloat16 [32, 1024, 768], P(('dp', 'fsdp'))
- clip_scale: float32 [32], replicated
- ln1_gain_grad: float32 [768], P('fsdp')
- ln1_bias_grad: float32 [768], P('fsdp')
- ln2_gain_grad: float32 [768], P('fsdp')
- ln2_bias_grad: float32 [768], P('fsdp')
- qkv_weight_grad: float32 [768, 2304], P('fsdp')
- qkv_bias_grad: float32 [2304], P('fsdp')
- out_weight_grad: float32 [768, 768], P('fsdp')
- out_bias_grad: float32 [768], P('fsdp')
- up_weight_grad: float32 [768, 3072], P('fsdp')
- up_bias_grad: float32 [3072], P('fsdp')
- down_weight_grad: float32 [3072, 768], P('fsdp')
- down_bias_grad: float32 [768], P('fsdp')
The draws below stay inside these ranges and needn't reach their ends.
Inputs may be any that keep to these rules, and one draw needn't show every extreme that they name: `lengths`: every slot's length lies between 128 and 1024; both ends occur in every draw. `assignment`: each example number occurs once.
All inputs are finite; a program needn't handle non-finite values.
Results may differ from the reference program's by a relative error of at most 0.0095.
Values may be sent and summed in bfloat16 or wider, within the bound.
No kernel may reach another device: no remote copies, remote signals or barrier semaphores. Data moves between devices by JAX's collectives and lax.ppermute only.
A program may use at most 256 MiB of HBM per device.

```python
import jax
import jax.numpy as jnp
from jax import lax

D = 768
HEADS = 12
HEAD_DIM = 64
FF = 3072
ROT_DIM = 16
SEQ_SLOT = 1024
MIN_LEN = 128
EXAMPLES = 32


def draw_lengths(key, part):
    picked = jax.random.randint(key, (EXAMPLES,), MIN_LEN, SEQ_SLOT + 1)
    order = jax.random.permutation(jax.random.fold_in(key, 7), EXAMPLES)
    picked = picked.at[order[0]].set(SEQ_SLOT)
    picked = picked.at[order[1]].set(MIN_LEN)
    return picked.astype(jnp.int32)


def level_of(own_key, shape, pieces, smallest, largest):
    level = 1.0
    for axis_at, blocks in pieces:
        heights = jax.random.uniform(jax.random.fold_in(jax.random.fold_in(own_key, 6), axis_at), (blocks,), jnp.float32, smallest / len(pieces), largest / len(pieces))
        level = level * jnp.repeat(jnp.exp(heights), shape[axis_at] // blocks).reshape((-1,) + (1,) * (len(shape) - 1 - axis_at))
    return level


def noise(key, dims, width, most, shards=(), kind=jnp.bfloat16):
    array = width * jax.random.normal(key, dims, jnp.float32)
    if shards:
        array = array * level_of(key, dims, shards, -0.22, 0.18)
    return jnp.clip(array, -most, most).astype(kind)


def setup_inputs(seed: int = 0) -> dict:
    keys = jax.random.split(jax.random.key(seed), 18)
    return {
        "tokens_in": noise(keys[0], (EXAMPLES, SEQ_SLOT, D), 1.0, 6.0, ((0, 32),)),
        "ln1_gain": jnp.clip(1.0 + 0.1 * jax.random.normal(keys[1], (D,), jnp.float32), 0.5, 1.5).astype(jnp.bfloat16),
        "ln1_bias": noise(keys[2], (D,), 0.5, 3.0, ((0, 8),)),
        "ln2_gain": jnp.clip(1.0 + 0.1 * jax.random.normal(keys[3], (D,), jnp.float32), 0.5, 1.5).astype(jnp.bfloat16),
        "ln2_bias": noise(keys[4], (D,), 0.5, 3.0, ((0, 8),)),
        "qkv_weight": noise(keys[5], (D, 3 * D), D ** -0.5, 0.21875, ((0, 8),)),
        "qkv_bias": noise(keys[6], (3 * D,), 0.3, 2.0, ((0, 8),)),
        "out_weight": noise(keys[7], (D, D), (D // 8) ** -0.5, 0.625, ((0, 8),)),
        "out_bias": noise(keys[8], (D,), 0.3, 2.0, ((0, 8),)),
        "up_weight": noise(keys[9], (D, FF), D ** -0.5, 0.21875, ((0, 8),)),
        "up_bias": noise(keys[10], (FF,), 0.3, 2.0, ((0, 8),)),
        "down_weight": noise(keys[11], (FF, D), (FF // 2) ** -0.5, 0.15625, ((0, 8),)),
        "down_bias": noise(keys[12], (D,), 0.3, 2.0, ((0, 8),)),
        "cotangent": noise(keys[13], (EXAMPLES, SEQ_SLOT, D), 1.0, 6.0, ((0, 32),)),
        "lengths": draw_lengths(jax.random.fold_in(keys[17], 71), 0),
        "assignment": jax.random.permutation(keys[15], EXAMPLES).astype(jnp.int32),
        "clip_bound": jax.random.randint(keys[16], (1,), 6, 11).astype(jnp.int32),
    }


@jax.custom_vjp
def low(v):
    return lax.optimization_barrier(v.astype(jnp.bfloat16)).astype(jnp.float32)

@jax.custom_vjp
def low_back(v):
    return v

def low_keep(v):
    return (low(v), None)

def low_pass(kept, grad):
    return (grad,)

def back_keep(v):
    return (v, None)

def back_low(kept, grad):
    return (low(grad),)
low.defvjp(low_keep, low_pass)
low_back.defvjp(back_keep, back_low)

def matmul(left, right):
    return jnp.dot(left, right, precision=lax.Precision.HIGHEST)

def norm_rows(values, gain, shift):
    row_mean = lax.optimization_barrier(jnp.mean(values, -1, keepdims=True))
    centred = values - row_mean
    variance = lax.optimization_barrier(jnp.mean(centred * centred, -1, keepdims=True))
    return centred * lax.rsqrt(variance + 1e-05) * gain + shift

def rotary_tables(count):
    positions = jnp.arange(count).astype(jnp.float32)
    inverse = 10000.0 ** (-jnp.arange(0, ROT_DIM, 2).astype(jnp.float32) / ROT_DIM)
    angles = positions[:, None] * inverse[None, :]
    angles = jnp.concatenate([angles, angles], -1)
    return (jnp.cos(angles)[:, None, :], jnp.sin(angles)[:, None, :])

def rotate_part(block, cosine, sine):
    half_dim = ROT_DIM // 2
    front = block[..., :ROT_DIM]
    turned = jnp.concatenate([-front[..., half_dim:], front[..., :half_dim]], -1)
    return jnp.concatenate([front * cosine + turned * sine, block[..., ROT_DIM:]], -1)

def layer(params, tokens, length):
    gain_first, shift_first, gain_second, shift_second, weight_qkv, bias_qkv, weight_out, bias_out, weight_up, bias_up, weight_down, bias_down = params
    count = tokens.shape[0]
    first = low(norm_rows(tokens, gain_first, shift_first))
    second = low(norm_rows(tokens, gain_second, shift_second))
    packed = low_back(matmul(first, weight_qkv) + bias_qkv).reshape(count, HEADS, 3 * HEAD_DIM)
    cosine, sine = rotary_tables(count)
    queries = low(rotate_part(packed[..., :HEAD_DIM], cosine, sine))
    keys_rot = low(rotate_part(packed[..., HEAD_DIM:2 * HEAD_DIM], cosine, sine))
    values_all = low(packed[..., 2 * HEAD_DIM:])
    scores = jnp.einsum('qhd,khd->hqk', queries, keys_rot, precision=lax.Precision.HIGHEST) * HEAD_DIM ** (-0.5)
    scores = low_back(scores)
    positions = jnp.arange(count).astype(jnp.int32)
    allowed = (positions[None, :] <= positions[:, None]) & (positions[None, :] < length)
    scores = jnp.where(allowed[None], scores, -1e+30)
    weights = low(jax.nn.softmax(scores, -1))
    heads_out = jnp.einsum('hqk,khd->qhd', weights, values_all, precision=lax.Precision.HIGHEST).reshape(count, D)
    heads_out = low(low_back(heads_out))
    attention = matmul(heads_out, weight_out) + bias_out
    inner = low_back(matmul(second, weight_up) + bias_up)
    activated = low(jax.nn.gelu(inner, approximate=False))
    feed = matmul(activated, weight_down) + bias_down
    valid_rows = (positions < length).astype(jnp.float32)[:, None]
    return valid_rows * (tokens + attention + feed)

def example(params, tokens, cot, length):
    output, pullback = jax.vjp(lambda weights, inputs: layer(weights, inputs, length), params, tokens)
    grads, token_grad = pullback(cot)
    squares = sum((jnp.sum(entry * entry) for entry in grads))
    return (output, grads, token_grad, squares)

def reference(tokens_in, ln1_gain, ln1_bias, ln2_gain, ln2_bias, qkv_weight, qkv_bias, out_weight, out_bias, up_weight, up_bias, down_weight, down_bias, cotangent, lengths, assignment, clip_bound):
    params = tuple((entry.astype(jnp.float32) for entry in (ln1_gain, ln1_bias, ln2_gain, ln2_bias, qkv_weight, qkv_bias, out_weight, out_bias, up_weight, up_bias, down_weight, down_bias)))
    inputs = tokens_in.astype(jnp.float32)
    cotangents = cotangent.astype(jnp.float32)

    def first_pass(element):
        tokens, cot, length = element
        output, grads, token_grad, squares = example(params, tokens, cot, length)
        return (output.astype(jnp.bfloat16), token_grad, squares)
    mixed, token_grads, squares = lax.map(first_pass, (inputs, cotangents, lengths))
    norms = jnp.zeros((EXAMPLES,), jnp.float32).at[assignment].set(jnp.sqrt(squares))
    median = jnp.sort(norms)[EXAMPLES // 2]
    bound = median * clip_bound[0].astype(jnp.float32) / 8.0
    clip_scale = jnp.minimum(1.0, bound / (norms + 1e-06))
    factors = clip_scale[assignment]
    tokens_grad = (factors[:, None, None] * token_grads).astype(jnp.bfloat16)

    def second_pass(carry, element):
        tokens, cot, length, factor = element
        output, grads, token_grad, squares_one = example(params, tokens, cot, length)
        weight_scale = factor / EXAMPLES
        return (tuple((running + weight_scale * gradient for running, gradient in zip(carry, grads))), None)
    zeros = tuple((jnp.zeros(entry.shape, jnp.float32) for entry in params))
    totals, unused = lax.scan(second_pass, zeros, (inputs, cotangents, lengths, factors))
    return (mixed, tokens_grad, clip_scale, totals[0], totals[1], totals[2], totals[3], totals[4], totals[5], totals[6], totals[7], totals[8], totals[9], totals[10], totals[11])
```

```python
import functools
import math

import jax
import jax.numpy as jnp
from jax import lax
from jax.experimental import pallas as pl
from jax.experimental.pallas import tpu as pltpu
from jax.sharding import PartitionSpec as P

HEAD_DIM = 64
ROT_DIM = 16
LANES = 128
f32 = jnp.float32
bf16 = jnp.bfloat16
VMEM_LIMIT = 60 * 2**20


def nn(left, right):
    return lax.dot_general(left, right, (((1,), (0,)), ((), ())), preferred_element_type=f32)


def nt(left, right):
    return lax.dot_general(left, right, (((1,), (1,)), ((), ())), preferred_element_type=f32)


def tn(left, right):
    return lax.dot_general(left, right, (((0,), (0,)), ((), ())), preferred_element_type=f32)


def fold(row):
    total = row[:, 0:LANES]
    for start in range(LANES, row.shape[1], LANES):
        total = total + row[:, start : start + LANES]
    return total


def fixed(shape):
    return pl.BlockSpec(shape, lambda *_: (0,) * len(shape), pipeline_mode=pl.Buffered(1))


def params():
    return pltpu.CompilerParams(vmem_limit_bytes=VMEM_LIMIT)


def store_rows(value, coords, keep_ref, send_ref):
    rows = value.shape[0] // 8
    half = rows // 2
    first = coords[0] == 0
    for z in range(4):
        even = value[2 * z * rows : (2 * z + 1) * rows].astype(bf16)
        odd = value[(2 * z + 1) * rows : (2 * z + 2) * rows].astype(bf16)
        kept = jnp.where(first, even, odd)
        sent = jnp.where(first, odd, even)
        for y in range(2):
            for t in range(value.shape[1] // LANES):
                at = (0, y ^ coords[2], z ^ coords[3], t)
                lanes = slice(t * LANES, (t + 1) * LANES)
                keep_ref[at] = kept[y * half : (y + 1) * half, lanes]
                send_ref[at] = sent[y * half : (y + 1) * half, lanes]


def qkv_kernel(x_ref, ln_ref, w_ref, b_ref, c_ref, sa_ref, sb_ref, h1_ref, h2_ref, o_ref):
    x = x_ref[...].astype(f32)
    centred = x - jnp.mean(x, -1, keepdims=True)
    normed = centred * lax.rsqrt(jnp.mean(centred * centred, -1, keepdims=True) + 1e-05)
    h1 = (normed * ln_ref[0:1, :] + ln_ref[1:2, :]).astype(bf16)
    h2_ref[...] = (normed * ln_ref[2:3, :] + ln_ref[3:4, :]).astype(bf16)
    h1_ref[...] = h1
    width = x.shape[1]
    cosine, ahead, behind = c_ref[...], sa_ref[...], sb_ref[...]
    low = lax.broadcasted_iota(jnp.int32, (1, LANES), 1) < HEAD_DIM

    def turn(y):
        return y * cosine - pltpu.roll(y * ahead, LANES - 8, 1) - pltpu.roll(y * behind, 8, 1)

    for part in range(3):
        cols = slice(part * width, (part + 1) * width)
        y = nn(h1, w_ref[:, cols]) + b_ref[:, cols]
        for pair in range(2):
            base = pair * 3 * LANES
            t0 = y[:, base : base + LANES]
            t1 = y[:, base + LANES : base + 2 * LANES]
            t2 = y[:, base + 2 * LANES : base + 3 * LANES]
            queries = turn(jnp.where(low, t0, t1)) * (HEAD_DIM**-0.5)
            keys = turn(pltpu.roll(jnp.where(low, t2, t0), HEAD_DIM, 1))
            at = (2 * part + pair) * LANES
            o_ref[:, at : at + LANES] = queries.astype(bf16)
            o_ref[:, width + at : width + at + LANES] = keys.astype(bf16)
            o_ref[:, 2 * width + at : 2 * width + at + LANES] = jnp.where(low, t1, t2).astype(bf16)


def qkv_forward(x, ln, weight, bias, tables, rows=256):
    count, width = x.shape
    block = lambda n: pl.BlockSpec((rows, n), lambda i: (i, 0))
    return pl.pallas_call(
        qkv_kernel,
        grid=(count // rows,),
        in_specs=[block(width), fixed(ln.shape), fixed(weight.shape), fixed(bias.shape)]
        + [block(LANES)] * 3,
        out_specs=[block(width), block(width), block(3 * width)],
        out_shape=[
            jax.ShapeDtypeStruct((count, width), bf16),
            jax.ShapeDtypeStruct((count, width), bf16),
            jax.ShapeDtypeStruct((count, 3 * width), bf16),
        ],
        compiler_params=params(),
        cost_estimate=pl.CostEstimate(
            flops=6 * count * width * width, bytes_accessed=14 * 2**20, transcendentals=0
        ),
        name="qkv_forward",
    )(x, ln, weight, bias, *tables)


def rotary_tables(count):
    positions = jnp.arange(count).astype(f32)
    inverse = 10000.0 ** (-jnp.arange(0, ROT_DIM, 2).astype(f32) / ROT_DIM)
    angles = positions[:, None] * inverse[None, :]
    cosine, sine = jnp.cos(angles), jnp.sin(angles)
    rest = HEAD_DIM - ROT_DIM
    one, zero, none = jnp.ones((count, rest), f32), jnp.zeros((count, rest), f32), jnp.zeros_like(sine)
    return (
        jnp.concatenate([cosine, cosine, one] * 2, -1),
        jnp.concatenate([none, sine, zero] * 2, -1),
        jnp.concatenate([-sine, none, zero] * 2, -1),
    )


def attention_kernel(
    q_ref, k_ref, v_ref, cot_ref, w_ref, c_ref, sa_ref, sb_ref, a_ref, dqkv_ref, dq, dkt, dvt, *, rows
):
    count = q_ref.shape[0]
    blocks = count // rows
    low = lax.broadcasted_iota(jnp.int32, (1, LANES), 1) < HEAD_DIM
    causal = lax.broadcasted_iota(jnp.int32, (rows, rows), 1) <= lax.broadcasted_iota(
        jnp.int32, (rows, rows), 0
    )

    def unturn(y):
        return (
            y * c_ref[...]
            + pltpu.roll(y * sa_ref[...], LANES - 8, 1)
            + pltpu.roll(y * sb_ref[...], 8, 1)
        )

    for i in reversed(range(blocks)):
        before = rows * i
        here = slice(before, before + rows)
        past = slice(0, before)
        q = q_ref[here, :]
        da = nt(cot_ref[here, :], w_ref[...]).astype(bf16)
        q_turned, da_turned = q.T, da.T
        outs, grads = [], []
        for h in range(2):
            mine = low if h == 0 else jnp.logical_not(low)
            head = slice(HEAD_DIM * h, HEAD_DIM * (h + 1))
            qh = jnp.where(mine, q, jnp.zeros_like(q))
            dah = jnp.where(mine, da, jnp.zeros_like(da))
            s_here = jnp.where(causal, nt(qh, k_ref[here, :]), -1e30)
            highest = jnp.max(s_here, -1, keepdims=True)
            if before:
                s_past = nt(qh, k_ref[past, :])
                highest = jnp.maximum(highest, jnp.max(s_past, -1, keepdims=True))
                e_past = jnp.exp(s_past - highest)
            e_here = jnp.exp(s_here - highest)
            total = jnp.sum(e_here, -1, keepdims=True)
            if before:
                total = total + jnp.sum(e_past, -1, keepdims=True)
            inverse = 1.0 / total
            p_here = e_here * inverse
            l_here = p_here.astype(bf16)
            out = nn(l_here, v_ref[here, :])
            if before:
                p_past = e_past * inverse
                l_past = p_past.astype(bf16)
                out = out + nn(l_past, v_ref[past, :])
            row_dot = jnp.sum(jnp.where(mine, out * dah.astype(f32), 0.0), -1, keepdims=True)
            ds_here = (p_here * (nt(dah, v_ref[here, :]) - row_dot)).astype(bf16)
            grad = nn(ds_here, k_ref[here, :])
            if before:
                ds_past = (p_past * (nt(dah, v_ref[past, :]) - row_dot)).astype(bf16)
                grad = grad + nn(ds_past, k_ref[past, :])
            outs.append(out)
            grads.append(grad)
            qt, dat = q_turned[head, :], da_turned[head, :]
            if i == blocks - 1:
                dkt[head, here] = nn(qt, ds_here)
                dvt[head, here] = nn(dat, l_here)
                if before:
                    dkt[head, past] = nn(qt, ds_past)
                    dvt[head, past] = nn(dat, l_past)
            else:
                dkt[head, here] += nn(qt, ds_here)
                dvt[head, here] += nn(dat, l_here)
                if before:
                    dkt[head, past] += nn(qt, ds_past)
                    dvt[head, past] += nn(dat, l_past)
        a_ref[here, :] = jnp.where(low, outs[0], outs[1]).astype(bf16)
        dq[here, :] = jnp.where(low, grads[0], grads[1]) * (HEAD_DIM**-0.5)
    gq = unturn(dq[...])
    gk = pltpu.roll(unturn(dkt[...].T), HEAD_DIM, 1)
    gv = dvt[...].T
    dqkv_ref[:, 0:LANES] = jnp.where(low, gq, gk).astype(bf16)
    dqkv_ref[:, LANES : 2 * LANES] = jnp.where(low, gv, gq).astype(bf16)
    dqkv_ref[:, 2 * LANES : 3 * LANES] = jnp.where(low, gk, gv).astype(bf16)


def attention(qkv, cot, out_weight, tables, rows=256):
    count, width = cot.shape
    pairs = width // LANES
    column = lambda offset: pl.BlockSpec((count, LANES), lambda p: (0, offset + p))
    return pl.pallas_call(
        functools.partial(attention_kernel, rows=rows),
        grid=(pairs,),
        in_specs=[column(0), column(pairs), column(2 * pairs), fixed((count, width))]
        + [pl.BlockSpec((LANES, width), lambda p: (p, 0))]
        + [fixed((count, LANES))] * 3,
        out_specs=[column(0), pl.BlockSpec((count, 3 * LANES), lambda p: (0, p))],
        out_shape=[
            jax.ShapeDtypeStruct((count, width), bf16),
            jax.ShapeDtypeStruct((count, 3 * width), bf16),
        ],
        scratch_shapes=[
            pltpu.VMEM((count, LANES), f32),
            pltpu.VMEM((LANES, count), f32),
            pltpu.VMEM((LANES, count), f32),
        ],
        compiler_params=params(),
        cost_estimate=pl.CostEstimate(
            flops=30 * 10**9, bytes_accessed=20 * 2**20, transcendentals=8 * 10**6
        ),
        name="attention",
    )(qkv, qkv, qkv, cot, out_weight, *tables)


def feed_kernel(
    co_ref, h2_ref, cot_ref, up_ref, upb_ref, down_ref,
    g_ref, upk_ref, ups_ref, dnk_ref, dns_ref, ubg_ref, dh2_ref, sq_ref,
):
    j = pl.program_id(0)
    u = nn(h2_ref[...], up_ref[...]) + upb_ref[...]
    act = nt(cot_ref[...], down_ref[...])
    cdf = 0.5 * (1.0 + lax.erf(u * math.sqrt(0.5)))
    pdf = jnp.exp(-0.5 * u * u) * (1.0 / math.sqrt(2.0 * math.pi))
    g = (u * cdf).astype(bf16)
    du = (act * (cdf + u * pdf)).astype(bf16)
    g_ref[...] = g
    bias_grad = jnp.sum(du.astype(f32), 0, keepdims=True)
    ubg_ref[...] = bias_grad
    up_grad = tn(h2_ref[...], du)
    down_grad = tn(g, cot_ref[...])
    store_rows(up_grad, co_ref, upk_ref, ups_ref)
    x_mine = co_ref[1]
    for unit in range(2):
        place = 2 * (j % 3) + unit
        core, sub = place // 3, place % 3
        rows = down_grad[unit * LANES : (unit + 1) * LANES].astype(bf16)
        half = LANES // 2

        def put(ref):
            for x in range(2):
                for y in range(2):
                    for t in range(3):
                        lanes = slice((3 * x + t) * LANES, (3 * x + t + 1) * LANES)
                        ref[x ^ x_mine, y ^ co_ref[2], 0, sub, t] = rows[y * half : (y + 1) * half, lanes]

        pl.when(core == co_ref[0])(lambda: put(dnk_ref))
        pl.when(core != co_ref[0])(lambda: put(dns_ref))
    part = nt(du, up_ref[...])

    @pl.when(j == 0)
    def _():
        dh2_ref[...] = part
        sq_ref[...] = jnp.zeros_like(sq_ref)

    @pl.when(j > 0)
    def _():
        dh2_ref[...] += part

    sq_ref[0:1, :] += fold(
        jnp.sum(up_grad * up_grad, 0, keepdims=True) + bias_grad * bias_grad
    ) + fold(jnp.sum(down_grad * down_grad, 0, keepdims=True))


def feed(coords, h2, cot, up, up_bias, down, tile=256):
    count, width = h2.shape
    hidden = up.shape[1]
    per_x = hidden // 2 // tile
    tiles = tile // LANES
    up_piece = jax.ShapeDtypeStruct((2, 2, 4, hidden // 2 // LANES, width // 16, LANES), bf16)
    down_piece = jax.ShapeDtypeStruct((2, 2, 4, 3, width // 2 // LANES, LANES // 2, LANES), bf16)
    up_spec = pl.BlockSpec(
        (1, 2, 4, tiles, width // 16, LANES),
        lambda j, co: ((j // per_x) ^ co[1], 0, 0, j % per_x, 0, 0),
    )
    down_spec = pl.BlockSpec(
        (2, 2, 1) + down_piece.shape[3:], lambda j, co: (0, 0, (j // 3) ^ co[3], 0, 0, 0, 0)
    )
    return pl.pallas_call(
        feed_kernel,
        grid_spec=pltpu.PrefetchScalarGridSpec(
            num_scalar_prefetch=1,
            grid=(hidden // tile,),
            in_specs=[
                fixed((count, width)),
                fixed((count, width)),
                pl.BlockSpec((width, tile), lambda j, co: (0, j)),
                pl.BlockSpec((1, tile), lambda j, co: (0, j)),
                pl.BlockSpec((tile, width), lambda j, co: (j, 0)),
            ],
            out_specs=[
                pl.BlockSpec((count, tile), lambda j, co: (0, j)),
                up_spec,
                up_spec,
                down_spec,
                down_spec,
                pl.BlockSpec((1, tile), lambda j, co: (0, j)),
                pl.BlockSpec((count, width), lambda j, co: (0, 0)),
                pl.BlockSpec((8, LANES), lambda j, co: (0, 0)),
            ],
        ),
        out_shape=[
            jax.ShapeDtypeStruct((count, hidden), bf16),
            up_piece,
            up_piece,
            down_piece,
            down_piece,
            jax.ShapeDtypeStruct((1, hidden), f32),
            jax.ShapeDtypeStruct((count, width), f32),
            jax.ShapeDtypeStruct((8, LANES), f32),
        ],
        compiler_params=params(),
        cost_estimate=pl.CostEstimate(
            flops=10 * count * width * hidden, bytes_accessed=32 * 2**20, transcendentals=8 * 10**6
        ),
        name="feed",
    )(coords, h2, cot, up, up_bias, down)


def grad_kernel(co_ref, left_ref, right_ref, w_ref, keep_ref, send_ref, bias_ref, back_ref, sq_ref):
    j = pl.program_id(0)
    right = right_ref[...]
    grad = tn(left_ref[...], right)
    bias_grad = jnp.sum(right.astype(f32), 0, keepdims=True)
    bias_ref[...] = bias_grad
    store_rows(grad, co_ref, keep_ref, send_ref)
    part = nt(right, w_ref[...])

    @pl.when(j == 0)
    def _():
        back_ref[...] = part
        sq_ref[...] = jnp.zeros_like(sq_ref)

    @pl.when(j > 0)
    def _():
        back_ref[...] += part

    sq_ref[0:1, :] += fold(jnp.sum(grad * grad, 0, keepdims=True) + bias_grad * bias_grad)


def plain_grad_kernel(co_ref, left_ref, right_ref, keep_ref, send_ref, bias_ref, sq_ref):
    right = right_ref[...]
    grad = tn(left_ref[...], right)
    bias_grad = jnp.sum(right.astype(f32), 0, keepdims=True)
    bias_ref[...] = bias_grad
    store_rows(grad, co_ref, keep_ref, send_ref)

    @pl.when(pl.program_id(0) == 0)
    def _():
        sq_ref[...] = jnp.zeros_like(sq_ref)

    sq_ref[0:1, :] += fold(jnp.sum(grad * grad, 0, keepdims=True) + 2.0 * bias_grad * bias_grad)


def weight_grad(coords, left, right, weight=None, tile=384):
    count, width = left.shape
    cols = right.shape[1]
    per_x = cols // 2 // tile
    piece = jax.ShapeDtypeStruct((2, 2, 4, cols // 2 // LANES, width // 16, LANES), bf16)
    spec = pl.BlockSpec(
        (1, 2, 4, tile // LANES, width // 16, LANES),
        lambda j, co: ((j // per_x) ^ co[1], 0, 0, j % per_x, 0, 0),
    )
    back = [] if weight is None else [weight]
    return pl.pallas_call(
        plain_grad_kernel if weight is None else grad_kernel,
        grid_spec=pltpu.PrefetchScalarGridSpec(
            num_scalar_prefetch=1,
            grid=(cols // tile,),
            in_specs=[fixed((count, width)), pl.BlockSpec((count, tile), lambda j, co: (0, j))]
            + [pl.BlockSpec((width, tile), lambda j, co: (0, j))] * len(back),
            out_specs=[spec, spec, pl.BlockSpec((1, tile), lambda j, co: (0, j))]
            + [pl.BlockSpec((count, width), lambda j, co: (0, 0))] * len(back)
            + [pl.BlockSpec((8, LANES), lambda j, co: (0, 0))],
        ),
        out_shape=[piece, piece, jax.ShapeDtypeStruct((1, cols), f32)]
        + [jax.ShapeDtypeStruct((count, width), f32)] * len(back)
        + [jax.ShapeDtypeStruct((8, LANES), f32)],
        compiler_params=params(),
        cost_estimate=pl.CostEstimate(
            flops=2 * (1 + len(back)) * count * width * cols,
            bytes_accessed=16 * 2**20,
            transcendentals=0,
        ),
        name="weight_grad",
    )(coords, left, right, *back)


def norm_back_kernel(x_ref, cot_ref, dh1_ref, dh2_ref, ln_ref, dx_ref, sums_ref):
    x = x_ref[...].astype(f32)
    centred = x - jnp.mean(x, -1, keepdims=True)
    inverse = lax.rsqrt(jnp.mean(centred * centred, -1, keepdims=True) + 1e-05)
    normed = centred * inverse
    dh1, dh2 = dh1_ref[...], dh2_ref[...]
    scaled = dh1 * ln_ref[0:1, :] + dh2 * ln_ref[2:3, :]
    spread = (
        scaled
        - jnp.mean(scaled, -1, keepdims=True)
        - normed * jnp.mean(scaled * normed, -1, keepdims=True)
    )
    dx_ref[...] = cot_ref[...].astype(f32) + inverse * spread

    @pl.when(pl.program_id(0) == 0)
    def _():
        sums_ref[...] = jnp.zeros_like(sums_ref)

    for row, value in enumerate((dh1 * normed, dh1, dh2 * normed, dh2)):
        sums_ref[row : row + 1, :] += jnp.sum(value, 0, keepdims=True)


def norm_back(x, cot, dh1, dh2, ln, rows=256):
    count, width = x.shape
    block = pl.BlockSpec((rows, width), lambda i: (i, 0))
    return pl.pallas_call(
        norm_back_kernel,
        grid=(count // rows,),
        in_specs=[block] * 4 + [fixed(ln.shape)],
        out_specs=[block, pl.BlockSpec((8, width), lambda i: (0, 0))],
        out_shape=[
            jax.ShapeDtypeStruct((count, width), f32),
            jax.ShapeDtypeStruct((8, width), f32),
        ],
        compiler_params=params(),
        cost_estimate=pl.CostEstimate(
            flops=30 * count * width, bytes_accessed=12 * 2**20, transcendentals=0
        ),
        name="norm_back",
    )(x, cot, dh1, dh2, ln)


def body(
    tokens_in, ln1_gain, ln1_bias, ln2_gain, ln2_bias, qkv_weight, qkv_bias, out_weight, out_bias,
    up_weight, up_bias, down_weight, down_bias, cotangent, lengths, assignment, clip_bound,
):
    dp, fsdp = lax.axis_size("dp"), lax.axis_size("fsdp")
    both = ("dp", "fsdp")
    total = dp * fsdp
    fast = (dp, fsdp) == (4, 8)
    me = lax.axis_index("dp") * fsdp + lax.axis_index("fsdp")

    def swap(value, bit):
        return lax.ppermute(value, both, [(i, i ^ bit) for i in range(total)])

    def spread_sum(value, bits):
        for bit in bits:
            value = value + swap(value, bit)
        return value

    smalls = (ln1_gain, ln1_bias, ln2_gain, ln2_bias, qkv_bias, out_bias, up_bias, down_bias)
    packed = jnp.concatenate(smalls)
    if fast:
        slot = lax.broadcasted_iota(jnp.int32, (fsdp, 1), 0) == lax.axis_index("fsdp")
        rows = jnp.where(slot, packed[None, :], jnp.zeros_like(packed)[None, :])
        rows = spread_sum(rows, (1, 2, 4))
    else:
        rows = lax.all_gather(packed, "fsdp", axis=0)
    vectors, start = [], 0
    for entry in smalls:
        stop = start + entry.shape[0]
        vectors.append(rows[:, start:stop].reshape(1, -1).astype(f32))
        start = stop
    ln = jnp.concatenate(vectors[:4] + [jnp.zeros((4, vectors[0].shape[1]), f32)], 0)
    qkv_b, out_b, up_b, down_b = vectors[4:]

    gather = lambda w: lax.all_gather(w, "fsdp", axis=0, tiled=True)
    w_qkv, w_out, w_up, w_down = (gather(w) for w in (qkv_weight, out_weight, up_weight, down_weight))

    if fast:
        coords = jnp.stack([me & 1, (me >> 3) & 1, (me >> 4) & 1, (me >> 1) & 3]).astype(jnp.int32)
    else:
        coords = jnp.zeros((4,), jnp.int32)

    tokens = tokens_in[0]
    count, width = tokens.shape
    valid = lax.broadcasted_iota(jnp.int32, (count, 1), 0) < lengths[0]
    cot = jnp.where(valid, cotangent[0], jnp.zeros_like(cotangent[0]))
    tables = rotary_tables(count)

    h1, h2, qkv = qkv_forward(tokens, ln, w_qkv, qkv_b, tables)
    heads, dqkv = attention(qkv, cot, w_out, tables)
    out_keep, out_send, cot_sum, out_sq = weight_grad(coords, heads, cot)
    qkv_keep, qkv_send, qkv_bias_grad, dh1, qkv_sq = weight_grad(coords, h1, dqkv, w_qkv)
    act, up_keep, up_send, down_keep, down_send, up_bias_grad, dh2, feed_sq = feed(
        coords, h2, cot, w_up, up_b, w_down
    )
    dx, ln_sums = norm_back(tokens, cot, dh1, dh2, ln)
    ln_grads = ln_sums[:4]

    squares = jnp.sum(out_sq + qkv_sq + feed_sq) + jnp.sum(ln_grads * ln_grads)
    mine = jnp.arange(total, dtype=jnp.int32) == assignment[0]
    held = jnp.where(mine, squares, 0.0)
    squares_all = spread_sum(held, (1, 2, 4, 8, 16)) if fast else lax.psum(held, both)
    norms = jnp.sqrt(squares_all)
    order = jnp.arange(total)
    ahead = (norms[None, :] < norms[:, None]) | (
        (norms[None, :] == norms[:, None]) & (order[None, :] < order[:, None])
    )
    rank = jnp.sum(ahead.astype(jnp.int32), 1)
    median = jnp.sum(jnp.where(rank == total // 2, norms, 0.0))
    bound = median * clip_bound[0].astype(f32) / 8.0
    clip_scale = jnp.minimum(1.0, bound / (norms + 1e-06))
    own = jnp.sum(jnp.where(mine, clip_scale, 0.0))
    share = own / total

    mixed = (
        tokens.astype(f32)
        + (nn(heads, w_out) + out_b)
        + (nn(act, w_down) + down_b)
    )
    mixed = jnp.where(valid, mixed, 0.0).astype(bf16)[None]
    tokens_grad = (own * dx).astype(bf16)[None]

    small_grads = jnp.concatenate(
        [ln_grads.reshape(-1), qkv_bias_grad[0], cot_sum[0], up_bias_grad[0]]
    ).reshape(-1, LANES)
    small_grads = small_grads * share
    small_grads = spread_sum(small_grads, (1, 2, 4, 8, 16)) if fast else lax.psum(small_grads, both)
    small_grads = small_grads.reshape(-1)

    def part(first, length):
        piece = small_grads[first : first + length].reshape(fsdp, length // fsdp)
        return lax.dynamic_index_in_dim(piece, lax.axis_index("fsdp"), 0, keepdims=False)

    offsets = [(i * width, width) for i in range(4)]
    offsets += [(4 * width, 3 * width), (7 * width, width), (8 * width, up_b.shape[1])]
    g1, b1, g2, b2, gqb, gob, gub = (part(*o) for o in offsets)

    pieces = (
        (qkv_keep, qkv_send), (out_keep, out_send), (up_keep, up_send), (down_keep, down_send)
    )

    if fast:
        other = jnp.sum(jnp.where(jnp.arange(total) == swap(assignment, 1)[0], clip_scale, 0.0)) / total
        finals = []
        for keep, send in pieces:
            recv = swap(send, 1)
            add = lambda a, b: (a.astype(f32) + b.astype(f32)).astype(bf16)
            summed = lambda at: (share * keep[at].astype(f32) + other * recv[at].astype(f32)).astype(bf16)
            near, far = slice(0, 2), slice(2, 4)
            near_sum = add(summed((0, slice(None), near)), swap(summed((1, slice(None), near)), 8))
            far_sum = add(summed((slice(None), 0, far)), swap(summed((slice(None), 1, far)), 16))
            near_sum = add(near_sum[0], swap(near_sum[1], 16))
            far_sum = add(far_sum[0], swap(far_sum[1], 8))
            line = add(near_sum, swap(far_sum, 4))
            line = add(line[0], swap(line[1], 2))
            row = jnp.stack([line, swap(line, 8)])
            finals.append(jnp.stack([row, swap(row, 16)], 1))
        x_mine, y_mine = coords[1], coords[2]
        outs = []
        for piece in finals:
            piece = jnp.where(x_mine == 0, piece, piece[::-1])
            piece = jnp.where(y_mine == 0, piece, piece[:, ::-1])
            outs.append(piece.astype(f32))
        gq, go, gu = (
            p.transpose(1, 3, 0, 2, 4).reshape(2 * p.shape[3], -1) for p in outs[:3]
        )
        gd = outs[3].transpose(2, 1, 4, 0, 3, 5).reshape(-1, width)
    else:
        outs = []
        for keep, send in pieces[:3]:
            whole = jnp.stack([keep, send])
            whole = whole.transpose(3, 0, 2, 5, 1, 4, 6).reshape(width, -1)
            outs.append((whole.astype(f32) * share).astype(bf16))
        whole = jnp.stack(pieces[3])
        whole = whole.transpose(3, 0, 4, 2, 6, 1, 5, 7).reshape(-1, width)
        outs.append((whole.astype(f32) * share).astype(bf16))
        gq, go, gu, gd = (
            lax.psum(
                lax.psum_scatter(w, "fsdp", scatter_dimension=0, tiled=True).astype(f32), "dp"
            )
            for w in outs
        )
    return (mixed, tokens_grad, clip_scale, g1, b1, g2, b2, gq, gqb, go, gob, gu, gub, gd, gob)


def solution(mesh):
    rows, cols, flat = P("fsdp", None), P("fsdp"), P(("dp", "fsdp"))
    slots = P(("dp", "fsdp"), None, None)
    return jax.shard_map(
        body,
        mesh=mesh,
        in_specs=(slots, cols, cols, cols, cols, rows, cols, rows, cols, rows, cols, rows, cols)
        + (slots, flat, flat, P()),
        out_specs=(slots, slots, P(), cols, cols, cols, cols, rows, cols, rows, cols, rows, cols)
        + (rows, cols),
        check_vma=False,
    )
```

```python
import functools
import math

import jax
import jax.numpy as jnp
from jax import lax
from jax.experimental import pallas as pl
from jax.experimental.pallas import tpu as pltpu
from jax.sharding import PartitionSpec as P


HEAD_DIM = 64
ROT_DIM = 16
LANES = 128
f32 = jnp.float32
bf16 = jnp.bfloat16
VMEM_LIMIT = 60 * 2**20


def nn(left, right):
    return lax.dot_general(left, right, (((1,), (0,)), ((), ())), preferred_element_type=f32)


def nt(left, right):
    return lax.dot_general(left, right, (((1,), (1,)), ((), ())), preferred_element_type=f32)


def tn(left, right):
    return lax.dot_general(left, right, (((0,), (0,)), ((), ())), preferred_element_type=f32)


def fold(row):
    total = row[:, 0:LANES]
    for start in range(LANES, row.shape[1], LANES):
        total = total + row[:, start : start + LANES]
    return total


def fixed(shape):
    return pl.BlockSpec(shape, lambda *_: (0,) * len(shape), pipeline_mode=pl.Buffered(1))


def params():
    return pltpu.CompilerParams(vmem_limit_bytes=VMEM_LIMIT)


def z_of(at, coords):
    return ((at % 2) * 2 + at // 2) ^ coords[3]


def z_at(z, coords):
    rel = z ^ coords[3]
    return (rel % 2) * 2 + rel // 2


def put_rows(scr, x, row, coords, refs, extra=()):
    half = scr.shape[0] // 16
    x_rel = x ^ coords[1]

    def put(c, near, pair):
        for z in range(4):
            shard = z_of(z, coords) * 2 + (c ^ coords[0])
            for y in range(2):
                start = pl.multiple_of((2 * shard + (y ^ coords[2])) * half, half)
                ref, s2 = (pair[0], y) if near else (pair[y], x_rel)
                for t in range(scr.shape[1] // LANES):
                    to = pl.ds(pl.multiple_of(row + t * half, half), half)
                    ref[(s2, z) + extra + (to, slice(None))] = scr[
                        pl.ds(start, half), t * LANES : (t + 1) * LANES
                    ]

    for c in range(2):
        kept, sent = refs[2 * c : 2 * c + 2]
        near = coords[0] == c
        pl.when(near & (x_rel == 0))(functools.partial(put, c, True, (kept,)))
        pl.when(near & (x_rel == 1))(functools.partial(put, c, True, (sent,)))
        pl.when(jnp.logical_not(near))(functools.partial(put, c, False, (kept, sent)))


def prepare_kernel(
    len_ref, x_ref, cot_ref, ln_ref, h1_ref, h2_ref, h1t_ref, h2t_ref, cotm_ref, cott_ref
):
    x = x_ref[...].astype(f32)
    centred = x - jnp.mean(x, -1, keepdims=True)
    normed = centred * lax.rsqrt(jnp.mean(centred * centred, -1, keepdims=True) + 1e-05)
    h1 = (normed * ln_ref[0:1, :] + ln_ref[1:2, :]).astype(bf16)
    h2 = (normed * ln_ref[2:3, :] + ln_ref[3:4, :]).astype(bf16)
    row = pl.program_id(0) * x.shape[0] + lax.broadcasted_iota(jnp.int32, (x.shape[0], 1), 0)
    cot = jnp.where(row < len_ref[0], cot_ref[...], jnp.zeros_like(cot_ref[...]))
    h1_ref[...] = h1
    h2_ref[...] = h2
    cotm_ref[...] = cot
    h1t_ref[...] = h1.T
    h2t_ref[...] = h2.T
    cott_ref[...] = cot.T


def prepare(lengths, x, cot, ln, rows=256):
    count, width = x.shape
    block = pl.BlockSpec((rows, width), lambda i, n: (i, 0))
    turned = pl.BlockSpec((width, rows), lambda i, n: (0, i))
    straight = jax.ShapeDtypeStruct((count, width), bf16)
    across = jax.ShapeDtypeStruct((width, count), bf16)
    return pl.pallas_call(
        prepare_kernel,
        grid_spec=pltpu.PrefetchScalarGridSpec(
            num_scalar_prefetch=1,
            grid=(count // rows,),
            in_specs=[block, block, fixed(ln.shape)],
            out_specs=[block, block, turned, turned, block, turned],
        ),
        out_shape=[straight, straight, across, across, straight, across],
        compiler_params=params(),
        cost_estimate=pl.CostEstimate(
            flops=20 * count * width, bytes_accessed=12 * 2**20, transcendentals=0
        ),
        name="prepare",
    )(lengths, x, cot, ln)


def cut_kernel(co_ref, qkv_ref, out_ref, up_ref, down_ref, in_ref, in0_ref, ff_ref, ff0_ref):
    half = qkv_ref.shape[0] // 2
    unit = LANES // 2
    for y in range(2):
        for x in range(2):
            at = (y ^ co_ref[2]) * 2 + (x ^ co_ref[1])

            def fill(inner, feeds):
                row = 0
                for ref in (qkv_ref, out_ref):
                    tiles = ref.shape[1] // 2 // LANES
                    for t in range(tiles):
                        lanes = slice((x * tiles + t) * LANES, (x * tiles + t + 1) * LANES)
                        inner[row : row + half, :] = ref[y * half : (y + 1) * half, lanes]
                        row += half
                for sub in range(3):
                    for z in range(2):
                        for c in range(2):
                            tile = (2 * (2 * x + z) + c) * 3 + sub
                            row = ((3 * z + sub) * 2 + c) * half
                            feeds[0, row : row + half, :] = up_ref[
                                y * half : (y + 1) * half, tile * LANES : (tile + 1) * LANES
                            ]
                    for t in range(3):
                        row = (3 * sub + t) * unit
                        start = sub * LANES + y * unit
                        lanes = slice((3 * x + t) * LANES, (3 * x + t + 1) * LANES)
                        feeds[1, row : row + unit, :] = down_ref[start : start + unit, lanes]

            fill(in_ref.at[at], ff_ref.at[at])
            pl.when(at == 0)(lambda: fill(in0_ref, ff0_ref))


def cut(coords, qkv, out, up, down):
    whole = lambda s: pl.BlockSpec(s, lambda i, co: (0,) * len(s))
    rows = qkv.shape[0] // 2 * ((qkv.shape[1] + out.shape[1]) // 2 // LANES)
    shapes = [(4, rows, LANES), (rows, LANES), (4, 2, rows, LANES), (2, rows, LANES)]
    return pl.pallas_call(
        cut_kernel,
        grid_spec=pltpu.PrefetchScalarGridSpec(
            num_scalar_prefetch=1,
            grid=(1,),
            in_specs=[whole(entry.shape) for entry in (qkv, out, up, down)],
            out_specs=[whole(shape) for shape in shapes],
        ),
        out_shape=[jax.ShapeDtypeStruct(shape, bf16) for shape in shapes],
        compiler_params=params(),
        name="cut",
    )(coords, qkv, out, up, down)


def piece_of(parts, q, k):
    own, line, side, up, diagonal = parts
    if k == 0:
        return own.at[q]
    return (line, side, up, diagonal)[q].at[k - 1]


def qkv_kernel(
    co_ref, h1_ref, b_ref, c_ref, sa_ref, sb_ref,
    p0, p1, p2, p3, p4, r0, r1, r2, r3, r4, o_ref, w_ref, wo_ref,
):
    width = h1_ref.shape[1]
    half = width // 16

    @pl.when(pl.program_id(0) == 0)
    def _():
        for other, parts in enumerate(((p0, p1, p2, p3, p4), (r0, r1, r2, r3, r4))):
            for k in range(4):
                for q in range(4):
                    ref = piece_of(parts, q, k)
                    shard = (k ^ co_ref[3]) * 2 + (other ^ co_ref[0])
                    row = pl.multiple_of(shard * 2 * half + ((q // 2) ^ co_ref[2]) * half, half)
                    x = (q % 2) ^ co_ref[1]
                    start = 0
                    for target in (w_ref, wo_ref):
                        tiles = target.shape[1] // 2 // LANES
                        for t in range(tiles):
                            lane = pl.multiple_of((x * tiles + t) * LANES, LANES)
                            target[pl.ds(row, half), pl.ds(lane, LANES)] = ref[start : start + half, :]
                            start += half

    h1 = h1_ref[...]
    cosine, ahead, behind = c_ref[...], sa_ref[...], sb_ref[...]
    low = lax.broadcasted_iota(jnp.int32, (1, LANES), 1) < HEAD_DIM

    def turn(y):
        return y * cosine - pltpu.roll(y * ahead, LANES - 8, 1) - pltpu.roll(y * behind, 8, 1)

    for part in range(3):
        cols = slice(part * width, (part + 1) * width)
        y = nn(h1, w_ref[:, cols]) + b_ref[:, cols]
        for pair in range(2):
            base = pair * 3 * LANES
            t0 = y[:, base : base + LANES]
            t1 = y[:, base + LANES : base + 2 * LANES]
            t2 = y[:, base + 2 * LANES : base + 3 * LANES]
            queries = turn(jnp.where(low, t0, t1)) * (HEAD_DIM**-0.5)
            keys = turn(pltpu.roll(jnp.where(low, t2, t0), HEAD_DIM, 1))
            at = (2 * part + pair) * LANES
            o_ref[:, at : at + LANES] = queries.astype(bf16)
            o_ref[:, width + at : width + at + LANES] = keys.astype(bf16)
            o_ref[:, 2 * width + at : 2 * width + at + LANES] = jnp.where(low, t1, t2).astype(bf16)


def qkv_forward(coords, h1, bias, tables, pieces, rows=256):
    count, width = h1.shape
    block = lambda n: pl.BlockSpec((rows, n), lambda i, co: (i, 0))
    whole = lambda s: pl.BlockSpec(s, lambda i, co: (0,) * len(s))
    arrays = [entry for part in pieces for entry in part]
    return pl.pallas_call(
        qkv_kernel,
        grid_spec=pltpu.PrefetchScalarGridSpec(
            num_scalar_prefetch=1,
            grid=(count // rows,),
            in_specs=[block(width), fixed(bias.shape)]
            + [block(LANES)] * 3
            + [fixed(entry.shape) for entry in arrays],
            out_specs=[block(3 * width), whole((width, 3 * width)), whole((width, width))],
        ),
        out_shape=[
            jax.ShapeDtypeStruct((count, 3 * width), bf16),
            jax.ShapeDtypeStruct((width, 3 * width), bf16),
            jax.ShapeDtypeStruct((width, width), bf16),
        ],
        compiler_params=params(),
        cost_estimate=pl.CostEstimate(
            flops=6 * count * width * width, bytes_accessed=18 * 2**20, transcendentals=0
        ),
        name="qkv_forward",
    )(coords, h1, bias, *tables, *arrays)


def rotary_tables(count):
    lane = lax.broadcasted_iota(jnp.int32, (1, LANES), 1) % HEAD_DIM
    inverse = 10000.0 ** (-(2 * (lane % (ROT_DIM // 2))).astype(f32) / ROT_DIM)
    angles = lax.broadcasted_iota(jnp.int32, (count, 1), 0).astype(f32) * inverse
    cosine, sine = jnp.cos(angles), jnp.sin(angles)
    return (
        jnp.where(lane < ROT_DIM, cosine, 1.0),
        jnp.where((lane >= ROT_DIM // 2) & (lane < ROT_DIM), sine, 0.0),
        jnp.where(lane < ROT_DIM // 2, -sine, 0.0),
    )


def attention_kernel(
    q_ref, k_ref, v_ref, cot_ref, w_ref, c_ref, sa_ref, sb_ref, a_ref, dqkv_ref, dq, dkt, dvt, *, rows
):
    count = q_ref.shape[0]
    blocks = count // rows
    low = lax.broadcasted_iota(jnp.int32, (1, LANES), 1) < HEAD_DIM
    causal = lax.broadcasted_iota(jnp.int32, (rows, rows), 1) <= lax.broadcasted_iota(
        jnp.int32, (rows, rows), 0
    )

    def unturn(y):
        return (
            y * c_ref[...]
            + pltpu.roll(y * sa_ref[...], LANES - 8, 1)
            + pltpu.roll(y * sb_ref[...], 8, 1)
        )

    for i in reversed(range(blocks)):
        before = rows * i
        here = slice(before, before + rows)
        past = slice(0, before)
        q = q_ref[here, :]
        da = nt(cot_ref[here, :], w_ref[...]).astype(bf16)
        q_turned, da_turned = q.T, da.T
        outs, grads = [], []
        for h in range(2):
            mine = low if h == 0 else jnp.logical_not(low)
            head = slice(HEAD_DIM * h, HEAD_DIM * (h + 1))
            qh = jnp.where(mine, q, jnp.zeros_like(q))
            dah = jnp.where(mine, da, jnp.zeros_like(da))
            s_here = jnp.where(causal, nt(qh, k_ref[here, :]), -1e30)
            highest = jnp.max(s_here, -1, keepdims=True)
            if before:
                s_past = nt(qh, k_ref[past, :])
                highest = jnp.maximum(highest, jnp.max(s_past, -1, keepdims=True))
                e_past = jnp.exp(s_past - highest)
            e_here = jnp.exp(s_here - highest)
            total = jnp.sum(e_here, -1, keepdims=True)
            if before:
                total = total + jnp.sum(e_past, -1, keepdims=True)
            inverse = 1.0 / total
            p_here = e_here * inverse
            l_here = p_here.astype(bf16)
            out = nn(l_here, v_ref[here, :])
            if before:
                p_past = e_past * inverse
                l_past = p_past.astype(bf16)
                out = out + nn(l_past, v_ref[past, :])
            row_dot = jnp.sum(jnp.where(mine, out * dah.astype(f32), 0.0), -1, keepdims=True)
            ds_here = (p_here * (nt(dah, v_ref[here, :]) - row_dot)).astype(bf16)
            grad = nn(ds_here, k_ref[here, :])
            if before:
                ds_past = (p_past * (nt(dah, v_ref[past, :]) - row_dot)).astype(bf16)
                grad = grad + nn(ds_past, k_ref[past, :])
            outs.append(out)
            grads.append(grad)
            qt, dat = q_turned[head, :], da_turned[head, :]
            if i == blocks - 1:
                dkt[head, here] = nn(qt, ds_here)
                dvt[head, here] = nn(dat, l_here)
                if before:
                    dkt[head, past] = nn(qt, ds_past)
                    dvt[head, past] = nn(dat, l_past)
            else:
                dkt[head, here] += nn(qt, ds_here)
                dvt[head, here] += nn(dat, l_here)
                if before:
                    dkt[head, past] += nn(qt, ds_past)
                    dvt[head, past] += nn(dat, l_past)
        a_ref[here, :] = jnp.where(low, outs[0], outs[1]).astype(bf16)
        dq[here, :] = jnp.where(low, grads[0], grads[1]) * (HEAD_DIM**-0.5)
    gq = unturn(dq[...])
    gk = pltpu.roll(unturn(dkt[...].T), HEAD_DIM, 1)
    gv = dvt[...].T
    dqkv_ref[:, 0:LANES] = jnp.where(low, gq, gk).astype(bf16)
    dqkv_ref[:, LANES : 2 * LANES] = jnp.where(low, gv, gq).astype(bf16)
    dqkv_ref[:, 2 * LANES : 3 * LANES] = jnp.where(low, gk, gv).astype(bf16)


def attention(qkv, cot, out_weight, tables, rows=256):
    count, width = cot.shape
    pairs = width // LANES
    column = lambda offset: pl.BlockSpec((count, LANES), lambda p: (0, offset + p))
    return pl.pallas_call(
        functools.partial(attention_kernel, rows=rows),
        grid=(pairs,),
        in_specs=[column(0), column(pairs), column(2 * pairs), fixed((count, width))]
        + [pl.BlockSpec((LANES, width), lambda p: (p, 0))]
        + [fixed((count, LANES))] * 3,
        out_specs=[column(0), pl.BlockSpec((count, 3 * LANES), lambda p: (0, p))],
        out_shape=[
            jax.ShapeDtypeStruct((count, width), bf16),
            jax.ShapeDtypeStruct((count, 3 * width), bf16),
        ],
        scratch_shapes=[
            pltpu.VMEM((count, LANES), f32),
            pltpu.VMEM((LANES, count), f32),
            pltpu.VMEM((LANES, count), f32),
        ],
        compiler_params=params(),
        cost_estimate=pl.CostEstimate(
            flops=30 * 10**9, bytes_accessed=20 * 2**20, transcendentals=8 * 10**6
        ),
        name="attention",
    )(qkv, qkv, qkv, cot, out_weight, *tables)


def feed_kernel(
    co_ref, h2_ref, h2t_ref, cot_ref, cott_ref, upb_ref, acc0_ref, before_ref,
    p0, p1, p2, p3, p4, r0, r1, r2, r3, r4, e0, e1, e2, e3, e4, f0, f1, f2, f3, f4,
    mix_ref, k0_ref, s0_ref, k1_ref, s1_ref, ubg_ref, dh2_ref, sq_ref, up_ref, down_ref, us, ds, *acc,
):
    j = pl.program_id(0)
    z, sub = j % 4, j // 4
    rows = up_ref.shape[0] // 16
    unit = LANES // 2
    x_here = (z // 2) ^ co_ref[1]

    def fill_up(x):
        for other, parts in enumerate(((p0, p1, p2, p3, p4), (r0, r1, r2, r3, r4))):
            for k in range(4):
                for y in range(2):
                    ref = piece_of(parts, 2 * y + x, k)
                    shard = (k ^ co_ref[3]) * 2 + (other ^ co_ref[0])
                    row = pl.multiple_of((2 * shard + (y ^ co_ref[2])) * rows, rows)
                    for t in range(2):
                        up_ref[pl.ds(row, rows), t * LANES : (t + 1) * LANES] = ref[
                            0, t * rows : (t + 1) * rows, :
                        ]

    pl.when(x_here == 0)(lambda: fill_up(0))
    pl.when(x_here == 1)(lambda: fill_up(1))

    def fill_down(k):
        for other, parts in enumerate(((e0, e1, e2, e3, e4), (f0, f1, f2, f3, f4))):
            first = (other ^ co_ref[0]) * LANES
            for q in range(4):
                ref = piece_of(parts, q, k)
                row = pl.multiple_of(first + ((q // 2) ^ co_ref[2]) * unit, unit)
                for t in range(3):
                    lane = pl.multiple_of((((q % 2) ^ co_ref[1]) * 3 + t) * LANES, LANES)
                    down_ref[pl.ds(row, unit), pl.ds(lane, LANES)] = ref[0, t * unit : (t + 1) * unit, :]

    k_here = z ^ co_ref[3]
    pl.when(k_here == 0)(lambda: fill_down(0))
    pl.when(k_here != 0)(lambda: fill_down(1))

    u = nn(h2_ref[...], up_ref[...]) + upb_ref[...]
    act = nt(cot_ref[...], down_ref[...])
    cdf = 0.5 * (1.0 + lax.erf(u * math.sqrt(0.5)))
    pdf = jnp.exp(-0.5 * u * u) * (1.0 / math.sqrt(2.0 * math.pi))
    g = (u * cdf).astype(bf16)
    du = (act * (cdf + u * pdf)).astype(bf16)
    acc_ref = acc[0] if acc else mix_ref
    fed = nn(g, down_ref[...])

    @pl.when(j == 0)
    def _():
        acc_ref[...] = acc0_ref[...] + fed

    @pl.when(j > 0)
    def _():
        acc_ref[...] += fed

    bias_grad = jnp.sum(du.astype(f32), 0, keepdims=True)
    ubg_ref[...] = bias_grad
    up_grad = nn(h2t_ref[...], du)
    us[...] = up_grad.astype(bf16)
    down_grad = nn(cott_ref[...], g)
    ds[...] = down_grad.astype(bf16)
    refs = (k0_ref, s0_ref, k1_ref, s1_ref)
    put_rows(us, z % 2, (2 * sub + z // 2) * 2 * rows, co_ref, refs)
    first = pl.num_programs(0) * rows
    z_here = z_at(z, co_ref)

    def put_down(c, pair):
        for x in range(2):
            for y in range(2):
                ref, s2 = (pair[x], y) if c == 0 else (pair[y], x)
                for t in range(3):
                    start = ((x ^ co_ref[1]) * 3 + t) * LANES + (y ^ co_ref[2]) * unit
                    to = pl.ds(pl.multiple_of(first + (3 * sub + t) * unit, unit), unit)
                    ref[s2, z_here, to, :] = ds[
                        pl.ds(pl.multiple_of(start, unit), unit), c * LANES : (c + 1) * LANES
                    ]

    for c in range(2):
        pl.when(co_ref[0] == c)(functools.partial(put_down, c, refs[:2]))
        pl.when(co_ref[0] != c)(functools.partial(put_down, c, refs[2:]))
    part = nt(du, up_ref[...])

    @pl.when(j == 0)
    def _():
        dh2_ref[...] = part if before_ref is None else before_ref[...] + part
        sq_ref[...] = jnp.zeros_like(sq_ref)

    @pl.when(j > 0)
    def _():
        dh2_ref[...] += part

    sq_ref[0:1, :] += fold(
        jnp.sum(up_grad * up_grad + down_grad * down_grad, 0, keepdims=True)
        + bias_grad * bias_grad
    )
    if not acc:
        return

    @pl.when(j == pl.num_programs(0) - 1)
    def _():
        row = lax.broadcasted_iota(jnp.int32, (mix_ref.shape[0], 1), 0)
        mix_ref[...] = jnp.where(row < co_ref[4], acc_ref[...], 0.0).astype(bf16)


def feed(coords, h2, h2t, cot, cott, up_bias, acc, before, pieces, first, subs):
    count, width = h2.shape
    tile = 2 * LANES
    hidden = 4 * subs * tile
    rows = width // 16
    last = before is not None
    piece = jax.ShapeDtypeStruct((2, 4, subs * (4 * rows + 3 * LANES // 2), LANES), bf16)
    window = 2 * rows
    at_up = lambda j: (j % 2) * 3 + first + j // 4
    at_line = lambda j, co: jnp.maximum((j % 4) ^ co[3], 1) - 1
    up_parts = [pl.BlockSpec((4, 1, window, LANES), lambda j, co: (0, 0, at_up(j), 0))]
    up_parts += [pl.BlockSpec((3, 1, window, LANES), lambda j, co: (0, 0, at_up(j), 0))] * 4
    window = 3 * LANES // 2
    down_parts = [pl.BlockSpec((4, 1, window, LANES), lambda j, co: (0, 1, first + j // 4, 0))]
    down_parts += [
        pl.BlockSpec((1, 1, window, LANES), lambda j, co: (at_line(j, co), 1, first + j // 4, 0))
    ] * 4
    arrays = [entry for part in pieces for entry in part]
    whole = lambda s: pl.BlockSpec(s, lambda j, co: (0,) * len(s))
    start = [before] if last else []
    kernel = feed_kernel
    if not last:
        kernel = lambda *refs: feed_kernel(*refs[:7], None, *refs[7:])
    return pl.pallas_call(
        kernel,
        grid_spec=pltpu.PrefetchScalarGridSpec(
            num_scalar_prefetch=1,
            grid=(4 * subs,),
            in_specs=[
                fixed((count, width)),
                fixed((width, count)),
                fixed((count, width)),
                fixed((width, count)),
                pl.BlockSpec((1, tile), lambda j, co: (0, 4 * first + j)),
                fixed((count, width)),
            ]
            + [fixed((count, width))] * len(start)
            + up_parts * 2
            + down_parts * 2,
            out_specs=[whole((count, width))]
            + [whole(piece.shape)] * 4
            + [
                pl.BlockSpec((1, tile), lambda j, co: (0, j)),
                whole((count, width)),
                whole((8, LANES)),
            ],
            scratch_shapes=[
                pltpu.VMEM((width, tile), bf16),
                pltpu.VMEM((tile, width), bf16),
                pltpu.VMEM((width, tile), bf16),
                pltpu.VMEM((width, tile), bf16),
            ]
            + [pltpu.VMEM((count, width), f32)] * len(start),
        ),
        out_shape=[jax.ShapeDtypeStruct((count, width), bf16 if last else f32)]
        + [piece] * 4
        + [
            jax.ShapeDtypeStruct((1, hidden), f32),
            jax.ShapeDtypeStruct((count, width), f32),
            jax.ShapeDtypeStruct((8, LANES), f32),
        ],
        compiler_params=params(),
        cost_estimate=pl.CostEstimate(
            flops=12 * count * width * hidden,
            bytes_accessed=12 * subs * 2**20,
            transcendentals=2 * count * hidden,
        ),
        name="feed",
    )(coords, h2, h2t, cot, cott, up_bias, acc, *start, *arrays, *arrays)


def inner_kernel(
    co_ref, h1t_ref, dqkv_ref, w_ref, heads_ref, cot_ref, x_ref, wo_ref, ob_ref,
    k0_ref, s0_ref, k1_ref, s1_ref, bias_ref, cotsum_ref, dh1_ref, acc_ref, sq_ref, scr,
):
    j = pl.program_id(0)
    inner = j < pl.num_programs(0) - 2

    @pl.when(j == 0)
    def _():
        sq_ref[...] = jnp.zeros_like(sq_ref)

    @pl.when(inner)
    def _():
        right = dqkv_ref[...]
        grad = nn(h1t_ref[...], right)
        scr[...] = grad.astype(bf16)
        bias_grad = jnp.sum(right.astype(f32), 0, keepdims=True)
        bias_ref[...] = bias_grad
        part = nt(right, w_ref[...])

        @pl.when(j == 0)
        def _():
            dh1_ref[...] = part

        @pl.when(j > 0)
        def _():
            dh1_ref[...] += part

        sq_ref[0:1, :] += fold(jnp.sum(grad * grad, 0, keepdims=True) + bias_grad * bias_grad)

    @pl.when(jnp.logical_not(inner))
    def _():
        right = cot_ref[...]
        grad = tn(heads_ref[...], right)
        scr[...] = grad.astype(bf16)
        bias_grad = jnp.sum(right.astype(f32), 0, keepdims=True)
        cotsum_ref[...] = bias_grad
        acc_ref[...] = x_ref[...].astype(f32) + nn(heads_ref[...], wo_ref[...]) + ob_ref[...]
        sq_ref[0:1, :] += fold(jnp.sum(grad * grad, 0, keepdims=True) + 2.0 * bias_grad * bias_grad)

    put_rows(scr, j % 2, 0, co_ref, (k0_ref, s0_ref, k1_ref, s1_ref), (0,))


def inner_grads(coords, h1t, dqkv, weight, heads, cot, x, out_weight, out_bias):
    count, width = heads.shape
    cols = dqkv.shape[1]
    tile = width // 2
    steps = cols // tile + 2
    inner = lambda j: jnp.minimum(j, steps - 3)
    outer = lambda j: jnp.maximum(j - (steps - 2), 0)
    piece = jax.ShapeDtypeStruct((2, 4, steps // 2, tile // LANES * width // 16, LANES), bf16)
    spec = pl.BlockSpec((2, 4, 1) + piece.shape[3:], lambda j, co: (0, 0, j // 2, 0, 0))
    outer_block = lambda r: pl.BlockSpec((r, tile), lambda j, co: (0, outer(j)))
    return pl.pallas_call(
        inner_kernel,
        grid_spec=pltpu.PrefetchScalarGridSpec(
            num_scalar_prefetch=1,
            grid=(steps,),
            in_specs=[
                fixed((width, count)),
                pl.BlockSpec((count, tile), lambda j, co: (0, inner(j))),
                pl.BlockSpec((width, tile), lambda j, co: (0, inner(j))),
                fixed((count, width)),
                outer_block(count),
                outer_block(count),
                outer_block(width),
                outer_block(1),
            ],
            out_specs=[spec] * 4
            + [
                pl.BlockSpec((1, tile), lambda j, co: (0, inner(j))),
                outer_block(1),
                pl.BlockSpec((count, width), lambda j, co: (0, 0)),
                outer_block(count),
                pl.BlockSpec((8, LANES), lambda j, co: (0, 0)),
            ],
            scratch_shapes=[pltpu.VMEM((width, tile), bf16)],
        ),
        out_shape=[piece] * 4
        + [
            jax.ShapeDtypeStruct((1, cols), f32),
            jax.ShapeDtypeStruct((1, width), f32),
            jax.ShapeDtypeStruct((count, width), f32),
            jax.ShapeDtypeStruct((count, width), f32),
            jax.ShapeDtypeStruct((8, LANES), f32),
        ],
        compiler_params=params(),
        cost_estimate=pl.CostEstimate(
            flops=16 * count * width * width, bytes_accessed=24 * 2**20, transcendentals=0
        ),
        name="inner_grads",
    )(coords, h1t, dqkv, weight, heads, cot, x, out_weight, out_bias)


def combine_kernel(scale_ref, a_ref, b_ref, c_ref, d_ref, send_ref, keep_ref):
    for s2, ref in enumerate((keep_ref, send_ref)):
        total = scale_ref[0] * a_ref[s2].astype(f32)
        for at, came in enumerate((b_ref, c_ref, d_ref)):
            total = total + scale_ref[1 + at] * came[s2].astype(f32)
        ref[...] = total.astype(bf16)


def combine(scales, arrays):
    rows = arrays[0].shape[2]
    line = pl.BlockSpec((1, rows, LANES), lambda i, s: (i, 0, 0))
    return pl.pallas_call(
        combine_kernel,
        grid_spec=pltpu.PrefetchScalarGridSpec(
            num_scalar_prefetch=1,
            grid=(4,),
            in_specs=[pl.BlockSpec((2, 1, rows, LANES), lambda i, s: (0, i, 0, 0))] * 4,
            out_specs=[line, line],
        ),
        out_shape=[jax.ShapeDtypeStruct((4, rows, LANES), bf16)] * 2,
        compiler_params=params(),
        cost_estimate=pl.CostEstimate(
            flops=10**7, bytes_accessed=80 * rows * LANES, transcendentals=0
        ),
        name="combine",
    )(scales, *arrays)


def pack_kernel(ln_ref, qkv_ref, cot_ref, ub1_ref, ub2_ref, out_ref):
    for f in range(8):
        to = 0
        sources = [ln_ref.at[i : i + 1] for i in range(4)] + [qkv_ref, cot_ref]
        for ref in sources:
            size = ref.shape[1] // 8
            out_ref[f : f + 1, to : to + size] = ref[:, f * size : (f + 1) * size]
            to += size
        for sub in range(3):
            ref, at = (ub1_ref, 8 * sub + f) if sub < 2 else (ub2_ref, f)
            out_ref[f : f + 1, to : to + LANES] = ref[:, at * LANES : (at + 1) * LANES]
            to += LANES


def pack(*arrays):
    whole = lambda s: pl.BlockSpec(s, lambda i: (0, 0))
    width = (4 * arrays[0].shape[1] + sum(entry.shape[1] for entry in arrays[1:])) // 8
    return pl.pallas_call(
        pack_kernel,
        grid=(1,),
        in_specs=[whole(entry.shape) for entry in arrays],
        out_specs=whole((8, width)),
        out_shape=jax.ShapeDtypeStruct((8, width), f32),
        compiler_params=params(),
        name="pack",
    )(*arrays)


def finish_kernel(co_ref, *refs):
    groups = refs[0:4], refs[4:8], refs[8:12]
    gq_ref, go_ref, gu_ref, gd_ref = refs[12:16]
    half = gq_ref.shape[0] // 2
    unit = LANES // 2
    for group, parts, scr in zip(range(3), groups, refs[16:19]):
        for at, part in enumerate(parts):
            scr[((at // 2) ^ co_ref[2]) * 2 + ((at % 2) ^ co_ref[1])] = part[...]
        for y in range(2):
            rows = slice(y * half, (y + 1) * half)
            for x in range(2):
                owner = 2 * y + x
                if group == 0:
                    for window in range(4):
                        for t in range(3):
                            at = (window * 3 + t) * half
                            value = scr[owner, at : at + half, :].astype(f32)
                            ref, tile = gq_ref, (2 * window + x) * 3 + t
                            if window == 3:
                                ref, tile = go_ref, x * 3 + t
                            ref[rows, tile * LANES : (tile + 1) * LANES] = value
                    continue
                for i in range(2 // group):
                    sub = 2 * (group - 1) + i
                    for z in range(2):
                        for c in range(2):
                            at = ((2 * i + z) * 2 + c) * half
                            tile = (2 * (2 * z + x) + c) * 3 + sub
                            gu_ref[rows, tile * LANES : (tile + 1) * LANES] = scr[
                                owner, at : at + half, :
                            ].astype(f32)
        if group == 0:
            continue
        for i in range(2 // group):
            sub = 2 * (group - 1) + i
            for x in range(2):
                for t in range(3):
                    at = 4 * (2 // group) * half + (3 * i + t) * unit
                    block = jnp.concatenate([scr[2 * y + x, at : at + unit, :] for y in range(2)], 0)
                    lanes = slice((3 * x + t) * LANES, (3 * x + t + 1) * LANES)
                    gd_ref[sub * LANES : (sub + 1) * LANES, lanes] = block.astype(f32).T


def finish(coords, groups, shapes):
    whole = lambda s: pl.BlockSpec(s, lambda i, co: (0,) * len(s))
    arrays = [entry for group in groups for entry in group]
    return pl.pallas_call(
        finish_kernel,
        grid_spec=pltpu.PrefetchScalarGridSpec(
            num_scalar_prefetch=1,
            grid=(1,),
            in_specs=[whole(entry.shape) for entry in arrays],
            out_specs=[whole(s) for s in shapes],
            scratch_shapes=[pltpu.VMEM((4,) + group[0].shape, bf16) for group in groups],
        ),
        out_shape=[jax.ShapeDtypeStruct(s, f32) for s in shapes],
        compiler_params=params(),
        name="finish",
    )(coords, *arrays)


def norm_back_kernel(x_ref, cot_ref, dh1_ref, dh2_ref, ln_ref, dx_ref, sums_ref):
    x = x_ref[...].astype(f32)
    centred = x - jnp.mean(x, -1, keepdims=True)
    inverse = lax.rsqrt(jnp.mean(centred * centred, -1, keepdims=True) + 1e-05)
    normed = centred * inverse
    dh1, dh2 = dh1_ref[...], dh2_ref[...]
    scaled = dh1 * ln_ref[0:1, :] + dh2 * ln_ref[2:3, :]
    spread = (
        scaled
        - jnp.mean(scaled, -1, keepdims=True)
        - normed * jnp.mean(scaled * normed, -1, keepdims=True)
    )
    dx_ref[...] = cot_ref[...].astype(f32) + inverse * spread

    @pl.when(pl.program_id(0) == 0)
    def _():
        sums_ref[...] = jnp.zeros_like(sums_ref)

    for row, value in enumerate((dh1 * normed, dh1, dh2 * normed, dh2)):
        sums_ref[row : row + 1, :] += jnp.sum(value, 0, keepdims=True)


def norm_back(x, cot, dh1, dh2, ln, rows=256):
    count, width = x.shape
    block = pl.BlockSpec((rows, width), lambda i: (i, 0))
    return pl.pallas_call(
        norm_back_kernel,
        grid=(count // rows,),
        in_specs=[block] * 4 + [fixed(ln.shape)],
        out_specs=[block, pl.BlockSpec((8, width), lambda i: (0, 0))],
        out_shape=[
            jax.ShapeDtypeStruct((count, width), f32),
            jax.ShapeDtypeStruct((8, width), f32),
        ],
        compiler_params=params(),
        cost_estimate=pl.CostEstimate(
            flops=30 * count * width, bytes_accessed=12 * 2**20, transcendentals=0
        ),
        name="norm_back",
    )(x, cot, dh1, dh2, ln)


def body(
    tokens_in, ln1_gain, ln1_bias, ln2_gain, ln2_bias, qkv_weight, qkv_bias, out_weight, out_bias,
    up_weight, up_bias, down_weight, down_bias, cotangent, lengths, assignment, clip_bound,
):
    dp, fsdp = lax.axis_size("dp"), lax.axis_size("fsdp")
    both = ("dp", "fsdp")
    total = dp * fsdp
    fast = (dp, fsdp) == (4, 8)
    me = lax.axis_index("dp") * fsdp + lax.axis_index("fsdp")

    def swap(value, even, odd=None):
        pairs = [(i, i ^ (even if odd is None or i % 2 == 0 else odd)) for i in range(total)]
        return lax.ppermute(value, both, pairs)

    width = tokens_in.shape[2]
    smalls = (ln1_gain, ln1_bias, ln2_gain, ln2_bias, qkv_bias, out_bias, up_bias, down_bias)
    packed = jnp.concatenate(smalls)
    if fast:
        slot = lax.broadcasted_iota(jnp.int32, (fsdp, 1), 0) == lax.axis_index("fsdp")
        rows = jnp.where(slot, packed[None, :], jnp.zeros_like(packed)[None, :])
        for at in range(3):
            rows = rows + swap(rows, 2**at)
    else:
        rows = lax.all_gather(packed, "fsdp", axis=0)
    vectors, start = [], 0
    for entry in smalls:
        stop = start + entry.shape[0]
        vectors.append(rows[:, start:stop].reshape(1, -1).astype(f32))
        start = stop
    ln = jnp.concatenate(vectors[:4] + [jnp.zeros((4, vectors[0].shape[1]), f32)], 0)
    qkv_b, out_b, up_b, down_b = vectors[4:]

    spot = [me & 1, (me >> 3) & 1, (me >> 4) & 1, (me >> 1) & 3] if fast else [0 * me] * 4
    coords = jnp.stack(spot + [lengths[0]]).astype(jnp.int32)
    if fast:
        in_own, in_mine, ff_own, ff_mine = cut(coords, qkv_weight, out_weight, up_weight, down_weight)
        lines = []
        for piece in (in_mine, ff_mine):
            lines.append([swap(piece, 2 * k) for k in (1, 2, 3)])
        gathered = []
        for own, line in ((in_own, lines[0]), (ff_own, lines[1])):
            line = jnp.stack(line)
            mine = [own, line] + [swap(line, 8 * way) for way in (1, 2, 3)]
            theirs = [swap(entry, 1) for entry in mine]
            gathered.append((mine, theirs))
    else:
        whole = [
            lax.all_gather(w, "fsdp", axis=0, tiled=True)
            for w in (qkv_weight, out_weight, up_weight, down_weight)
        ]
        flat = lambda w: w.reshape(4, 2, 2, w.shape[0] // 16, 2, -1, LANES).transpose(
            0, 1, 2, 4, 5, 3, 6
        ).reshape(4, 2, 4, -1, LANES)
        qkv_p, out_p, up_p = (flat(w) for w in whole[:3])
        down_p = whole[3].reshape(4, 2, 3, 2, LANES // 2, 2, 3, LANES).transpose(0, 1, 3, 5, 2, 6, 4, 7)
        down_p = down_p.reshape(up_p.shape)
        up_p = up_p.reshape(4, 2, 4, 2, 2, 3, width // 16, LANES).swapaxes(4, 5).reshape(up_p.shape)
        gathered = []
        for entry in (jnp.concatenate([qkv_p, out_p], 3), jnp.stack([up_p, down_p], 3)):
            gathered.append(
                tuple([entry[0, c]] + [entry[1:, c, q] for q in range(4)] for c in range(2))
            )

    tokens = tokens_in[0]
    count, width = tokens.shape
    tables = rotary_tables(count)
    h1, h2, h1t, h2t, cot, cott = prepare(lengths, tokens, cotangent[0], ln)
    qkv, w_qkv, w_out = qkv_forward(coords, h1, qkv_b, tables, gathered[0])
    heads, dqkv = attention(qkv, cot, w_out, tables)
    *in_pieces, qkv_bias_grad, cot_sum, dh1, acc, in_sq = inner_grads(
        coords, h1t, dqkv, w_qkv, heads, cot, tokens, w_out, out_b + down_b
    )
    up_b = up_b.reshape(8, 3, LANES).swapaxes(0, 1).reshape(1, -1)
    ff = (coords, h2, h2t, cot, cott, up_b)
    acc, *f1_pieces, ub_grad1, dh2, f1_sq = feed(*ff, acc, None, gathered[1], 0, 2)
    mixed, *f2_pieces, ub_grad2, dh2, f2_sq = feed(*ff, acc, dh2, gathered[1], 2, 1)
    groups = []
    for pieces in (in_pieces, f1_pieces, f2_pieces):
        kept, sent, kept_other, sent_other = (entry.reshape(2, 4, -1, LANES) for entry in pieces)
        if fast:
            sent, sent_other = swap(sent, 8, 16), swap(sent_other, 16, 8)
            kept_other, sent_other = swap(kept_other, 1), swap(sent_other, 1)
        groups.append((kept, sent, kept_other, sent_other))
    dx, ln_sums = norm_back(tokens, cot, dh1, dh2, ln)
    ln_grads = ln_sums[:4]

    squares = jnp.sum(in_sq + f1_sq + f2_sq) + jnp.sum(ln_grads * ln_grads)
    slots = jnp.arange(total, dtype=jnp.int32)
    facts = jnp.stack([squares, assignment[0].astype(f32)])[:, None]
    facts = jnp.where(slots[None, :] == me, facts, 0.0)
    if fast:
        for at in range(5):
            facts = facts + swap(facts, 2**at)
    else:
        facts = lax.psum(facts, both)
    norms, numbers = jnp.sqrt(facts[0]), facts[1].astype(jnp.int32)
    ahead = (norms[None, :] < norms[:, None]) | (
        (norms[None, :] == norms[:, None]) & (slots[None, :] < slots[:, None])
    )
    rank = jnp.sum(ahead.astype(jnp.int32), 1)
    median = jnp.sum(jnp.where(rank == total // 2, norms, 0.0))
    bound = median * clip_bound[0].astype(f32) / 8.0
    slot_scale = jnp.minimum(1.0, bound / (norms + 1e-06))
    clip_scale = jnp.sum(jnp.where(numbers[None, :] == slots[:, None], slot_scale[None, :], 0.0), 1)
    if fast:
        next_slot = me ^ jnp.where(me % 2 == 0, 8, 16)
        sources = jnp.stack([me, next_slot, me ^ 1, next_slot ^ 1])
    else:
        sources = jnp.stack([me] * 4)
    own_scales = jnp.sum(jnp.where(slots[None, :] == sources[:, None], slot_scale[None, :], 0.0), 1)
    own = own_scales[0]
    scales = own_scales / total
    share = scales[0]

    if fast:
        vector_grads = pack(ln_sums, qkv_bias_grad, cot_sum, ub_grad1, ub_grad2)
        vector_grads = vector_grads * share
        for at in range(5):
            vector_grads = vector_grads + swap(vector_grads, 2**at)
        finals = []
        for name, arrays in zip("abc", groups):
            sent, kept = combine(scales, arrays)
            came = swap(sent, 16, 8)
            add = lambda at, *more: sum((e.astype(f32) for e in more), kept[at].astype(f32) + came[at])
            near = swap(add(slice(2, 4)).astype(bf16), 2)
            last = swap(add(1, near[1]).astype(bf16), 4)
            line = add(0, near[0], last).astype(bf16)
            along_x, along_y = swap(line, 8), swap(line, 16)
            turn = (along_y, 8) if name == "b" else (along_x, 16)
            finals.append((line, along_x, along_y, swap(*turn)))
        own_rows = width // fsdp
        hidden = up_b.shape[1]
        shapes = [(own_rows, 3 * width), (own_rows, width), (own_rows, hidden)]
        shapes.append((hidden // fsdp, width))
        gq, go, gu, gd = finish(coords, finals, shapes)
    else:
        up_bias_grad = jnp.concatenate([ub_grad1, ub_grad2], 1).reshape(3, 8, LANES).swapaxes(0, 1)
        vector_grads = [ln_grads[i] for i in range(4)] + [qkv_bias_grad, cot_sum, up_bias_grad]
        vector_grads = jnp.concatenate([entry.reshape(fsdp, -1) for entry in vector_grads], 1)
        vector_grads = lax.psum(vector_grads * share, both)

        def plain(arrays):
            kept, sent, kept_other, sent_other = (
                entry.reshape(2, 2, 2, -1, LANES).swapaxes(1, 2).reshape(entry.shape)
                for entry in arrays
            )
            return jnp.stack([jnp.stack([kept, sent]), jnp.stack([kept_other, sent_other], 1)])

        half = width // 16
        inner = plain(groups[0]).reshape(2, 2, 2, 4, 4, 3, half, LANES)
        flat = lambda e: e.transpose(3, 0, 2, 6, 4, 1, 5, 7).reshape(width, -1)
        outs = [flat(inner[:, :, :, :, :3]), flat(inner[:, :, :, :, 3:])]
        ups, downs = [], []
        for entry in groups[1:]:
            up, down = jnp.split(plain(entry), 2, 4)
            ups.append(up.reshape(2, 2, 2, 4, -1, 2, 2, half, LANES))
            downs.append(down.reshape(2, 2, 2, 4, -1, 3, LANES // 2, LANES))
        up, down = jnp.concatenate(ups, 4), jnp.concatenate(downs, 4)
        outs.append(up.transpose(3, 0, 2, 7, 5, 1, 6, 4, 8).reshape(width, -1))
        outs.append(down.transpose(3, 0, 4, 7, 1, 5, 2, 6).reshape(-1, width))
        outs = [(entry.astype(f32) * share).astype(bf16) for entry in outs]
        gq, go, gu, gd = (
            lax.psum(
                lax.psum_scatter(w, "fsdp", scatter_dimension=0, tiled=True).astype(f32), "dp"
            )
            for w in outs
        )

    tokens_grad = (own * dx).astype(bf16)[None]
    own_row = lax.dynamic_index_in_dim(vector_grads, lax.axis_index("fsdp"), 0, keepdims=False)
    sizes = [ln1_gain.shape[0]] * 4 + [qkv_bias.shape[0], out_bias.shape[0], up_bias.shape[0]]
    parts, start = [], 0
    for size in sizes:
        parts.append(own_row[start : start + size])
        start += size
    g1, b1, g2, b2, gqb, gob, gub = parts
    return (mixed[None], tokens_grad, clip_scale, g1, b1, g2, b2, gq, gqb, go, gob, gu, gub, gd, gob)


def solution(mesh):
    step = mapped(mesh)
    if dict(mesh.shape) != {"dp": 4, "fsdp": 8}:
        return step
    return step


def mapped(mesh):
    rows, cols, flat = P("fsdp", None), P("fsdp"), P(("dp", "fsdp"))
    slots = P(("dp", "fsdp"), None, None)
    return jax.shard_map(
        body,
        mesh=mesh,
        in_specs=(slots, cols, cols, cols, cols, rows, cols, rows, cols, rows, cols, rows, cols)
        + (slots, flat, flat, P()),
        out_specs=(slots, slots, P(), cols, cols, cols, cols, rows, cols, rows, cols, rows, cols)
        + (rows, cols),
        check_vma=False,
    )
```

```python
import functools
import math

import jax
import jax.numpy as jnp
from jax import lax
from jax.experimental import pallas as pl
from jax.experimental.pallas import tpu as pltpu
from jax.sharding import PartitionSpec as P


HEAD_DIM = 64
ROT_DIM = 16
LANES = 128
f32 = jnp.float32
bf16 = jnp.bfloat16


def nn(left, right):
    return lax.dot_general(left, right, (((1,), (0,)), ((), ())), preferred_element_type=f32)


def nt(left, right):
    return lax.dot_general(left, right, (((1,), (1,)), ((), ())), preferred_element_type=f32)


def tn(left, right):
    return lax.dot_general(left, right, (((0,), (0,)), ((), ())), preferred_element_type=f32)


def fold(row):
    total = row[:, 0:LANES]
    for start in range(LANES, row.shape[1], LANES):
        total = total + row[:, start : start + LANES]
    return total


def fixed(shape):
    return pl.BlockSpec(shape, lambda *_: (0,) * len(shape), pipeline_mode=pl.Buffered(1))


def params(mib=60):
    return pltpu.CompilerParams(vmem_limit_bytes=mib * 2**20)


def z_of(at, coords):
    return ((at % 2) * 2 + at // 2) ^ coords[3]


def z_at(z, coords):
    rel = z ^ coords[3]
    return (rel % 2) * 2 + rel // 2


def put_rows(scr, x, row, coords, refs, extra=(), tiles=None):
    half = scr.shape[0] // 16
    x_rel = x ^ coords[1]

    def put(c, near, pair):
        def one(z):
            shard = z_of(z, coords) * 2 + (c ^ coords[0])
            for y in range(2):
                start = pl.multiple_of((2 * shard + (y ^ coords[2])) * half, half)
                ref, s2 = (pair[0], y) if near else (pair[y], x_rel)
                for t, tile in enumerate(tiles or range(scr.shape[1] // LANES)):
                    to = pl.ds(pl.multiple_of(row + t * half, half), half)
                    ref[(s2, z) + extra + (to, slice(None))] = scr[
                        pl.ds(start, half), tile * LANES : (tile + 1) * LANES
                    ]

        if extra:
            for z in range(4):
                one(z)
        else:
            pl.loop(0, 4)(one)

    for c in range(2):
        kept, sent = refs[2 * c : 2 * c + 2]
        near = coords[0] == c
        pl.when(near & (x_rel == 0))(functools.partial(put, c, True, (kept,)))
        pl.when(near & (x_rel == 1))(functools.partial(put, c, True, (sent,)))
        pl.when(jnp.logical_not(near))(functools.partial(put, c, False, (kept, sent)))


def prepare_kernel(
    len_ref, x_ref, cot_ref, ln_ref, h1_ref, h2_ref, h1t_ref, h2t_ref, cotm_ref, cott_ref
):
    x = x_ref[...].astype(f32)
    centred = x - jnp.mean(x, -1, keepdims=True)
    normed = centred * lax.rsqrt(jnp.mean(centred * centred, -1, keepdims=True) + 1e-05)
    h1 = (normed * ln_ref[0:1, :] + ln_ref[1:2, :]).astype(bf16)
    h2 = (normed * ln_ref[2:3, :] + ln_ref[3:4, :]).astype(bf16)
    row = pl.program_id(0) * x.shape[0] + lax.broadcasted_iota(jnp.int32, (x.shape[0], 1), 0)
    cot = jnp.where(row < len_ref[0], cot_ref[...], jnp.zeros_like(cot_ref[...]))
    h1_ref[...] = h1
    h2_ref[...] = h2
    cotm_ref[...] = cot
    h1t_ref[...] = h1.T
    h2t_ref[...] = h2.T
    cott_ref[...] = cot.T


def prepare(lengths, x, cot, ln, rows=256):
    count, width = x.shape
    block = pl.BlockSpec((rows, width), lambda i, n: (i, 0))
    turned = pl.BlockSpec((width, rows), lambda i, n: (0, i))
    straight = jax.ShapeDtypeStruct((count, width), bf16)
    across = jax.ShapeDtypeStruct((width, count), bf16)
    return pl.pallas_call(
        prepare_kernel,
        grid_spec=pltpu.PrefetchScalarGridSpec(
            num_scalar_prefetch=1,
            grid=(count // rows,),
            in_specs=[block, block, fixed(ln.shape)],
            out_specs=[block, block, turned, turned, block, turned],
        ),
        out_shape=[straight, straight, across, across, straight, across],
        compiler_params=params(24),
        cost_estimate=pl.CostEstimate(
            flops=20 * count * width, bytes_accessed=12 * 2**20, transcendentals=0
        ),
        name="prepare",
    )(lengths, x, cot, ln)


def cut_kernel(co_ref, qkv_ref, out_ref, up_ref, down_ref, in_ref, in0_ref, ff_ref, ff0_ref):
    half = qkv_ref.shape[0] // 2
    unit = LANES // 2
    for y in range(2):
        for x in range(2):
            at = (y ^ co_ref[2]) * 2 + (x ^ co_ref[1])

            def fill(inner, feeds):
                row = 0
                for ref in (qkv_ref, out_ref):
                    tiles = ref.shape[1] // 2 // LANES
                    for t in range(tiles):
                        lanes = slice((x * tiles + t) * LANES, (x * tiles + t + 1) * LANES)
                        inner[row : row + half, :] = ref[y * half : (y + 1) * half, lanes]
                        row += half
                for sub in range(3):
                    for z in range(2):
                        for c in range(2):
                            tile = (2 * (2 * x + z) + c) * 3 + sub
                            row = ((3 * z + sub) * 2 + c) * half
                            feeds[0, row : row + half, :] = up_ref[
                                y * half : (y + 1) * half, tile * LANES : (tile + 1) * LANES
                            ]
                    for t in range(3):
                        row = (3 * sub + t) * unit
                        start = sub * LANES + y * unit
                        lanes = slice((3 * x + t) * LANES, (3 * x + t + 1) * LANES)
                        feeds[1, row : row + unit, :] = down_ref[start : start + unit, lanes]

            fill(in_ref.at[at], ff_ref.at[at])
            pl.when(at == 0)(lambda: fill(in0_ref, ff0_ref))


def cut(coords, qkv, out, up, down):
    whole = lambda s: pl.BlockSpec(s, lambda i, co: (0,) * len(s))
    rows = qkv.shape[0] // 2 * ((qkv.shape[1] + out.shape[1]) // 2 // LANES)
    shapes = [(4, rows, LANES), (rows, LANES), (4, 2, rows, LANES), (2, rows, LANES)]
    return pl.pallas_call(
        cut_kernel,
        grid_spec=pltpu.PrefetchScalarGridSpec(
            num_scalar_prefetch=1,
            grid=(1,),
            in_specs=[whole(entry.shape) for entry in (qkv, out, up, down)],
            out_specs=[whole(shape) for shape in shapes],
        ),
        out_shape=[jax.ShapeDtypeStruct(shape, bf16) for shape in shapes],
        compiler_params=params(12),
        name="cut",
    )(coords, qkv, out, up, down)


def piece_of(parts, q, k):
    own, line, side, up, diagonal = parts
    if isinstance(k, int) and k == 0:
        return own.at[q]
    return (line, side, up, diagonal)[q].at[k - 1]


def qkv_kernel(
    co_ref, h1_ref, b_ref, c_ref, sa_ref, sb_ref,
    p0, p1, p2, p3, p4, r0, r1, r2, r3, r4, o_ref, w_ref, wo_ref,
):
    width = h1_ref.shape[1]
    half = width // 16

    @pl.when(pl.program_id(0) == 0)
    def _():
        for other, parts in enumerate(((p0, p1, p2, p3, p4), (r0, r1, r2, r3, r4))):


            def fill(k, other=other, parts=parts):
                for q in range(4):
                    ref = piece_of(parts, q, k)
                    shard = (k ^ co_ref[3]) * 2 + (other ^ co_ref[0])
                    row = pl.multiple_of(shard * 2 * half + ((q // 2) ^ co_ref[2]) * half, half)
                    x = (q % 2) ^ co_ref[1]
                    start = 0
                    for target in (w_ref, wo_ref):
                        tiles = target.shape[1] // 2 // LANES
                        for t in range(tiles):
                            lane = pl.multiple_of((x * tiles + t) * LANES, LANES)
                            target[pl.ds(row, half), pl.ds(lane, LANES)] = ref[start : start + half, :]
                            start += half

            fill(0)
            pl.loop(1, 4)(fill)

    h1 = h1_ref[...]
    cosine, ahead, behind = c_ref[...], sa_ref[...], sb_ref[...]
    low = lax.broadcasted_iota(jnp.int32, (1, LANES), 1) < HEAD_DIM

    def turn(y):
        return y * cosine - pltpu.roll(y * ahead, LANES - 8, 1) - pltpu.roll(y * behind, 8, 1)

    for part in range(3):
        cols = slice(part * width, (part + 1) * width)
        y = nn(h1, w_ref[:, cols]) + b_ref[:, cols]
        for pair in range(2):
            base = pair * 3 * LANES
            t0 = y[:, base : base + LANES]
            t1 = y[:, base + LANES : base + 2 * LANES]
            t2 = y[:, base + 2 * LANES : base + 3 * LANES]
            queries = turn(jnp.where(low, t0, t1)) * (HEAD_DIM**-0.5)
            keys = turn(pltpu.roll(jnp.where(low, t2, t0), HEAD_DIM, 1))
            at = (2 * part + pair) * LANES
            o_ref[:, at : at + LANES] = queries.astype(bf16)
            o_ref[:, width + at : width + at + LANES] = keys.astype(bf16)
            o_ref[:, 2 * width + at : 2 * width + at + LANES] = jnp.where(low, t1, t2).astype(bf16)


def qkv_forward(coords, h1, bias, tables, pieces, rows=256):
    count, width = h1.shape
    block = lambda n: pl.BlockSpec((rows, n), lambda i, co: (i, 0))
    whole = lambda s: pl.BlockSpec(s, lambda i, co: (0,) * len(s))
    arrays = [entry for part in pieces for entry in part]
    return pl.pallas_call(
        qkv_kernel,
        grid_spec=pltpu.PrefetchScalarGridSpec(
            num_scalar_prefetch=1,
            grid=(count // rows,),
            in_specs=[block(width), fixed(bias.shape)]
            + [block(LANES)] * 3
            + [fixed(entry.shape) for entry in arrays],
            out_specs=[block(3 * width), whole((width, 3 * width)), whole((width, width))],
        ),
        out_shape=[
            jax.ShapeDtypeStruct((count, 3 * width), bf16),
            jax.ShapeDtypeStruct((width, 3 * width), bf16),
            jax.ShapeDtypeStruct((width, width), bf16),
        ],
        compiler_params=params(34),
        cost_estimate=pl.CostEstimate(
            flops=6 * count * width * width, bytes_accessed=18 * 2**20, transcendentals=0
        ),
        name="qkv_forward",
    )(coords, h1, bias, *tables[:3], *arrays)


def rotary_tables(count):
    half = ROT_DIM // 2
    lane = lax.broadcasted_iota(jnp.int32, (1, LANES), 1) % HEAD_DIM
    row = lax.broadcasted_iota(jnp.int32, (half, 1), 0)
    inverse = lambda at: 10000.0 ** (-(2 * (at % half)).astype(f32) / ROT_DIM)
    angles = lax.broadcasted_iota(jnp.int32, (count, 1), 0).astype(f32) * inverse(lane)
    turned = lax.broadcasted_iota(jnp.int32, (1, count), 1).astype(f32) * inverse(row)
    cosine, sine = jnp.cos(angles), jnp.sin(angles)
    return (
        jnp.where(lane < ROT_DIM, cosine, 1.0),
        jnp.where((lane >= half) & (lane < ROT_DIM), sine, 0.0),
        jnp.where(lane < half, -sine, 0.0),
        jnp.cos(turned),
        jnp.sin(turned),
    )


def attention_kernel(
    q_ref, k_ref, v_ref, cot_ref, w_ref, c_ref, sa_ref, sb_ref, ct_ref, st_ref,
    a_ref, dqkv_ref, da_ref, qt_ref, dat_ref, dq, dkt, dvt, *, rows,
):
    count = q_ref.shape[0]
    blocks = count // rows
    low = lax.broadcasted_iota(jnp.int32, (1, LANES), 1) < HEAD_DIM
    causal = lax.broadcasted_iota(jnp.int32, (rows, rows), 1) <= lax.broadcasted_iota(
        jnp.int32, (rows, rows), 0
    )
    da_ref[...] = nt(cot_ref[...], w_ref[...]).astype(bf16)
    qt_ref[...] = q_ref[...].T
    dat_ref[...] = da_ref[...].T

    def products(i, h):
        here, past = slice(i * rows, (i + 1) * rows), slice(0, i * rows)
        mine = low if h == 0 else jnp.logical_not(low)
        q, da = q_ref[here, :], da_ref[here, :]
        q = jnp.where(mine, q, jnp.zeros_like(q))
        da = jnp.where(mine, da, jnp.zeros_like(da))
        s_here, d_here = nt(q, k_ref[here, :]), nt(da, v_ref[here, :])
        if not i:
            return [s_here], [d_here]
        return [s_here, nt(q, k_ref[past, :])], [d_here, nt(da, v_ref[past, :])]

    def rest(i, h, scores, grads):
        here, past = slice(i * rows, (i + 1) * rows), slice(0, i * rows)
        head = slice(HEAD_DIM * h, HEAD_DIM * (h + 1))
        spans = (here, past)[: len(scores)]
        scores = [jnp.where(causal, scores[0], -1e30)] + scores[1:]
        highest = jnp.max(scores[0], -1, keepdims=True)
        for s in scores[1:]:
            highest = jnp.maximum(highest, jnp.max(s, -1, keepdims=True))
        raised = [jnp.exp(s - highest) for s in scores]
        inverse = 1.0 / sum(jnp.sum(e, -1, keepdims=True) for e in raised)
        probs = [e * inverse for e in raised]
        row_dot = sum(jnp.sum(p * d, -1, keepdims=True) for p, d in zip(probs, grads))
        out, grad = 0.0, 0.0
        for span, p, d in zip(spans, probs, grads):
            weights = p.astype(bf16)
            ds = (p * (d - row_dot)).astype(bf16)
            out = out + nn(weights, v_ref[span, :])
            grad = grad + nn(ds, k_ref[span, :])
            dk, dv = nn(qt_ref[head, here], ds), nn(dat_ref[head, here], weights)
            if i == blocks - 1:
                dkt[head, span], dvt[head, span] = dk, dv
            else:
                dkt[head, span] += dk
                dvt[head, span] += dv
        return out, grad

    units = [(i, h) for i in reversed(range(blocks)) for h in range(2)]
    ready = products(*units[0])
    results = {}
    for at, unit in enumerate(units):
        now = ready
        if at + 1 < len(units):
            ready = products(*units[at + 1])
        results[unit] = rest(*unit, *now)
        i, h = unit
        if h == 1:
            here = slice(i * rows, (i + 1) * rows)
            first, second = results.pop((i, 0)), results.pop((i, 1))
            a_ref[here, :] = jnp.where(low, first[0], second[0]).astype(bf16)
            y = jnp.where(low, first[1], second[1]) * (HEAD_DIM**-0.5)
            dq[here, :] = (
                y * c_ref[here, :]
                + pltpu.roll(y * sa_ref[here, :], LANES - 8, 1)
                + pltpu.roll(y * sb_ref[here, :], 8, 1)
            )
    cosine, sine = ct_ref[...], st_ref[...]
    for h in range(2):
        one = slice(HEAD_DIM * h, HEAD_DIM * h + 8)
        two = slice(HEAD_DIM * h + 8, HEAD_DIM * h + 16)
        first, second = dkt[one, :], dkt[two, :]
        dkt[one, :] = first * cosine + second * sine
        dkt[two, :] = second * cosine - first * sine
    gk = dkt[...].astype(bf16).T
    gv = dvt[...].astype(bf16).T
    gq = dq[...].astype(bf16)
    gk = jnp.concatenate([gk[:, HEAD_DIM:], gk[:, :HEAD_DIM]], 1)
    dqkv_ref[:, 0:LANES] = jnp.where(low, gq, gk)
    dqkv_ref[:, LANES : 2 * LANES] = jnp.where(low, gv, gq)
    dqkv_ref[:, 2 * LANES : 3 * LANES] = jnp.where(low, gk, gv)


def attention(qkv, cot, out_weight, tables, rows=256):
    count, width = cot.shape
    pairs = width // LANES
    column = lambda offset: pl.BlockSpec((count, LANES), lambda p: (0, offset + p))
    return pl.pallas_call(
        functools.partial(attention_kernel, rows=rows),
        grid=(pairs,),
        in_specs=[column(0), column(pairs), column(2 * pairs), fixed((count, width))]
        + [pl.BlockSpec((LANES, width), lambda p: (p, 0))]
        + [fixed((count, LANES))] * 3
        + [fixed((8, count))] * 2,
        out_specs=[column(0), pl.BlockSpec((count, 3 * LANES), lambda p: (0, p))],
        out_shape=[
            jax.ShapeDtypeStruct((count, width), bf16),
            jax.ShapeDtypeStruct((count, 3 * width), bf16),
        ],
        scratch_shapes=[
            pltpu.VMEM((count, LANES), bf16),
            pltpu.VMEM((LANES, count), bf16),
            pltpu.VMEM((LANES, count), bf16),
            pltpu.VMEM((count, LANES), f32),
            pltpu.VMEM((LANES, count), f32),
            pltpu.VMEM((LANES, count), f32),
        ],
        compiler_params=params(26),
        cost_estimate=pl.CostEstimate(
            flops=30 * 10**9, bytes_accessed=20 * 2**20, transcendentals=8 * 10**6
        ),
        name="attention",
    )(qkv, qkv, qkv, cot, out_weight, *tables)


def feed_kernel(
    co_ref, h2_ref, h2t_ref, cot_ref, cott_ref, upb_ref, acc0_ref, before_ref,
    p0, p1, p2, p3, p4, r0, r1, r2, r3, r4, e0, e1, e2, e3, e4, f0, f1, f2, f3, f4,
    mix_ref, k0_ref, s0_ref, k1_ref, s1_ref, ubg_ref, dh2_ref, sq_ref, up_ref, down_ref, us, ds, *acc,
):
    j = pl.program_id(0)
    side, sub = j % 2, j // 2
    rows = up_ref.shape[0] // 16
    unit = LANES // 2
    x_here = side ^ co_ref[1]
    acc_ref = acc[0] if acc else mix_ref

    @pl.when(j == 0)
    def _():
        acc_ref[...] = acc0_ref[...]
        dh2_ref[...] = jnp.zeros_like(dh2_ref) if before_ref is None else before_ref[...]
        sq_ref[...] = jnp.zeros_like(sq_ref)

    def fill_up(x, k):
        for other, parts in enumerate(((p0, p1, p2, p3, p4), (r0, r1, r2, r3, r4))):
            for y in range(2):
                ref = piece_of(parts, 2 * y + x, k)
                shard = (k ^ co_ref[3]) * 2 + (other ^ co_ref[0])
                row = pl.multiple_of((2 * shard + (y ^ co_ref[2])) * rows, rows)
                for t in range(4):
                    up_ref[pl.ds(row, rows), t * LANES : (t + 1) * LANES] = ref[
                        0, t // 2, 0, (t % 2) * rows : (t % 2 + 1) * rows, :
                    ]

    for x in range(2):

        @pl.when(x_here == x)
        def _(x=x):
            fill_up(x, 0)
            pl.loop(1, 4)(lambda k: fill_up(x, k))


    def fill_down(k):
        z = k ^ co_ref[3]
        for other, parts in enumerate(((e0, e1, e2, e3, e4), (f0, f1, f2, f3, f4))):
            first = (2 * (z % 2) + (other ^ co_ref[0])) * LANES
            for q in range(4):
                ref = piece_of(parts, q, k)
                row = pl.multiple_of(first + ((q // 2) ^ co_ref[2]) * unit, unit)
                for t in range(3):
                    lane = pl.multiple_of((((q % 2) ^ co_ref[1]) * 3 + t) * LANES, LANES)
                    down_ref[pl.ds(row, unit), pl.ds(lane, LANES)] = ref[0, t * unit : (t + 1) * unit, :]

    pl.when(co_ref[3] // 2 == side)(lambda: fill_down(0))

    @pl.loop(1, 4)
    def _(k):
        pl.when((k ^ co_ref[3]) // 2 == side)(lambda: fill_down(k))


    u = nn(h2_ref[...], up_ref[...]) + upb_ref[...]
    act = nt(cot_ref[...], down_ref[...])
    cdf = 0.5 * (1.0 + lax.erf(u * math.sqrt(0.5)))
    pdf = jnp.exp(-0.5 * u * u) * (1.0 / math.sqrt(2.0 * math.pi))
    g = (u * cdf).astype(bf16)
    du = (act * (cdf + u * pdf)).astype(bf16)
    fed = nn(g, down_ref[...])

    acc_ref[...] += fed
    bias_grad = jnp.sum(du.astype(f32), 0, keepdims=True)
    ubg_ref[...] = bias_grad
    up_grad = nn(h2t_ref[...], du)
    us[...] = up_grad.astype(bf16)
    down_grad = nn(cott_ref[...], g)
    ds[...] = down_grad.astype(bf16)
    refs = (k0_ref, s0_ref, k1_ref, s1_ref)
    for x in range(2):
        put_rows(us, x, (2 * sub + side) * 2 * rows, co_ref, refs, tiles=(2 * x, 2 * x + 1))
    first = pl.num_programs(0) * 2 * rows

    def put_down(c, pair):
        for z in range(2):
            tile = 2 * z + c
            for x in range(2):
                for y in range(2):
                    ref, s2 = (pair[x], y) if c == 0 else (pair[y], x)
                    for t in range(3):
                        start = ((x ^ co_ref[1]) * 3 + t) * LANES + (y ^ co_ref[2]) * unit
                        to = pl.ds(pl.multiple_of(first + (3 * sub + t) * unit, unit), unit)
                        ref[s2, z_at(2 * side + z, co_ref), to, :] = ds[
                            pl.ds(pl.multiple_of(start, unit), unit), tile * LANES : (tile + 1) * LANES
                        ]

    for c in range(2):
        pl.when(co_ref[0] == c)(functools.partial(put_down, c, refs[:2]))
        pl.when(co_ref[0] != c)(functools.partial(put_down, c, refs[2:]))
    part = nt(du, up_ref[...])

    dh2_ref[...] += part
    sq_ref[0:1, :] += fold(
        jnp.sum(up_grad * up_grad + down_grad * down_grad, 0, keepdims=True)
        + bias_grad * bias_grad
    )
    if not acc:
        return

    @pl.when(j == pl.num_programs(0) - 1)
    def _():
        row = lax.broadcasted_iota(jnp.int32, (mix_ref.shape[0], 1), 0)
        mix_ref[...] = jnp.where(row < co_ref[4], acc_ref[...], 0.0).astype(bf16)


def feed(coords, h2, h2t, cot, cott, up_bias, acc, before, pieces, first, subs):
    count, width = h2.shape
    tile = 4 * LANES
    hidden = 2 * subs * tile
    rows = width // 16
    last = before is not None
    piece = jax.ShapeDtypeStruct((2, 4, subs * (4 * rows + 3 * LANES // 2), LANES), bf16)
    up_pieces = [
        [entry.reshape(*entry.shape[:2], 2, 3, 2 * rows, LANES) for entry in part] for part in pieces
    ]
    up_spec = lambda n: pl.BlockSpec(
        (n, 1, 2, 1, 2 * rows, LANES), lambda j, co: (0, 0, 0, first + j // 2, 0, 0)
    )
    down_spec = lambda n: pl.BlockSpec(
        (n, 1, 3 * LANES // 2, LANES), lambda j, co: (0, 1, first + j // 2, 0)
    )
    up_parts = [up_spec(4)] + [up_spec(3)] * 4
    down_parts = [down_spec(4)] + [down_spec(3)] * 4
    up_arrays = [entry for part in up_pieces for entry in part]
    arrays = [entry for part in pieces for entry in part]
    whole = lambda s: pl.BlockSpec(s, lambda j, co: (0,) * len(s))
    start = [before] if last else []
    kernel = feed_kernel
    if not last:
        kernel = lambda *refs: feed_kernel(*refs[:7], None, *refs[7:])
    return pl.pallas_call(
        kernel,
        grid_spec=pltpu.PrefetchScalarGridSpec(
            num_scalar_prefetch=1,
            grid=(2 * subs,),
            in_specs=[
                fixed((count, width)),
                fixed((width, count)),
                fixed((count, width)),
                fixed((width, count)),
                pl.BlockSpec((1, tile), lambda j, co: (0, 2 * first + j)),
                fixed((count, width)),
            ]
            + [fixed((count, width))] * len(start)
            + up_parts * 2
            + down_parts * 2,
            out_specs=[whole((count, width))]
            + [whole(piece.shape)] * 4
            + [
                pl.BlockSpec((1, tile), lambda j, co: (0, j)),
                whole((count, width)),
                whole((8, LANES)),
            ],
            scratch_shapes=[
                pltpu.VMEM((width, tile), bf16),
                pltpu.VMEM((tile, width), bf16),
                pltpu.VMEM((width, tile), bf16),
                pltpu.VMEM((width, tile), bf16),
            ]
            + [pltpu.VMEM((count, width), f32)] * len(start),
        ),
        out_shape=[jax.ShapeDtypeStruct((count, width), bf16 if last else f32)]
        + [piece] * 4
        + [
            jax.ShapeDtypeStruct((1, hidden), f32),
            jax.ShapeDtypeStruct((count, width), f32),
            jax.ShapeDtypeStruct((8, LANES), f32),
        ],
        compiler_params=params(60),
        cost_estimate=pl.CostEstimate(
            flops=12 * count * width * hidden,
            bytes_accessed=12 * subs * 2**20,
            transcendentals=2 * count * hidden,
        ),
        name="feed",
    )(coords, h2, h2t, cot, cott, up_bias, acc, *start, *up_arrays, *arrays)


def inner_kernel(
    co_ref, h1t_ref, dqkv_ref, w_ref, heads_ref, cot_ref, x_ref, wo_ref, ob_ref,
    k0_ref, s0_ref, k1_ref, s1_ref, bias_ref, cotsum_ref, dh1_ref, acc_ref, sq_ref, scr,
):
    j = pl.program_id(0)
    inner = j < pl.num_programs(0) - 1

    @pl.when(j == 0)
    def _():
        sq_ref[...] = jnp.zeros_like(sq_ref)

    @pl.when(inner)
    def _():
        right = dqkv_ref[...]
        grad = nn(h1t_ref[...], right)
        scr[...] = grad.astype(bf16)
        bias_grad = jnp.sum(right.astype(f32), 0, keepdims=True)
        bias_ref[...] = bias_grad
        part = nt(right, w_ref[...])

        @pl.when(j == 0)
        def _():
            dh1_ref[...] = part

        @pl.when(j > 0)
        def _():
            dh1_ref[...] += part

        sq_ref[0:1, :] += fold(jnp.sum(grad * grad, 0, keepdims=True) + bias_grad * bias_grad)

    @pl.when(jnp.logical_not(inner))
    def _():
        right = cot_ref[...]
        grad = tn(heads_ref[...], right)
        scr[...] = grad.astype(bf16)
        bias_grad = jnp.sum(right.astype(f32), 0, keepdims=True)
        cotsum_ref[...] = bias_grad
        acc_ref[...] = x_ref[...].astype(f32) + nn(heads_ref[...], wo_ref[...]) + ob_ref[...]
        sq_ref[0:1, :] += fold(jnp.sum(grad * grad, 0, keepdims=True) + 2.0 * bias_grad * bias_grad)

    half = scr.shape[1] // LANES // 2
    for x in range(2):
        tiles = range(x * half, (x + 1) * half)
        put_rows(scr, x, 0, co_ref, (k0_ref, s0_ref, k1_ref, s1_ref), (0,), tiles)


def inner_grads(coords, h1t, dqkv, weight, heads, cot, x, out_weight, out_bias):
    count, width = heads.shape
    cols = dqkv.shape[1]
    tile = width
    steps = cols // tile + 1
    inner = lambda j: jnp.minimum(j, steps - 2)
    piece = jax.ShapeDtypeStruct((2, 4, steps, tile // LANES // 2 * width // 16, LANES), bf16)
    spec = pl.BlockSpec((2, 4, 1) + piece.shape[3:], lambda j, co: (0, 0, j, 0, 0))
    outer_block = lambda r: fixed((r, tile))
    outer_out = lambda r: pl.BlockSpec((r, tile), lambda j, co: (0, 0))
    return pl.pallas_call(
        inner_kernel,
        grid_spec=pltpu.PrefetchScalarGridSpec(
            num_scalar_prefetch=1,
            grid=(steps,),
            in_specs=[
                fixed((width, count)),
                pl.BlockSpec((count, tile), lambda j, co: (0, inner(j))),
                pl.BlockSpec((width, tile), lambda j, co: (0, inner(j))),
                fixed((count, width)),
                outer_block(count),
                outer_block(count),
                outer_block(width),
                outer_block(1),
            ],
            out_specs=[spec] * 4
            + [
                pl.BlockSpec((1, tile), lambda j, co: (0, inner(j))),
                outer_out(1),
                pl.BlockSpec((count, width), lambda j, co: (0, 0)),
                outer_out(count),
                pl.BlockSpec((8, LANES), lambda j, co: (0, 0)),
            ],
            scratch_shapes=[pltpu.VMEM((width, tile), bf16)],
        ),
        out_shape=[piece] * 4
        + [
            jax.ShapeDtypeStruct((1, cols), f32),
            jax.ShapeDtypeStruct((1, width), f32),
            jax.ShapeDtypeStruct((count, width), f32),
            jax.ShapeDtypeStruct((count, width), f32),
            jax.ShapeDtypeStruct((8, LANES), f32),
        ],
        compiler_params=params(48),
        cost_estimate=pl.CostEstimate(
            flops=16 * count * width * width, bytes_accessed=24 * 2**20, transcendentals=0
        ),
        name="inner_grads",
    )(coords, h1t, dqkv, weight, heads, cot, x, out_weight, out_bias)


def combine_kernel(scale_ref, co_ref, *refs, vectors):
    pieces, out_ref = refs[:4], refs[-1]
    weigh = lambda parts: sum(scale_ref[at] * part.astype(f32) for at, part in enumerate(parts)).astype(bf16)
    rows = pieces[0].shape[2]
    out_ref[0, :rows] = weigh([ref[0, 0] for ref in pieces])
    if vectors:
        owner = 2 * z_of(pl.program_id(0), co_ref) + co_ref[0]
        out_ref[0, rows:] = weigh([ref[pl.ds(owner, 1)][0] for ref in refs[4:8]])


def combine(scales, coords, s2, arrays, vectors=()):
    rows = arrays[0].shape[2]
    extra = vectors[0].shape[1] if vectors else 0
    return pl.pallas_call(
        functools.partial(combine_kernel, vectors=bool(vectors)),
        grid_spec=pltpu.PrefetchScalarGridSpec(
            num_scalar_prefetch=2,
            grid=(4,),
            in_specs=[pl.BlockSpec((1, 1, rows, LANES), lambda i, s, co: (s2, i, 0, 0))] * 4
            + [fixed(entry.shape) for entry in vectors],
            out_specs=pl.BlockSpec((1, rows + extra, LANES), lambda i, s, co: (i, 0, 0)),
        ),
        out_shape=jax.ShapeDtypeStruct((4, rows + extra, LANES), bf16),
        compiler_params=params(12),
        cost_estimate=pl.CostEstimate(
            flops=10**7, bytes_accessed=40 * rows * LANES, transcendentals=0
        ),
        name="combine",
    )(scales, coords, *arrays, *vectors)


def pack_kernel(ln_ref, qkv_ref, cot_ref, ub1_ref, ub2_ref, out_ref, row_ref):
    out_ref[...] = jnp.zeros_like(out_ref)
    for f in range(8):
        to = 0
        sources = [ln_ref.at[i : i + 1] for i in range(4)] + [qkv_ref, cot_ref]
        for ref in sources:
            size = ref.shape[1] // 8
            row_ref[f : f + 1, to : to + size] = ref[:, f * size : (f + 1) * size]
            to += size
        for sub in range(3):
            ref, at = (ub1_ref, 8 * sub + f) if sub < 2 else (ub2_ref, f)
            row_ref[f : f + 1, to : to + LANES] = ref[:, at * LANES : (at + 1) * LANES]
            to += LANES
        for row in range(row_ref.shape[1] // LANES):
            out_ref[f, row : row + 1, :] = row_ref[f : f + 1, row * LANES : (row + 1) * LANES]


def pack(*arrays):
    whole = lambda s: pl.BlockSpec(s, lambda i: (0,) * len(s))
    width = (4 * arrays[0].shape[1] + sum(entry.shape[1] for entry in arrays[1:])) // 8
    rows = -(-width // LANES // 16) * 16
    return pl.pallas_call(
        pack_kernel,
        grid=(1,),
        in_specs=[whole(entry.shape) for entry in arrays],
        out_specs=whole((8, rows, LANES)),
        out_shape=jax.ShapeDtypeStruct((8, rows, LANES), f32),
        scratch_shapes=[pltpu.VMEM((8, width), f32)],
        compiler_params=params(6),
        name="pack",
    )(*arrays)


def finish_kernel(co_ref, *refs):
    groups = refs[0:4], refs[4:8], refs[8:12]
    gq_ref, go_ref, gu_ref, gd_ref, gv_ref = refs[12:17]
    half = gq_ref.shape[0] // 2
    unit = LANES // 2
    for group, parts, scr in zip(range(3), groups, refs[17:20]):
        for at, part in enumerate(parts):
            scr[((at // 2) ^ co_ref[2]) * 2 + ((at % 2) ^ co_ref[1])] = part[...]
        for y in range(2):
            rows = slice(y * half, (y + 1) * half)
            for x in range(2):
                owner = 2 * y + x
                if group == 0:
                    for window in range(4):
                        for t in range(3):
                            at = (window * 3 + t) * half
                            value = scr[owner, at : at + half, :].astype(f32)
                            ref, tile = gq_ref, (2 * window + x) * 3 + t
                            if window == 3:
                                ref, tile = go_ref, x * 3 + t
                            ref[rows, tile * LANES : (tile + 1) * LANES] = value
                    continue
                for i in range(2 // group):
                    sub = 2 * (group - 1) + i
                    for z in range(2):
                        for c in range(2):
                            at = ((2 * i + z) * 2 + c) * half
                            tile = (2 * (2 * z + x) + c) * 3 + sub
                            gu_ref[rows, tile * LANES : (tile + 1) * LANES] = scr[
                                owner, at : at + half, :
                            ].astype(f32)
        if group == 0:
            continue
        for i in range(2 // group):
            sub = 2 * (group - 1) + i
            for x in range(2):
                for t in range(3):
                    at = 4 * (2 // group) * half + (3 * i + t) * unit
                    block = jnp.concatenate([scr[2 * y + x, at : at + unit, :] for y in range(2)], 0)
                    lanes = slice((3 * x + t) * LANES, (3 * x + t + 1) * LANES)
                    gd_ref[sub * LANES : (sub + 1) * LANES, lanes] = block.astype(f32).T
    gv_ref[...] = scr[0, scr.shape[1] - gv_ref.shape[0] :, :].astype(f32)


def finish(coords, groups, shapes):
    whole = lambda s: pl.BlockSpec(s, lambda i, co: (0,) * len(s))
    arrays = [entry for group in groups for entry in group]
    return pl.pallas_call(
        finish_kernel,
        grid_spec=pltpu.PrefetchScalarGridSpec(
            num_scalar_prefetch=1,
            grid=(1,),
            in_specs=[whole(entry.shape) for entry in arrays],
            out_specs=[whole(s) for s in shapes],
            scratch_shapes=[pltpu.VMEM((4,) + group[0].shape, bf16) for group in groups],
        ),
        out_shape=[jax.ShapeDtypeStruct(s, f32) for s in shapes],
        compiler_params=params(24),
        name="finish",
    )(coords, *arrays)


def norm_back_kernel(x_ref, cot_ref, dh1_ref, dh2_ref, ln_ref, dx_ref, sums_ref):
    x = x_ref[...].astype(f32)
    centred = x - jnp.mean(x, -1, keepdims=True)
    inverse = lax.rsqrt(jnp.mean(centred * centred, -1, keepdims=True) + 1e-05)
    normed = centred * inverse
    dh1, dh2 = dh1_ref[...], dh2_ref[...]
    scaled = dh1 * ln_ref[0:1, :] + dh2 * ln_ref[2:3, :]
    spread = (
        scaled
        - jnp.mean(scaled, -1, keepdims=True)
        - normed * jnp.mean(scaled * normed, -1, keepdims=True)
    )
    dx_ref[...] = cot_ref[...].astype(f32) + inverse * spread

    @pl.when(pl.program_id(0) == 0)
    def _():
        sums_ref[...] = jnp.zeros_like(sums_ref)

    for row, value in enumerate((dh1 * normed, dh1, dh2 * normed, dh2)):
        sums_ref[row : row + 1, :] += jnp.sum(value, 0, keepdims=True)


def norm_back(x, cot, dh1, dh2, ln, rows=256):
    count, width = x.shape
    block = pl.BlockSpec((rows, width), lambda i: (i, 0))
    return pl.pallas_call(
        norm_back_kernel,
        grid=(count // rows,),
        in_specs=[block] * 4 + [fixed(ln.shape)],
        out_specs=[block, pl.BlockSpec((8, width), lambda i: (0, 0))],
        out_shape=[
            jax.ShapeDtypeStruct((count, width), f32),
            jax.ShapeDtypeStruct((8, width), f32),
        ],
        compiler_params=params(22),
        cost_estimate=pl.CostEstimate(
            flops=30 * count * width, bytes_accessed=12 * 2**20, transcendentals=0
        ),
        name="norm_back",
    )(x, cot, dh1, dh2, ln)


def body(
    tokens_in, ln1_gain, ln1_bias, ln2_gain, ln2_bias, qkv_weight, qkv_bias, out_weight, out_bias,
    up_weight, up_bias, down_weight, down_bias, cotangent, lengths, assignment, clip_bound,
):
    dp, fsdp = lax.axis_size("dp"), lax.axis_size("fsdp")
    both = ("dp", "fsdp")
    total = dp * fsdp
    fast = (dp, fsdp) == (4, 8)
    me = lax.axis_index("dp") * fsdp + lax.axis_index("fsdp")

    def swap(value, even, odd=None):
        pairs = [(i, i ^ (even if odd is None or i % 2 == 0 else odd)) for i in range(total)]
        return lax.ppermute(value, both, pairs)

    width = tokens_in.shape[2]
    smalls = (ln1_gain, ln1_bias, ln2_gain, ln2_bias, qkv_bias, out_bias, up_bias, down_bias)
    packed = jnp.concatenate(smalls)
    if fast:
        slot = lax.broadcasted_iota(jnp.int32, (fsdp, 1), 0) == lax.axis_index("fsdp")
        rows = jnp.where(slot, packed[None, :], jnp.zeros_like(packed)[None, :])
        for at in range(3):
            rows = rows + swap(rows, 2**at)
    else:
        rows = lax.all_gather(packed, "fsdp", axis=0)
    vectors, start = [], 0
    for entry in smalls:
        stop = start + entry.shape[0]
        vectors.append(rows[:, start:stop].reshape(1, -1).astype(f32))
        start = stop
    ln = jnp.concatenate(vectors[:4] + [jnp.zeros((4, vectors[0].shape[1]), f32)], 0)
    qkv_b, out_b, up_b, down_b = vectors[4:]

    spot = [me & 1, (me >> 3) & 1, (me >> 4) & 1, (me >> 1) & 3] if fast else [0 * me] * 4
    coords = jnp.stack(spot + [lengths[0]]).astype(jnp.int32)
    if fast:
        in_own, in_mine, ff_own, ff_mine = cut(coords, qkv_weight, out_weight, up_weight, down_weight)
        lines = []
        for piece in (in_mine, ff_mine):
            lines.append([swap(piece, 2 * k) for k in (1, 2, 3)])
        gathered = []
        for own, line in ((in_own, lines[0]), (ff_own, lines[1])):
            line = lax.optimization_barrier(jnp.stack(line))
            mine = [own, line] + [swap(line, 8 * way) for way in (1, 2, 3)]
            theirs = [swap(entry, 1) for entry in mine]
            gathered.append((mine, theirs))
    else:
        whole = [
            lax.all_gather(w, "fsdp", axis=0, tiled=True)
            for w in (qkv_weight, out_weight, up_weight, down_weight)
        ]
        flat = lambda w: w.reshape(4, 2, 2, w.shape[0] // 16, 2, -1, LANES).transpose(
            0, 1, 2, 4, 5, 3, 6
        ).reshape(4, 2, 4, -1, LANES)
        qkv_p, out_p, up_p = (flat(w) for w in whole[:3])
        down_p = whole[3].reshape(4, 2, 3, 2, LANES // 2, 2, 3, LANES).transpose(0, 1, 3, 5, 2, 6, 4, 7)
        down_p = down_p.reshape(up_p.shape)
        up_p = up_p.reshape(4, 2, 4, 2, 2, 3, width // 16, LANES).swapaxes(4, 5).reshape(up_p.shape)
        gathered = []
        for entry in (jnp.concatenate([qkv_p, out_p], 3), jnp.stack([up_p, down_p], 3)):
            gathered.append(
                tuple([entry[0, c]] + [entry[1:, c, q] for q in range(4)] for c in range(2))
            )

    tokens = tokens_in[0]
    count, width = tokens.shape
    tables = rotary_tables(count)
    h1, h2, h1t, h2t, cot, cott = prepare(lengths, tokens, cotangent[0], ln)
    qkv, w_qkv, w_out = qkv_forward(coords, h1, qkv_b, tables, gathered[0])
    heads, dqkv = attention(qkv, cot, w_out, tables)
    *in_pieces, qkv_bias_grad, cot_sum, dh1, acc, in_sq = inner_grads(
        coords, h1t, dqkv, w_qkv, heads, cot, tokens, w_out, out_b + down_b
    )
    up_b = up_b.reshape(8, 3, LANES).swapaxes(0, 1).reshape(1, -1)
    ff = (coords, h2, h2t, cot, cott, up_b)
    acc, *f1_pieces, ub_grad1, dh2, f1_sq = feed(*ff, acc, None, gathered[1], 0, 2)
    mixed, *f2_pieces, ub_grad2, dh2, f2_sq = feed(*ff, acc, dh2, gathered[1], 2, 1)
    groups = []
    for pieces in (in_pieces, f1_pieces, f2_pieces):
        kept, sent, kept_other, sent_other = (entry.reshape(2, 4, -1, LANES) for entry in pieces)
        if fast:
            sent, sent_other = swap(sent, 8, 16), swap(sent_other, 16, 8)
            kept_other, sent_other = swap(kept_other, 1), swap(sent_other, 1)
        groups.append((kept, sent, kept_other, sent_other))
    dx, ln_sums = norm_back(tokens, cot, dh1, dh2, ln)
    ln_grads = ln_sums[:4]

    squares = jnp.sum(in_sq + f1_sq + f2_sq) + jnp.sum(ln_grads * ln_grads)
    slots = jnp.arange(total, dtype=jnp.int32)
    facts = jnp.stack([squares, assignment[0].astype(f32)])[:, None]
    facts = jnp.where(slots[None, :] == me, facts, 0.0)
    if fast:
        facts = facts + swap(facts, 1)
        packed = pack(ln_sums, qkv_bias_grad, cot_sum, ub_grad1, ub_grad2)
        vectors = [packed, swap(packed, 8, 16)]
        facts = facts + swap(facts, 8) + swap(facts, 16) + swap(facts, 24)
        vectors += [swap(packed, 1), swap(packed, 17, 9)]
        facts = facts + swap(facts, 2) + swap(facts, 4) + swap(facts, 6)
    else:
        facts = lax.psum(facts, both)
    norms, numbers = jnp.sqrt(facts[0]), facts[1].astype(jnp.int32)
    ahead = (norms[None, :] < norms[:, None]) | (
        (norms[None, :] == norms[:, None]) & (slots[None, :] < slots[:, None])
    )
    rank = jnp.sum(ahead.astype(jnp.int32), 1)
    median = jnp.sum(jnp.where(rank == total // 2, norms, 0.0))
    bound = median * clip_bound[0].astype(f32) / 8.0
    slot_scale = jnp.minimum(1.0, bound / (norms + 1e-06))
    clip_scale = jnp.sum(jnp.where(numbers[None, :] == slots[:, None], slot_scale[None, :], 0.0), 1)
    if fast:
        next_slot = me ^ jnp.where(me % 2 == 0, 8, 16)
        sources = jnp.stack([me, next_slot, me ^ 1, next_slot ^ 1])
    else:
        sources = jnp.stack([me] * 4)
    own_scales = jnp.sum(jnp.where(slots[None, :] == sources[:, None], slot_scale[None, :], 0.0), 1)
    own = own_scales[0]
    scales = own_scales / total
    share = scales[0]

    if fast:
        finals, kepts = [], []
        for arrays, more in zip(groups, ((), (), vectors)):
            sent = combine(scales, coords, 1, arrays, more)
            kepts.append(swap(sent, 16, 8))
        for name, arrays, came, more in zip("abc", groups, kepts, ((), (), vectors)):
            kept = combine(scales, coords, 0, arrays, more)
            add = lambda at, *more: sum((e.astype(f32) for e in more), kept[at].astype(f32) + came[at])
            near = swap(add(slice(2, 4)).astype(bf16), 2)
            last = swap(add(1, near[1]).astype(bf16), 4)
            line = add(0, near[0], last).astype(bf16)
            along_x, along_y = swap(line, 8), swap(line, 16)
            turn = (along_y, 8) if name == "b" else (along_x, 16)
            finals.append((line, along_x, along_y, swap(*turn)))
        own_rows = width // fsdp
        hidden = up_b.shape[1]
        shapes = [(own_rows, 3 * width), (own_rows, width), (own_rows, hidden)]
        shapes += [(hidden // fsdp, width), vectors[0].shape[1:]]
        gq, go, gu, gd, own_row = finish(coords, finals, shapes)
        own_row = own_row.reshape(-1)
    else:
        up_bias_grad = jnp.concatenate([ub_grad1, ub_grad2], 1).reshape(3, 8, LANES).swapaxes(0, 1)
        vector_grads = [ln_grads[i] for i in range(4)] + [qkv_bias_grad, cot_sum, up_bias_grad]
        vector_grads = jnp.concatenate([entry.reshape(fsdp, -1) for entry in vector_grads], 1)
        vector_grads = lax.psum(vector_grads * share, both)
        own_row = lax.dynamic_index_in_dim(vector_grads, lax.axis_index("fsdp"), 0, keepdims=False)

        def plain(arrays):
            kept, sent, kept_other, sent_other = (
                entry.reshape(2, 2, 2, -1, LANES).swapaxes(1, 2).reshape(entry.shape)
                for entry in arrays
            )
            return jnp.stack([jnp.stack([kept, sent]), jnp.stack([kept_other, sent_other], 1)])

        half = width // 16
        inner = plain(groups[0]).reshape(2, 2, 2, 4, 4, 3, half, LANES)
        flat = lambda e: e.transpose(3, 0, 2, 6, 4, 1, 5, 7).reshape(width, -1)
        outs = [flat(inner[:, :, :, :, :3]), flat(inner[:, :, :, :, 3:])]
        ups, downs = [], []
        for entry in groups[1:]:
            up, down = jnp.split(plain(entry), 2, 4)
            ups.append(up.reshape(2, 2, 2, 4, -1, 2, 2, half, LANES))
            downs.append(down.reshape(2, 2, 2, 4, -1, 3, LANES // 2, LANES))
        up, down = jnp.concatenate(ups, 4), jnp.concatenate(downs, 4)
        outs.append(up.transpose(3, 0, 2, 7, 5, 1, 6, 4, 8).reshape(width, -1))
        outs.append(down.transpose(3, 0, 4, 7, 1, 5, 2, 6).reshape(-1, width))
        outs = [(entry.astype(f32) * share).astype(bf16) for entry in outs]
        gq, go, gu, gd = (
            lax.psum(
                lax.psum_scatter(w, "fsdp", scatter_dimension=0, tiled=True).astype(f32), "dp"
            )
            for w in outs
        )

    tokens_grad = (own * dx).astype(bf16)[None]
    sizes = [ln1_gain.shape[0]] * 4 + [qkv_bias.shape[0], out_bias.shape[0], up_bias.shape[0]]
    parts, start = [], 0
    for size in sizes:
        parts.append(own_row[start : start + size])
        start += size
    g1, b1, g2, b2, gqb, gob, gub = parts
    return (mixed[None], tokens_grad, clip_scale, g1, b1, g2, b2, gq, gqb, go, gob, gu, gub, gd, gob)


def solution(mesh):
    step = mapped(mesh)
    if dict(mesh.shape) != {"dp": 4, "fsdp": 8}:
        return step
    return step


def mapped(mesh):
    rows, cols, flat = P("fsdp", None), P("fsdp"), P(("dp", "fsdp"))
    slots = P(("dp", "fsdp"), None, None)
    return jax.shard_map(
        body,
        mesh=mesh,
        in_specs=(slots, cols, cols, cols, cols, rows, cols, rows, cols, rows, cols, rows, cols)
        + (slots, flat, flat, P()),
        out_specs=(slots, slots, P(), cols, cols, cols, cols, rows, cols, rows, cols, rows, cols)
        + (rows, cols),
        check_vma=False,
    )
```

```python
import functools
import math

import jax
import jax.numpy as jnp
from jax import lax
from jax.experimental import pallas as pl
from jax.experimental.pallas import tpu as pltpu
from jax.sharding import PartitionSpec as P


HEAD_DIM = 64
ROT_DIM = 16
LANES = 128
f32 = jnp.float32
bf16 = jnp.bfloat16


def nn(left, right):
    return lax.dot_general(left, right, (((1,), (0,)), ((), ())), preferred_element_type=f32)


def nt(left, right):
    return lax.dot_general(left, right, (((1,), (1,)), ((), ())), preferred_element_type=f32)


def tn(left, right):
    return lax.dot_general(left, right, (((0,), (0,)), ((), ())), preferred_element_type=f32)


def fold(row):
    total = row[:, 0:LANES]
    for start in range(LANES, row.shape[1], LANES):
        total = total + row[:, start : start + LANES]
    return total


def fixed(shape):
    return pl.BlockSpec(shape, lambda *_: (0,) * len(shape), pipeline_mode=pl.Buffered(1))


def params(mib=60):
    return pltpu.CompilerParams(vmem_limit_bytes=mib * 2**20)


def z_of(at, coords):
    return ((at % 2) * 2 + at // 2) ^ coords[3]


def z_at(z, coords):
    rel = z ^ coords[3]
    return (rel % 2) * 2 + rel // 2


def put_rows(scr, x, row, coords, refs, extra=(), tiles=None):
    half = scr.shape[0] // 16
    x_rel = x ^ coords[1]

    def put(c, near, pair):
        def one(z):
            shard = z_of(z, coords) * 2 + (c ^ coords[0])
            for y in range(2):
                start = pl.multiple_of((2 * shard + (y ^ coords[2])) * half, half)
                ref, s2 = (pair[0], y) if near else (pair[y], x_rel)
                for t, tile in enumerate(tiles or range(scr.shape[1] // LANES)):
                    to = pl.ds(pl.multiple_of(row + t * half, half), half)
                    ref[(s2, z) + extra + (to, slice(None))] = scr[
                        pl.ds(start, half), tile * LANES : (tile + 1) * LANES
                    ]

        if extra:
            for z in range(4):
                one(z)
        else:
            pl.loop(0, 4)(one)

    for c in range(2):
        kept, sent = refs[2 * c : 2 * c + 2]
        near = coords[0] == c
        pl.when(near & (x_rel == 0))(functools.partial(put, c, True, (kept,)))
        pl.when(near & (x_rel == 1))(functools.partial(put, c, True, (sent,)))
        pl.when(jnp.logical_not(near))(functools.partial(put, c, False, (kept, sent)))


def prepare_kernel(
    len_ref, x_ref, cot_ref, ln_ref, h1_ref, h2_ref, h1t_ref, h2t_ref, cotm_ref, cott_ref
):
    x = x_ref[...].astype(f32)
    centred = x - jnp.mean(x, -1, keepdims=True)
    normed = centred * lax.rsqrt(jnp.mean(centred * centred, -1, keepdims=True) + 1e-05)
    h1 = (normed * ln_ref[0:1, :] + ln_ref[1:2, :]).astype(bf16)
    h2 = (normed * ln_ref[2:3, :] + ln_ref[3:4, :]).astype(bf16)
    row = pl.program_id(0) * x.shape[0] + lax.broadcasted_iota(jnp.int32, (x.shape[0], 1), 0)
    cot = jnp.where(row < len_ref[0], cot_ref[...], jnp.zeros_like(cot_ref[...]))
    h1_ref[...] = h1
    h2_ref[...] = h2
    cotm_ref[...] = cot
    h1t_ref[...] = h1.T
    h2t_ref[...] = h2.T
    cott_ref[...] = cot.T


def prepare(lengths, x, cot, ln, rows=256):
    count, width = x.shape
    block = pl.BlockSpec((rows, width), lambda i, n: (i, 0))
    turned = pl.BlockSpec((width, rows), lambda i, n: (0, i))
    straight = jax.ShapeDtypeStruct((count, width), bf16)
    across = jax.ShapeDtypeStruct((width, count), bf16)
    return pl.pallas_call(
        prepare_kernel,
        grid_spec=pltpu.PrefetchScalarGridSpec(
            num_scalar_prefetch=1,
            grid=(count // rows,),
            in_specs=[block, block, fixed(ln.shape)],
            out_specs=[block, block, turned, turned, block, turned],
        ),
        out_shape=[straight, straight, across, across, straight, across],
        compiler_params=params(),
        cost_estimate=pl.CostEstimate(
            flops=20 * count * width, bytes_accessed=12 * 2**20, transcendentals=0
        ),
        name="prepare",
    )(lengths, x, cot, ln)


def cut_kernel(co_ref, qkv_ref, out_ref, up_ref, down_ref, in_ref, in0_ref, ff_ref, ff0_ref):
    half = qkv_ref.shape[0] // 2
    unit = LANES // 2
    for y in range(2):
        for x in range(2):
            at = (y ^ co_ref[2]) * 2 + (x ^ co_ref[1])

            def fill(inner, feeds):
                row = 0
                for ref in (qkv_ref, out_ref):
                    tiles = ref.shape[1] // 2 // LANES
                    for t in range(tiles):
                        lanes = slice((x * tiles + t) * LANES, (x * tiles + t + 1) * LANES)
                        inner[row : row + half, :] = ref[y * half : (y + 1) * half, lanes]
                        row += half
                for sub in range(3):
                    for z in range(2):
                        for c in range(2):
                            tile = (2 * (2 * x + z) + c) * 3 + sub
                            row = ((3 * z + sub) * 2 + c) * half
                            feeds[0, row : row + half, :] = up_ref[
                                y * half : (y + 1) * half, tile * LANES : (tile + 1) * LANES
                            ]
                    for t in range(3):
                        row = (3 * sub + t) * unit
                        start = sub * LANES + y * unit
                        lanes = slice((3 * x + t) * LANES, (3 * x + t + 1) * LANES)
                        feeds[1, row : row + unit, :] = down_ref[start : start + unit, lanes]

            fill(in_ref.at[at], ff_ref.at[at])
            pl.when(at == 0)(lambda: fill(in0_ref, ff0_ref))


def cut(coords, qkv, out, up, down):
    whole = lambda s: pl.BlockSpec(s, lambda i, co: (0,) * len(s))
    rows = qkv.shape[0] // 2 * ((qkv.shape[1] + out.shape[1]) // 2 // LANES)
    shapes = [(4, rows, LANES), (rows, LANES), (4, 2, rows, LANES), (2, rows, LANES)]
    return pl.pallas_call(
        cut_kernel,
        grid_spec=pltpu.PrefetchScalarGridSpec(
            num_scalar_prefetch=1,
            grid=(1,),
            in_specs=[whole(entry.shape) for entry in (qkv, out, up, down)],
            out_specs=[whole(shape) for shape in shapes],
        ),
        out_shape=[jax.ShapeDtypeStruct(shape, bf16) for shape in shapes],
        compiler_params=params(),
        name="cut",
    )(coords, qkv, out, up, down)


def piece_of(parts, q, k):
    own, line, side, up, diagonal = parts
    if isinstance(k, int) and k == 0:
        return own.at[q]
    return (line, side, up, diagonal)[q].at[k - 1]


def qkv_kernel(
    co_ref, h1_ref, b_ref, c_ref, sa_ref, sb_ref,
    p0, p1, p2, p3, p4, r0, r1, r2, r3, r4, o_ref, w_ref, wo_ref,
):
    width = h1_ref.shape[1]
    half = width // 16

    @pl.when(pl.program_id(0) == 0)
    def _():
        for other, parts in enumerate(((p0, p1, p2, p3, p4), (r0, r1, r2, r3, r4))):


            def fill(k, other=other, parts=parts):
                for q in range(4):
                    ref = piece_of(parts, q, k)
                    shard = (k ^ co_ref[3]) * 2 + (other ^ co_ref[0])
                    row = pl.multiple_of(shard * 2 * half + ((q // 2) ^ co_ref[2]) * half, half)
                    x = (q % 2) ^ co_ref[1]
                    start = 0
                    for target in (w_ref, wo_ref):
                        tiles = target.shape[1] // 2 // LANES
                        for t in range(tiles):
                            lane = pl.multiple_of((x * tiles + t) * LANES, LANES)
                            target[pl.ds(row, half), pl.ds(lane, LANES)] = ref[start : start + half, :]
                            start += half

            fill(0)
            pl.loop(1, 4)(fill)

    h1 = h1_ref[...]
    cosine, ahead, behind = c_ref[...], sa_ref[...], sb_ref[...]
    low = lax.broadcasted_iota(jnp.int32, (1, LANES), 1) < HEAD_DIM

    def turn(y):
        return y * cosine - pltpu.roll(y * ahead, LANES - 8, 1) - pltpu.roll(y * behind, 8, 1)

    for part in range(3):
        cols = slice(part * width, (part + 1) * width)
        y = nn(h1, w_ref[:, cols]) + b_ref[:, cols]
        for pair in range(2):
            base = pair * 3 * LANES
            t0 = y[:, base : base + LANES]
            t1 = y[:, base + LANES : base + 2 * LANES]
            t2 = y[:, base + 2 * LANES : base + 3 * LANES]
            queries = turn(jnp.where(low, t0, t1)) * (HEAD_DIM**-0.5)
            keys = turn(pltpu.roll(jnp.where(low, t2, t0), HEAD_DIM, 1))
            at = (2 * part + pair) * LANES
            o_ref[:, at : at + LANES] = queries.astype(bf16)
            o_ref[:, width + at : width + at + LANES] = keys.astype(bf16)
            o_ref[:, 2 * width + at : 2 * width + at + LANES] = jnp.where(low, t1, t2).astype(bf16)


def qkv_forward(coords, h1, bias, tables, pieces, rows=256):
    count, width = h1.shape
    block = lambda n: pl.BlockSpec((rows, n), lambda i, co: (i, 0))
    whole = lambda s: pl.BlockSpec(s, lambda i, co: (0,) * len(s))
    arrays = [entry for part in pieces for entry in part]
    return pl.pallas_call(
        qkv_kernel,
        grid_spec=pltpu.PrefetchScalarGridSpec(
            num_scalar_prefetch=1,
            grid=(count // rows,),
            in_specs=[block(width), fixed(bias.shape)]
            + [block(LANES)] * 3
            + [fixed(entry.shape) for entry in arrays],
            out_specs=[block(3 * width), whole((width, 3 * width)), whole((width, width))],
        ),
        out_shape=[
            jax.ShapeDtypeStruct((count, 3 * width), bf16),
            jax.ShapeDtypeStruct((width, 3 * width), bf16),
            jax.ShapeDtypeStruct((width, width), bf16),
        ],
        compiler_params=params(),
        cost_estimate=pl.CostEstimate(
            flops=6 * count * width * width, bytes_accessed=18 * 2**20, transcendentals=0
        ),
        name="qkv_forward",
    )(coords, h1, bias, *tables[:3], *arrays)


def rotary_tables(count):
    half = ROT_DIM // 2
    lane = lax.broadcasted_iota(jnp.int32, (1, LANES), 1) % HEAD_DIM
    row = lax.broadcasted_iota(jnp.int32, (half, 1), 0)
    inverse = lambda at: 10000.0 ** (-(2 * (at % half)).astype(f32) / ROT_DIM)
    angles = lax.broadcasted_iota(jnp.int32, (count, 1), 0).astype(f32) * inverse(lane)
    turned = lax.broadcasted_iota(jnp.int32, (1, count), 1).astype(f32) * inverse(row)
    cosine, sine = jnp.cos(angles), jnp.sin(angles)
    return (
        jnp.where(lane < ROT_DIM, cosine, 1.0),
        jnp.where((lane >= half) & (lane < ROT_DIM), sine, 0.0),
        jnp.where(lane < half, -sine, 0.0),
        jnp.cos(turned),
        jnp.sin(turned),
    )


def attention_kernel(
    q_ref, k_ref, v_ref, cot_ref, w_ref, c_ref, sa_ref, sb_ref, ct_ref, st_ref,
    a_ref, dqkv_ref, da_ref, qt_ref, dat_ref, dq, dkt, dvt, *, rows,
):
    count = q_ref.shape[0]
    blocks = count // rows
    low = lax.broadcasted_iota(jnp.int32, (1, LANES), 1) < HEAD_DIM
    causal = lax.broadcasted_iota(jnp.int32, (rows, rows), 1) <= lax.broadcasted_iota(
        jnp.int32, (rows, rows), 0
    )
    da_ref[...] = nt(cot_ref[...], w_ref[...]).astype(bf16)
    qt_ref[...] = q_ref[...].T
    dat_ref[...] = da_ref[...].T

    def products(i, h):
        here, past = slice(i * rows, (i + 1) * rows), slice(0, i * rows)
        mine = low if h == 0 else jnp.logical_not(low)
        q, da = q_ref[here, :], da_ref[here, :]
        q = jnp.where(mine, q, jnp.zeros_like(q))
        da = jnp.where(mine, da, jnp.zeros_like(da))
        s_here, d_here = nt(q, k_ref[here, :]), nt(da, v_ref[here, :])
        if not i:
            return [s_here], [d_here]
        return [s_here, nt(q, k_ref[past, :])], [d_here, nt(da, v_ref[past, :])]

    def rest(i, h, scores, grads):
        here, past = slice(i * rows, (i + 1) * rows), slice(0, i * rows)
        head = slice(HEAD_DIM * h, HEAD_DIM * (h + 1))
        spans = (here, past)[: len(scores)]
        scores = [jnp.where(causal, scores[0], -1e30)] + scores[1:]
        highest = jnp.max(scores[0], -1, keepdims=True)
        for s in scores[1:]:
            highest = jnp.maximum(highest, jnp.max(s, -1, keepdims=True))
        raised = [jnp.exp(s - highest) for s in scores]
        inverse = 1.0 / sum(jnp.sum(e, -1, keepdims=True) for e in raised)
        probs = [e * inverse for e in raised]
        row_dot = sum(jnp.sum(p * d, -1, keepdims=True) for p, d in zip(probs, grads))
        out, grad = 0.0, 0.0
        for span, p, d in zip(spans, probs, grads):
            weights = p.astype(bf16)
            ds = (p * (d - row_dot)).astype(bf16)
            out = out + nn(weights, v_ref[span, :])
            grad = grad + nn(ds, k_ref[span, :])
            dk, dv = nn(qt_ref[head, here], ds), nn(dat_ref[head, here], weights)
            if i == blocks - 1:
                dkt[head, span], dvt[head, span] = dk, dv
            else:
                dkt[head, span] += dk
                dvt[head, span] += dv
        return out, grad

    units = [(i, h) for i in reversed(range(blocks)) for h in range(2)]
    ready = products(*units[0])
    results = {}
    for at, unit in enumerate(units):
        now = ready
        if at + 1 < len(units):
            ready = products(*units[at + 1])
        results[unit] = rest(*unit, *now)
        i, h = unit
        if h == 1:
            here = slice(i * rows, (i + 1) * rows)
            first, second = results.pop((i, 0)), results.pop((i, 1))
            a_ref[here, :] = jnp.where(low, first[0], second[0]).astype(bf16)
            y = jnp.where(low, first[1], second[1]) * (HEAD_DIM**-0.5)
            dq[here, :] = (
                y * c_ref[here, :]
                + pltpu.roll(y * sa_ref[here, :], LANES - 8, 1)
                + pltpu.roll(y * sb_ref[here, :], 8, 1)
            )
    cosine, sine = ct_ref[...], st_ref[...]
    for h in range(2):
        one = slice(HEAD_DIM * h, HEAD_DIM * h + 8)
        two = slice(HEAD_DIM * h + 8, HEAD_DIM * h + 16)
        first, second = dkt[one, :], dkt[two, :]
        dkt[one, :] = first * cosine + second * sine
        dkt[two, :] = second * cosine - first * sine
    gk = dkt[...].astype(bf16).T
    gv = dvt[...].astype(bf16).T
    gq = dq[...].astype(bf16)
    gk = jnp.concatenate([gk[:, HEAD_DIM:], gk[:, :HEAD_DIM]], 1)
    dqkv_ref[:, 0:LANES] = jnp.where(low, gq, gk)
    dqkv_ref[:, LANES : 2 * LANES] = jnp.where(low, gv, gq)
    dqkv_ref[:, 2 * LANES : 3 * LANES] = jnp.where(low, gk, gv)


def attention(qkv, cot, out_weight, tables, rows=256):
    count, width = cot.shape
    pairs = width // LANES
    column = lambda offset: pl.BlockSpec((count, LANES), lambda p: (0, offset + p))
    return pl.pallas_call(
        functools.partial(attention_kernel, rows=rows),
        grid=(pairs,),
        in_specs=[column(0), column(pairs), column(2 * pairs), fixed((count, width))]
        + [pl.BlockSpec((LANES, width), lambda p: (p, 0))]
        + [fixed((count, LANES))] * 3
        + [fixed((8, count))] * 2,
        out_specs=[column(0), pl.BlockSpec((count, 3 * LANES), lambda p: (0, p))],
        out_shape=[
            jax.ShapeDtypeStruct((count, width), bf16),
            jax.ShapeDtypeStruct((count, 3 * width), bf16),
        ],
        scratch_shapes=[
            pltpu.VMEM((count, LANES), bf16),
            pltpu.VMEM((LANES, count), bf16),
            pltpu.VMEM((LANES, count), bf16),
            pltpu.VMEM((count, LANES), f32),
            pltpu.VMEM((LANES, count), f32),
            pltpu.VMEM((LANES, count), f32),
        ],
        compiler_params=params(),
        cost_estimate=pl.CostEstimate(
            flops=30 * 10**9, bytes_accessed=20 * 2**20, transcendentals=8 * 10**6
        ),
        name="attention",
    )(qkv, qkv, qkv, cot, out_weight, *tables)


def feed_kernel(
    co_ref, h2_ref, h2t_ref, cot_ref, cott_ref, upb_ref, acc0_ref, before_ref,
    p0, p1, p2, p3, p4, r0, r1, r2, r3, r4, e0, e1, e2, e3, e4, f0, f1, f2, f3, f4,
    mix_ref, k0_ref, s0_ref, k1_ref, s1_ref, ubg_ref, dh2_ref, sq_ref, up_ref, down_ref, us, ds, g_ref, du_ref, *acc,
):
    j = pl.program_id(0)
    side, sub = j % 2, j // 2
    rows = up_ref.shape[0] // 16
    unit = LANES // 2
    x_here = side ^ co_ref[1]
    acc_ref = acc[0] if acc else mix_ref

    @pl.when(j == 0)
    def _():
        acc_ref[...] = acc0_ref[...]
        dh2_ref[...] = jnp.zeros_like(dh2_ref) if before_ref is None else before_ref[...]
        sq_ref[...] = jnp.zeros_like(sq_ref)

    def fill_up(x, k):
        for other, parts in enumerate(((p0, p1, p2, p3, p4), (r0, r1, r2, r3, r4))):
            for y in range(2):
                ref = piece_of(parts, 2 * y + x, k)
                shard = (k ^ co_ref[3]) * 2 + (other ^ co_ref[0])
                row = pl.multiple_of((2 * shard + (y ^ co_ref[2])) * rows, rows)
                for t in range(4):
                    up_ref[pl.ds(row, rows), t * LANES : (t + 1) * LANES] = ref[
                        0, t // 2, 0, (t % 2) * rows : (t % 2 + 1) * rows, :
                    ]

    for x in range(2):

        @pl.when(x_here == x)
        def _(x=x):
            fill_up(x, 0)
            pl.loop(1, 4)(lambda k: fill_up(x, k))


    def fill_down(k):
        z = k ^ co_ref[3]
        for other, parts in enumerate(((e0, e1, e2, e3, e4), (f0, f1, f2, f3, f4))):
            first = (2 * (z % 2) + (other ^ co_ref[0])) * LANES
            for q in range(4):
                ref = piece_of(parts, q, k)
                row = pl.multiple_of(first + ((q // 2) ^ co_ref[2]) * unit, unit)
                for t in range(3):
                    lane = pl.multiple_of((((q % 2) ^ co_ref[1]) * 3 + t) * LANES, LANES)
                    down_ref[pl.ds(row, unit), pl.ds(lane, LANES)] = ref[0, t * unit : (t + 1) * unit, :]

    pl.when(co_ref[3] // 2 == side)(lambda: fill_down(0))

    @pl.loop(1, 4)
    def _(k):
        pl.when((k ^ co_ref[3]) // 2 == side)(lambda: fill_down(k))


    part = g_ref.shape[0] // 2
    ubg_ref[...] = jnp.zeros_like(ubg_ref)

    @pl.loop(0, 2)
    def _(at):
        here = pl.ds(pl.multiple_of(at * part, part), part)
        u = nn(h2_ref[here, :], up_ref[...]) + upb_ref[...]
        act = nt(cot_ref[here, :], down_ref[...])
        cdf = 0.5 * (1.0 + lax.erf(u * math.sqrt(0.5)))
        pdf = jnp.exp(-0.5 * u * u) * (1.0 / math.sqrt(2.0 * math.pi))
        g = (u * cdf).astype(bf16)
        du = (act * (cdf + u * pdf)).astype(bf16)
        g_ref[here, :] = g
        du_ref[here, :] = du
        ubg_ref[...] += jnp.sum(du.astype(f32), 0, keepdims=True)
        acc_ref[here, :] += nn(g, down_ref[...])
        dh2_ref[here, :] += nt(du, up_ref[...])

    bias_grad = ubg_ref[...]
    up_grad = nn(h2t_ref[...], du_ref[...])
    us[...] = up_grad.astype(bf16)
    down_grad = nn(cott_ref[...], g_ref[...])
    ds[...] = down_grad.astype(bf16)
    refs = (k0_ref, s0_ref, k1_ref, s1_ref)
    for x in range(2):
        put_rows(us, x, (2 * sub + side) * 2 * rows, co_ref, refs, tiles=(2 * x, 2 * x + 1))
    first = pl.num_programs(0) * 2 * rows

    def put_down(c, pair):
        for z in range(2):
            tile = 2 * z + c
            for x in range(2):
                for y in range(2):
                    ref, s2 = (pair[x], y) if c == 0 else (pair[y], x)
                    for t in range(3):
                        start = ((x ^ co_ref[1]) * 3 + t) * LANES + (y ^ co_ref[2]) * unit
                        to = pl.ds(pl.multiple_of(first + (3 * sub + t) * unit, unit), unit)
                        ref[s2, z_at(2 * side + z, co_ref), to, :] = ds[
                            pl.ds(pl.multiple_of(start, unit), unit), tile * LANES : (tile + 1) * LANES
                        ]

    for c in range(2):
        pl.when(co_ref[0] == c)(functools.partial(put_down, c, refs[:2]))
        pl.when(co_ref[0] != c)(functools.partial(put_down, c, refs[2:]))
    sq_ref[0:1, :] += fold(
        jnp.sum(up_grad * up_grad + down_grad * down_grad, 0, keepdims=True)
        + bias_grad * bias_grad
    )
    if not acc:
        return

    @pl.when(j == pl.num_programs(0) - 1)
    def _():
        row = lax.broadcasted_iota(jnp.int32, (mix_ref.shape[0], 1), 0)
        mix_ref[...] = jnp.where(row < co_ref[4], acc_ref[...], 0.0).astype(bf16)


def feed(coords, h2, h2t, cot, cott, up_bias, acc, before, pieces, first, subs):
    count, width = h2.shape
    tile = 4 * LANES
    hidden = 2 * subs * tile
    rows = width // 16
    last = before is not None
    piece = jax.ShapeDtypeStruct((2, 4, subs * (4 * rows + 3 * LANES // 2), LANES), bf16)
    up_pieces = [
        [entry.reshape(*entry.shape[:2], 2, 3, 2 * rows, LANES) for entry in part] for part in pieces
    ]
    up_spec = lambda n: pl.BlockSpec(
        (n, 1, 2, 1, 2 * rows, LANES), lambda j, co: (0, 0, 0, first + j // 2, 0, 0)
    )
    down_spec = lambda n: pl.BlockSpec(
        (n, 1, 3 * LANES // 2, LANES), lambda j, co: (0, 1, first + j // 2, 0)
    )
    up_parts = [up_spec(4)] + [up_spec(3)] * 4
    down_parts = [down_spec(4)] + [down_spec(3)] * 4
    up_arrays = [entry for part in up_pieces for entry in part]
    arrays = [entry for part in pieces for entry in part]
    whole = lambda s: pl.BlockSpec(s, lambda j, co: (0,) * len(s))
    start = [before] if last else []
    kernel = feed_kernel
    if not last:
        kernel = lambda *refs: feed_kernel(*refs[:7], None, *refs[7:])
    return pl.pallas_call(
        kernel,
        grid_spec=pltpu.PrefetchScalarGridSpec(
            num_scalar_prefetch=1,
            grid=(2 * subs,),
            in_specs=[
                fixed((count, width)),
                fixed((width, count)),
                fixed((count, width)),
                fixed((width, count)),
                pl.BlockSpec((1, tile), lambda j, co: (0, 2 * first + j)),
                fixed((count, width)),
            ]
            + [fixed((count, width))] * len(start)
            + up_parts * 2
            + down_parts * 2,
            out_specs=[whole((count, width))]
            + [whole(piece.shape)] * 4
            + [
                pl.BlockSpec((1, tile), lambda j, co: (0, j)),
                whole((count, width)),
                whole((8, LANES)),
            ],
            scratch_shapes=[
                pltpu.VMEM((width, tile), bf16),
                pltpu.VMEM((tile, width), bf16),
                pltpu.VMEM((width, tile), bf16),
                pltpu.VMEM((width, tile), bf16),
                pltpu.VMEM((count, tile), bf16),
                pltpu.VMEM((count, tile), bf16),
            ]
            + [pltpu.VMEM((count, width), f32)] * len(start),
        ),
        out_shape=[jax.ShapeDtypeStruct((count, width), bf16 if last else f32)]
        + [piece] * 4
        + [
            jax.ShapeDtypeStruct((1, hidden), f32),
            jax.ShapeDtypeStruct((count, width), f32),
            jax.ShapeDtypeStruct((8, LANES), f32),
        ],
        compiler_params=params(),
        cost_estimate=pl.CostEstimate(
            flops=12 * count * width * hidden,
            bytes_accessed=12 * subs * 2**20,
            transcendentals=2 * count * hidden,
        ),
        name="feed",
    )(coords, h2, h2t, cot, cott, up_bias, acc, *start, *up_arrays, *arrays)


def inner_kernel(
    co_ref, h1t_ref, dqkv_ref, w_ref, heads_ref, cot_ref, x_ref, wo_ref, ob_ref,
    k0_ref, s0_ref, k1_ref, s1_ref, bias_ref, cotsum_ref, dh1_ref, acc_ref, sq_ref, scr,
):
    j = pl.program_id(0)
    inner = j < pl.num_programs(0) - 1

    @pl.when(j == 0)
    def _():
        sq_ref[...] = jnp.zeros_like(sq_ref)

    @pl.when(inner)
    def _():
        right = dqkv_ref[...]
        grad = nn(h1t_ref[...], right)
        scr[...] = grad.astype(bf16)
        bias_grad = jnp.sum(right.astype(f32), 0, keepdims=True)
        bias_ref[...] = bias_grad
        part = nt(right, w_ref[...])

        @pl.when(j == 0)
        def _():
            dh1_ref[...] = part

        @pl.when(j > 0)
        def _():
            dh1_ref[...] += part

        sq_ref[0:1, :] += fold(jnp.sum(grad * grad, 0, keepdims=True) + bias_grad * bias_grad)

    @pl.when(jnp.logical_not(inner))
    def _():
        right = cot_ref[...]
        grad = tn(heads_ref[...], right)
        scr[...] = grad.astype(bf16)
        bias_grad = jnp.sum(right.astype(f32), 0, keepdims=True)
        cotsum_ref[...] = bias_grad
        acc_ref[...] = x_ref[...].astype(f32) + nn(heads_ref[...], wo_ref[...]) + ob_ref[...]
        sq_ref[0:1, :] += fold(jnp.sum(grad * grad, 0, keepdims=True) + 2.0 * bias_grad * bias_grad)

    half = scr.shape[1] // LANES // 2
    for x in range(2):
        tiles = range(x * half, (x + 1) * half)
        put_rows(scr, x, 0, co_ref, (k0_ref, s0_ref, k1_ref, s1_ref), (0,), tiles)


def inner_grads(coords, h1t, dqkv, weight, heads, cot, x, out_weight, out_bias):
    count, width = heads.shape
    cols = dqkv.shape[1]
    tile = width
    steps = cols // tile + 1
    inner = lambda j: jnp.minimum(j, steps - 2)
    piece = jax.ShapeDtypeStruct((2, 4, steps, tile // LANES // 2 * width // 16, LANES), bf16)
    spec = pl.BlockSpec((2, 4, 1) + piece.shape[3:], lambda j, co: (0, 0, j, 0, 0))
    outer_block = lambda r: fixed((r, tile))
    outer_out = lambda r: pl.BlockSpec((r, tile), lambda j, co: (0, 0))
    return pl.pallas_call(
        inner_kernel,
        grid_spec=pltpu.PrefetchScalarGridSpec(
            num_scalar_prefetch=1,
            grid=(steps,),
            in_specs=[
                fixed((width, count)),
                pl.BlockSpec((count, tile), lambda j, co: (0, inner(j))),
                pl.BlockSpec((width, tile), lambda j, co: (0, inner(j))),
                fixed((count, width)),
                outer_block(count),
                outer_block(count),
                outer_block(width),
                outer_block(1),
            ],
            out_specs=[spec] * 4
            + [
                pl.BlockSpec((1, tile), lambda j, co: (0, inner(j))),
                outer_out(1),
                pl.BlockSpec((count, width), lambda j, co: (0, 0)),
                outer_out(count),
                pl.BlockSpec((8, LANES), lambda j, co: (0, 0)),
            ],
            scratch_shapes=[pltpu.VMEM((width, tile), bf16)],
        ),
        out_shape=[piece] * 4
        + [
            jax.ShapeDtypeStruct((1, cols), f32),
            jax.ShapeDtypeStruct((1, width), f32),
            jax.ShapeDtypeStruct((count, width), f32),
            jax.ShapeDtypeStruct((count, width), f32),
            jax.ShapeDtypeStruct((8, LANES), f32),
        ],
        compiler_params=params(),
        cost_estimate=pl.CostEstimate(
            flops=16 * count * width * width, bytes_accessed=24 * 2**20, transcendentals=0
        ),
        name="inner_grads",
    )(coords, h1t, dqkv, weight, heads, cot, x, out_weight, out_bias)


def combine_kernel(scale_ref, co_ref, *refs, vectors):
    pieces, out_ref = refs[:4], refs[-1]
    weigh = lambda parts: sum(scale_ref[at] * part.astype(f32) for at, part in enumerate(parts)).astype(bf16)
    rows = pieces[0].shape[2]
    out_ref[0, :rows] = weigh([ref[0, 0] for ref in pieces])
    if vectors:
        owner = 2 * z_of(pl.program_id(0), co_ref) + co_ref[0]
        out_ref[0, rows:] = weigh([ref[pl.ds(owner, 1)][0] for ref in refs[4:8]])


def combine(scales, coords, s2, arrays, vectors=()):
    rows = arrays[0].shape[2]
    extra = vectors[0].shape[1] if vectors else 0
    return pl.pallas_call(
        functools.partial(combine_kernel, vectors=bool(vectors)),
        grid_spec=pltpu.PrefetchScalarGridSpec(
            num_scalar_prefetch=2,
            grid=(4,),
            in_specs=[pl.BlockSpec((1, 1, rows, LANES), lambda i, s, co: (s2, i, 0, 0))] * 4
            + [fixed(entry.shape) for entry in vectors],
            out_specs=pl.BlockSpec((1, rows + extra, LANES), lambda i, s, co: (i, 0, 0)),
        ),
        out_shape=jax.ShapeDtypeStruct((4, rows + extra, LANES), bf16),
        compiler_params=params(),
        cost_estimate=pl.CostEstimate(
            flops=10**7, bytes_accessed=40 * rows * LANES, transcendentals=0
        ),
        name="combine",
    )(scales, coords, *arrays, *vectors)


def pack_kernel(ln_ref, qkv_ref, cot_ref, ub1_ref, ub2_ref, out_ref, row_ref):
    out_ref[...] = jnp.zeros_like(out_ref)
    for f in range(8):
        to = 0
        sources = [ln_ref.at[i : i + 1] for i in range(4)] + [qkv_ref, cot_ref]
        for ref in sources:
            size = ref.shape[1] // 8
            row_ref[f : f + 1, to : to + size] = ref[:, f * size : (f + 1) * size]
            to += size
        for sub in range(3):
            ref, at = (ub1_ref, 8 * sub + f) if sub < 2 else (ub2_ref, f)
            row_ref[f : f + 1, to : to + LANES] = ref[:, at * LANES : (at + 1) * LANES]
            to += LANES
        for row in range(row_ref.shape[1] // LANES):
            out_ref[f, row : row + 1, :] = row_ref[f : f + 1, row * LANES : (row + 1) * LANES]


def pack(*arrays):
    whole = lambda s: pl.BlockSpec(s, lambda i: (0,) * len(s))
    width = (4 * arrays[0].shape[1] + sum(entry.shape[1] for entry in arrays[1:])) // 8
    rows = -(-width // LANES // 16) * 16
    return pl.pallas_call(
        pack_kernel,
        grid=(1,),
        in_specs=[whole(entry.shape) for entry in arrays],
        out_specs=whole((8, rows, LANES)),
        out_shape=jax.ShapeDtypeStruct((8, rows, LANES), f32),
        scratch_shapes=[pltpu.VMEM((8, width), f32)],
        compiler_params=params(),
        name="pack",
    )(*arrays)


def finish_kernel(co_ref, *refs):
    groups = refs[0:4], refs[4:8], refs[8:12]
    gq_ref, go_ref, gu_ref, gd_ref, gv_ref = refs[12:17]
    half = gq_ref.shape[0] // 2
    unit = LANES // 2
    for group, parts, scr in zip(range(3), groups, refs[17:20]):
        for at, part in enumerate(parts):
            scr[((at // 2) ^ co_ref[2]) * 2 + ((at % 2) ^ co_ref[1])] = part[...]
        for y in range(2):
            rows = slice(y * half, (y + 1) * half)
            for x in range(2):
                owner = 2 * y + x
                if group == 0:
                    for window in range(4):
                        for t in range(3):
                            at = (window * 3 + t) * half
                            value = scr[owner, at : at + half, :].astype(f32)
                            ref, tile = gq_ref, (2 * window + x) * 3 + t
                            if window == 3:
                                ref, tile = go_ref, x * 3 + t
                            ref[rows, tile * LANES : (tile + 1) * LANES] = value
                    continue
                for i in range(2 // group):
                    sub = 2 * (group - 1) + i
                    for z in range(2):
                        for c in range(2):
                            at = ((2 * i + z) * 2 + c) * half
                            tile = (2 * (2 * z + x) + c) * 3 + sub
                            gu_ref[rows, tile * LANES : (tile + 1) * LANES] = scr[
                                owner, at : at + half, :
                            ].astype(f32)
        if group == 0:
            continue
        for i in range(2 // group):
            sub = 2 * (group - 1) + i
            for x in range(2):
                for t in range(3):
                    at = 4 * (2 // group) * half + (3 * i + t) * unit
                    block = jnp.concatenate([scr[2 * y + x, at : at + unit, :] for y in range(2)], 0)
                    lanes = slice((3 * x + t) * LANES, (3 * x + t + 1) * LANES)
                    gd_ref[sub * LANES : (sub + 1) * LANES, lanes] = block.astype(f32).T
    gv_ref[...] = scr[0, scr.shape[1] - gv_ref.shape[0] :, :].astype(f32)


def finish(coords, groups, shapes):
    whole = lambda s: pl.BlockSpec(s, lambda i, co: (0,) * len(s))
    arrays = [entry for group in groups for entry in group]
    return pl.pallas_call(
        finish_kernel,
        grid_spec=pltpu.PrefetchScalarGridSpec(
            num_scalar_prefetch=1,
            grid=(1,),
            in_specs=[whole(entry.shape) for entry in arrays],
            out_specs=[whole(s) for s in shapes],
            scratch_shapes=[pltpu.VMEM((4,) + group[0].shape, bf16) for group in groups],
        ),
        out_shape=[jax.ShapeDtypeStruct(s, f32) for s in shapes],
        compiler_params=params(),
        name="finish",
    )(coords, *arrays)


def norm_back_kernel(x_ref, cot_ref, dh1_ref, dh2_ref, ln_ref, dx_ref, sums_ref):
    x = x_ref[...].astype(f32)
    centred = x - jnp.mean(x, -1, keepdims=True)
    inverse = lax.rsqrt(jnp.mean(centred * centred, -1, keepdims=True) + 1e-05)
    normed = centred * inverse
    dh1, dh2 = dh1_ref[...], dh2_ref[...]
    scaled = dh1 * ln_ref[0:1, :] + dh2 * ln_ref[2:3, :]
    spread = (
        scaled
        - jnp.mean(scaled, -1, keepdims=True)
        - normed * jnp.mean(scaled * normed, -1, keepdims=True)
    )
    dx_ref[...] = cot_ref[...].astype(f32) + inverse * spread

    @pl.when(pl.program_id(0) == 0)
    def _():
        sums_ref[...] = jnp.zeros_like(sums_ref)

    for row, value in enumerate((dh1 * normed, dh1, dh2 * normed, dh2)):
        sums_ref[row : row + 1, :] += jnp.sum(value, 0, keepdims=True)


def norm_back(x, cot, dh1, dh2, ln, rows=256):
    count, width = x.shape
    block = pl.BlockSpec((rows, width), lambda i: (i, 0))
    return pl.pallas_call(
        norm_back_kernel,
        grid=(count // rows,),
        in_specs=[block] * 4 + [fixed(ln.shape)],
        out_specs=[block, pl.BlockSpec((8, width), lambda i: (0, 0))],
        out_shape=[
            jax.ShapeDtypeStruct((count, width), f32),
            jax.ShapeDtypeStruct((8, width), f32),
        ],
        compiler_params=params(),
        cost_estimate=pl.CostEstimate(
            flops=30 * count * width, bytes_accessed=12 * 2**20, transcendentals=0
        ),
        name="norm_back",
    )(x, cot, dh1, dh2, ln)


def body(
    tokens_in, ln1_gain, ln1_bias, ln2_gain, ln2_bias, qkv_weight, qkv_bias, out_weight, out_bias,
    up_weight, up_bias, down_weight, down_bias, cotangent, lengths, assignment, clip_bound,
):
    dp, fsdp = lax.axis_size("dp"), lax.axis_size("fsdp")
    both = ("dp", "fsdp")
    total = dp * fsdp
    fast = (dp, fsdp) == (4, 8)
    me = lax.axis_index("dp") * fsdp + lax.axis_index("fsdp")

    def swap(value, even, odd=None):
        pairs = [(i, i ^ (even if odd is None or i % 2 == 0 else odd)) for i in range(total)]
        return lax.ppermute(value, both, pairs)

    width = tokens_in.shape[2]
    smalls = (ln1_gain, ln1_bias, ln2_gain, ln2_bias, qkv_bias, out_bias, up_bias, down_bias)
    packed = jnp.concatenate(smalls)
    if fast:
        slot = lax.broadcasted_iota(jnp.int32, (fsdp, 1), 0) == lax.axis_index("fsdp")
        rows = jnp.where(slot, packed[None, :], jnp.zeros_like(packed)[None, :])
        for at in range(3):
            rows = rows + swap(rows, 2**at)
    else:
        rows = lax.all_gather(packed, "fsdp", axis=0)
    vectors, start = [], 0
    for entry in smalls:
        stop = start + entry.shape[0]
        vectors.append(rows[:, start:stop].reshape(1, -1).astype(f32))
        start = stop
    ln = jnp.concatenate(vectors[:4] + [jnp.zeros((4, vectors[0].shape[1]), f32)], 0)
    qkv_b, out_b, up_b, down_b = vectors[4:]

    spot = [me & 1, (me >> 3) & 1, (me >> 4) & 1, (me >> 1) & 3] if fast else [0 * me] * 4
    coords = jnp.stack(spot + [lengths[0]]).astype(jnp.int32)
    if fast:
        in_own, in_mine, ff_own, ff_mine = cut(coords, qkv_weight, out_weight, up_weight, down_weight)
        lines = []
        for piece in (in_mine, ff_mine):
            lines.append([swap(piece, 2 * k) for k in (1, 2, 3)])
        gathered = []
        for own, line in ((in_own, lines[0]), (ff_own, lines[1])):
            line = lax.optimization_barrier(jnp.stack(line))
            mine = [own, line] + [swap(line, 8 * way) for way in (1, 2, 3)]
            theirs = [swap(entry, 1) for entry in mine]
            gathered.append((mine, theirs))
    else:
        whole = [
            lax.all_gather(w, "fsdp", axis=0, tiled=True)
            for w in (qkv_weight, out_weight, up_weight, down_weight)
        ]
        flat = lambda w: w.reshape(4, 2, 2, w.shape[0] // 16, 2, -1, LANES).transpose(
            0, 1, 2, 4, 5, 3, 6
        ).reshape(4, 2, 4, -1, LANES)
        qkv_p, out_p, up_p = (flat(w) for w in whole[:3])
        down_p = whole[3].reshape(4, 2, 3, 2, LANES // 2, 2, 3, LANES).transpose(0, 1, 3, 5, 2, 6, 4, 7)
        down_p = down_p.reshape(up_p.shape)
        up_p = up_p.reshape(4, 2, 4, 2, 2, 3, width // 16, LANES).swapaxes(4, 5).reshape(up_p.shape)
        gathered = []
        for entry in (jnp.concatenate([qkv_p, out_p], 3), jnp.stack([up_p, down_p], 3)):
            gathered.append(
                tuple([entry[0, c]] + [entry[1:, c, q] for q in range(4)] for c in range(2))
            )

    tokens = tokens_in[0]
    count, width = tokens.shape
    tables = rotary_tables(count)
    h1, h2, h1t, h2t, cot, cott = prepare(lengths, tokens, cotangent[0], ln)
    qkv, w_qkv, w_out = qkv_forward(coords, h1, qkv_b, tables, gathered[0])
    heads, dqkv = attention(qkv, cot, w_out, tables)
    *in_pieces, qkv_bias_grad, cot_sum, dh1, acc, in_sq = inner_grads(
        coords, h1t, dqkv, w_qkv, heads, cot, tokens, w_out, out_b + down_b
    )
    up_b = up_b.reshape(8, 3, LANES).swapaxes(0, 1).reshape(1, -1)
    ff = (coords, h2, h2t, cot, cott, up_b)
    acc, *f1_pieces, ub_grad1, dh2, f1_sq = feed(*ff, acc, None, gathered[1], 0, 2)
    mixed, *f2_pieces, ub_grad2, dh2, f2_sq = feed(*ff, acc, dh2, gathered[1], 2, 1)
    groups = []
    for pieces in (in_pieces, f1_pieces, f2_pieces):
        kept, sent, kept_other, sent_other = (entry.reshape(2, 4, -1, LANES) for entry in pieces)
        if fast:
            sent, sent_other = swap(sent, 8, 16), swap(sent_other, 16, 8)
            kept_other, sent_other = swap(kept_other, 1), swap(sent_other, 1)
        groups.append((kept, sent, kept_other, sent_other))
    dx, ln_sums = norm_back(tokens, cot, dh1, dh2, ln)
    ln_grads = ln_sums[:4]

    squares = jnp.sum(in_sq + f1_sq + f2_sq) + jnp.sum(ln_grads * ln_grads)
    slots = jnp.arange(total, dtype=jnp.int32)
    facts = jnp.stack([squares, assignment[0].astype(f32)])[:, None]
    facts = jnp.where(slots[None, :] == me, facts, 0.0)
    if fast:
        facts = facts + swap(facts, 1)
        packed = pack(ln_sums, qkv_bias_grad, cot_sum, ub_grad1, ub_grad2)
        vectors = [packed, swap(packed, 8, 16)]
        facts = facts + swap(facts, 8) + swap(facts, 16) + swap(facts, 24)
        vectors += [swap(packed, 1), swap(packed, 17, 9)]
        facts = facts + swap(facts, 2) + swap(facts, 4) + swap(facts, 6)
    else:
        facts = lax.psum(facts, both)
    norms, numbers = jnp.sqrt(facts[0]), facts[1].astype(jnp.int32)
    ahead = (norms[None, :] < norms[:, None]) | (
        (norms[None, :] == norms[:, None]) & (slots[None, :] < slots[:, None])
    )
    rank = jnp.sum(ahead.astype(jnp.int32), 1)
    median = jnp.sum(jnp.where(rank == total // 2, norms, 0.0))
    bound = median * clip_bound[0].astype(f32) / 8.0
    slot_scale = jnp.minimum(1.0, bound / (norms + 1e-06))
    clip_scale = jnp.sum(jnp.where(numbers[None, :] == slots[:, None], slot_scale[None, :], 0.0), 1)
    if fast:
        next_slot = me ^ jnp.where(me % 2 == 0, 8, 16)
        sources = jnp.stack([me, next_slot, me ^ 1, next_slot ^ 1])
    else:
        sources = jnp.stack([me] * 4)
    own_scales = jnp.sum(jnp.where(slots[None, :] == sources[:, None], slot_scale[None, :], 0.0), 1)
    own = own_scales[0]
    scales = own_scales / total
    share = scales[0]

    if fast:
        finals, kepts = [], []
        for arrays, more in zip(groups, ((), (), vectors)):
            sent = combine(scales, coords, 1, arrays, more)
            kepts.append(swap(sent, 16, 8))
        for name, arrays, came, more in zip("abc", groups, kepts, ((), (), vectors)):
            kept = combine(scales, coords, 0, arrays, more)
            add = lambda at, *more: sum((e.astype(f32) for e in more), kept[at].astype(f32) + came[at])
            near = swap(add(slice(2, 4)).astype(bf16), 2)
            last = swap(add(1, near[1]).astype(bf16), 4)
            line = add(0, near[0], last).astype(bf16)
            along_x, along_y = swap(line, 8), swap(line, 16)
            turn = (along_y, 8) if name == "b" else (along_x, 16)
            finals.append((line, along_x, along_y, swap(*turn)))
        own_rows = width // fsdp
        hidden = up_b.shape[1]
        shapes = [(own_rows, 3 * width), (own_rows, width), (own_rows, hidden)]
        shapes += [(hidden // fsdp, width), vectors[0].shape[1:]]
        gq, go, gu, gd, own_row = finish(coords, finals, shapes)
        own_row = own_row.reshape(-1)
    else:
        up_bias_grad = jnp.concatenate([ub_grad1, ub_grad2], 1).reshape(3, 8, LANES).swapaxes(0, 1)
        vector_grads = [ln_grads[i] for i in range(4)] + [qkv_bias_grad, cot_sum, up_bias_grad]
        vector_grads = jnp.concatenate([entry.reshape(fsdp, -1) for entry in vector_grads], 1)
        vector_grads = lax.psum(vector_grads * share, both)
        own_row = lax.dynamic_index_in_dim(vector_grads, lax.axis_index("fsdp"), 0, keepdims=False)

        def plain(arrays):
            kept, sent, kept_other, sent_other = (
                entry.reshape(2, 2, 2, -1, LANES).swapaxes(1, 2).reshape(entry.shape)
                for entry in arrays
            )
            return jnp.stack([jnp.stack([kept, sent]), jnp.stack([kept_other, sent_other], 1)])

        half = width // 16
        inner = plain(groups[0]).reshape(2, 2, 2, 4, 4, 3, half, LANES)
        flat = lambda e: e.transpose(3, 0, 2, 6, 4, 1, 5, 7).reshape(width, -1)
        outs = [flat(inner[:, :, :, :, :3]), flat(inner[:, :, :, :, 3:])]
        ups, downs = [], []
        for entry in groups[1:]:
            up, down = jnp.split(plain(entry), 2, 4)
            ups.append(up.reshape(2, 2, 2, 4, -1, 2, 2, half, LANES))
            downs.append(down.reshape(2, 2, 2, 4, -1, 3, LANES // 2, LANES))
        up, down = jnp.concatenate(ups, 4), jnp.concatenate(downs, 4)
        outs.append(up.transpose(3, 0, 2, 7, 5, 1, 6, 4, 8).reshape(width, -1))
        outs.append(down.transpose(3, 0, 4, 7, 1, 5, 2, 6).reshape(-1, width))
        outs = [(entry.astype(f32) * share).astype(bf16) for entry in outs]
        gq, go, gu, gd = (
            lax.psum(
                lax.psum_scatter(w, "fsdp", scatter_dimension=0, tiled=True).astype(f32), "dp"
            )
            for w in outs
        )

    tokens_grad = (own * dx).astype(bf16)[None]
    sizes = [ln1_gain.shape[0]] * 4 + [qkv_bias.shape[0], out_bias.shape[0], up_bias.shape[0]]
    parts, start = [], 0
    for size in sizes:
        parts.append(own_row[start : start + size])
        start += size
    g1, b1, g2, b2, gqb, gob, gub = parts
    return (mixed[None], tokens_grad, clip_scale, g1, b1, g2, b2, gq, gqb, go, gob, gu, gub, gd, gob)


def solution(mesh):
    step = mapped(mesh)
    if dict(mesh.shape) != {"dp": 4, "fsdp": 8}:
        return step
    return step


def mapped(mesh):
    rows, cols, flat = P("fsdp", None), P("fsdp"), P(("dp", "fsdp"))
    slots = P(("dp", "fsdp"), None, None)
    return jax.shard_map(
        body,
        mesh=mesh,
        in_specs=(slots, cols, cols, cols, cols, rows, cols, rows, cols, rows, cols, rows, cols)
        + (slots, flat, flat, P()),
        out_specs=(slots, slots, P(), cols, cols, cols, cols, rows, cols, rows, cols, rows, cols)
        + (rows, cols),
        check_vma=False,
    )
```

```python
import functools
import math

import jax
import jax.numpy as jnp
from jax import lax
from jax.experimental import pallas as pl
from jax.experimental.pallas import tpu as pltpu
from jax.sharding import PartitionSpec as P


HEAD_DIM = 64
ROT_DIM = 16
LANES = 128
f32 = jnp.float32
bf16 = jnp.bfloat16


def nn(left, right):
    return lax.dot_general(left, right, (((1,), (0,)), ((), ())), preferred_element_type=f32)


def nt(left, right):
    return lax.dot_general(left, right, (((1,), (1,)), ((), ())), preferred_element_type=f32)


def tn(left, right):
    return lax.dot_general(left, right, (((0,), (0,)), ((), ())), preferred_element_type=f32)


def fold(row):
    total = row[:, 0:LANES]
    for start in range(LANES, row.shape[1], LANES):
        total = total + row[:, start : start + LANES]
    return total


def fixed(shape):
    return pl.BlockSpec(shape, lambda *_: (0,) * len(shape), pipeline_mode=pl.Buffered(1))


def params(mib=60):
    return pltpu.CompilerParams(vmem_limit_bytes=mib * 2**20)


def z_of(at, coords):
    return ((at % 2) * 2 + at // 2) ^ coords[3]


def z_at(z, coords):
    rel = z ^ coords[3]
    return (rel % 2) * 2 + rel // 2


def put_rows(scr, x, row, coords, refs, extra=(), tiles=None):
    half = scr.shape[0] // 16
    x_rel = x ^ coords[1]

    def put(c, near, pair):
        def one(z):
            shard = z_of(z, coords) * 2 + (c ^ coords[0])
            for y in range(2):
                start = pl.multiple_of((2 * shard + (y ^ coords[2])) * half, half)
                ref, s2 = (pair[0], y) if near else (pair[y], x_rel)
                for t, tile in enumerate(tiles or range(scr.shape[1] // LANES)):
                    to = pl.ds(pl.multiple_of(row + t * half, half), half)
                    ref[(s2, z) + extra + (to, slice(None))] = scr[
                        pl.ds(start, half), tile * LANES : (tile + 1) * LANES
                    ]

        if extra:
            for z in range(4):
                one(z)
        else:
            pl.loop(0, 4)(one)

    for c in range(2):
        kept, sent = refs[2 * c : 2 * c + 2]
        near = coords[0] == c
        pl.when(near & (x_rel == 0))(functools.partial(put, c, True, (kept,)))
        pl.when(near & (x_rel == 1))(functools.partial(put, c, True, (sent,)))
        pl.when(jnp.logical_not(near))(functools.partial(put, c, False, (kept, sent)))


def prepare_kernel(
    len_ref, x_ref, cot_ref, ln_ref, h1_ref, h2_ref, h1t_ref, h2t_ref, cotm_ref, cott_ref
):
    x = x_ref[...].astype(f32)
    centred = x - jnp.mean(x, -1, keepdims=True)
    normed = centred * lax.rsqrt(jnp.mean(centred * centred, -1, keepdims=True) + 1e-05)
    h1 = (normed * ln_ref[0:1, :] + ln_ref[1:2, :]).astype(bf16)
    h2 = (normed * ln_ref[2:3, :] + ln_ref[3:4, :]).astype(bf16)
    row = pl.program_id(0) * x.shape[0] + lax.broadcasted_iota(jnp.int32, (x.shape[0], 1), 0)
    cot = jnp.where(row < len_ref[0], cot_ref[...], jnp.zeros_like(cot_ref[...]))
    h1_ref[...] = h1
    h2_ref[...] = h2
    cotm_ref[...] = cot
    h1t_ref[...] = h1.T
    h2t_ref[...] = h2.T
    cott_ref[...] = cot.T


def prepare(lengths, x, cot, ln, rows=256):
    count, width = x.shape
    block = pl.BlockSpec((rows, width), lambda i, n: (i, 0))
    turned = pl.BlockSpec((width, rows), lambda i, n: (0, i))
    straight = jax.ShapeDtypeStruct((count, width), bf16)
    across = jax.ShapeDtypeStruct((width, count), bf16)
    return pl.pallas_call(
        prepare_kernel,
        grid_spec=pltpu.PrefetchScalarGridSpec(
            num_scalar_prefetch=1,
            grid=(count // rows,),
            in_specs=[block, block, fixed(ln.shape)],
            out_specs=[block, block, turned, turned, block, turned],
        ),
        out_shape=[straight, straight, across, across, straight, across],
        compiler_params=params(),
        cost_estimate=pl.CostEstimate(
            flops=20 * count * width, bytes_accessed=12 * 2**20, transcendentals=0
        ),
        name="prepare",
    )(lengths, x, cot, ln)


def cut_kernel(co_ref, qkv_ref, out_ref, up_ref, down_ref, in_ref, in0_ref, ff_ref, ff0_ref):
    half = qkv_ref.shape[0] // 2
    unit = LANES // 2
    for y in range(2):
        for x in range(2):
            at = (y ^ co_ref[2]) * 2 + (x ^ co_ref[1])

            def fill(inner, feeds):
                row = 0
                for ref in (qkv_ref, out_ref):
                    tiles = ref.shape[1] // 2 // LANES
                    for t in range(tiles):
                        lanes = slice((x * tiles + t) * LANES, (x * tiles + t + 1) * LANES)
                        inner[row : row + half, :] = ref[y * half : (y + 1) * half, lanes]
                        row += half
                for sub in range(3):
                    for z in range(2):
                        for c in range(2):
                            tile = (2 * (2 * x + z) + c) * 3 + sub
                            row = ((3 * z + sub) * 2 + c) * half
                            feeds[0, row : row + half, :] = up_ref[
                                y * half : (y + 1) * half, tile * LANES : (tile + 1) * LANES
                            ]
                    for t in range(3):
                        row = (3 * sub + t) * unit
                        start = sub * LANES + y * unit
                        lanes = slice((3 * x + t) * LANES, (3 * x + t + 1) * LANES)
                        feeds[1, row : row + unit, :] = down_ref[start : start + unit, lanes]

            fill(in_ref.at[at], ff_ref.at[at])
            pl.when(at == 0)(lambda: fill(in0_ref, ff0_ref))


def cut(coords, qkv, out, up, down):
    whole = lambda s: pl.BlockSpec(s, lambda i, co: (0,) * len(s))
    rows = qkv.shape[0] // 2 * ((qkv.shape[1] + out.shape[1]) // 2 // LANES)
    shapes = [(4, rows, LANES), (rows, LANES), (4, 2, rows, LANES), (2, rows, LANES)]
    return pl.pallas_call(
        cut_kernel,
        grid_spec=pltpu.PrefetchScalarGridSpec(
            num_scalar_prefetch=1,
            grid=(1,),
            in_specs=[whole(entry.shape) for entry in (qkv, out, up, down)],
            out_specs=[whole(shape) for shape in shapes],
        ),
        out_shape=[jax.ShapeDtypeStruct(shape, bf16) for shape in shapes],
        compiler_params=params(),
        name="cut",
    )(coords, qkv, out, up, down)


def piece_of(parts, q, k):
    own, line, side, up, diagonal = parts
    if isinstance(k, int) and k == 0:
        return own.at[q]
    return (line, side, up, diagonal)[q].at[k - 1]


def qkv_kernel(
    co_ref, h1_ref, b_ref, c_ref, sa_ref, sb_ref,
    p0, p1, p2, p3, p4, r0, r1, r2, r3, r4, o_ref, w_ref, wo_ref,
):
    width = h1_ref.shape[1]
    half = width // 16

    @pl.when(pl.program_id(0) == 0)
    def _():
        for other, parts in enumerate(((p0, p1, p2, p3, p4), (r0, r1, r2, r3, r4))):


            def fill(k, other=other, parts=parts):
                for q in range(4):
                    ref = piece_of(parts, q, k)
                    shard = (k ^ co_ref[3]) * 2 + (other ^ co_ref[0])
                    row = pl.multiple_of(shard * 2 * half + ((q // 2) ^ co_ref[2]) * half, half)
                    x = (q % 2) ^ co_ref[1]
                    start = 0
                    for target in (w_ref, wo_ref):
                        tiles = target.shape[1] // 2 // LANES
                        for t in range(tiles):
                            lane = pl.multiple_of((x * tiles + t) * LANES, LANES)
                            target[pl.ds(row, half), pl.ds(lane, LANES)] = ref[start : start + half, :]
                            start += half

            fill(0)
            pl.loop(1, 4)(fill)

    h1 = h1_ref[...]
    cosine, ahead, behind = c_ref[...], sa_ref[...], sb_ref[...]
    low = lax.broadcasted_iota(jnp.int32, (1, LANES), 1) < HEAD_DIM

    def turn(y):
        return y * cosine - pltpu.roll(y * ahead, LANES - 8, 1) - pltpu.roll(y * behind, 8, 1)

    for part in range(3):
        cols = slice(part * width, (part + 1) * width)
        y = nn(h1, w_ref[:, cols]) + b_ref[:, cols]
        for pair in range(2):
            base = pair * 3 * LANES
            t0 = y[:, base : base + LANES]
            t1 = y[:, base + LANES : base + 2 * LANES]
            t2 = y[:, base + 2 * LANES : base + 3 * LANES]
            queries = turn(jnp.where(low, t0, t1)) * (HEAD_DIM**-0.5)
            keys = turn(pltpu.roll(jnp.where(low, t2, t0), HEAD_DIM, 1))
            at = (2 * part + pair) * LANES
            o_ref[:, at : at + LANES] = queries.astype(bf16)
            o_ref[:, width + at : width + at + LANES] = keys.astype(bf16)
            o_ref[:, 2 * width + at : 2 * width + at + LANES] = jnp.where(low, t1, t2).astype(bf16)


def qkv_forward(coords, h1, bias, tables, pieces, rows=256):
    count, width = h1.shape
    block = lambda n: pl.BlockSpec((rows, n), lambda i, co: (i, 0))
    whole = lambda s: pl.BlockSpec(s, lambda i, co: (0,) * len(s))
    arrays = [entry for part in pieces for entry in part]
    return pl.pallas_call(
        qkv_kernel,
        grid_spec=pltpu.PrefetchScalarGridSpec(
            num_scalar_prefetch=1,
            grid=(count // rows,),
            in_specs=[block(width), fixed(bias.shape)]
            + [block(LANES)] * 3
            + [fixed(entry.shape) for entry in arrays],
            out_specs=[block(3 * width), whole((width, 3 * width)), whole((width, width))],
        ),
        out_shape=[
            jax.ShapeDtypeStruct((count, 3 * width), bf16),
            jax.ShapeDtypeStruct((width, 3 * width), bf16),
            jax.ShapeDtypeStruct((width, width), bf16),
        ],
        compiler_params=params(),
        cost_estimate=pl.CostEstimate(
            flops=6 * count * width * width, bytes_accessed=18 * 2**20, transcendentals=0
        ),
        name="qkv_forward",
    )(coords, h1, bias, *tables[:3], *arrays)


def rotary_tables(count):
    half = ROT_DIM // 2
    lane = lax.broadcasted_iota(jnp.int32, (1, LANES), 1) % HEAD_DIM
    row = lax.broadcasted_iota(jnp.int32, (half, 1), 0)
    inverse = lambda at: 10000.0 ** (-(2 * (at % half)).astype(f32) / ROT_DIM)
    angles = lax.broadcasted_iota(jnp.int32, (count, 1), 0).astype(f32) * inverse(lane)
    turned = lax.broadcasted_iota(jnp.int32, (1, count), 1).astype(f32) * inverse(row)
    cosine, sine = jnp.cos(angles), jnp.sin(angles)
    return (
        jnp.where(lane < ROT_DIM, cosine, 1.0),
        jnp.where((lane >= half) & (lane < ROT_DIM), sine, 0.0),
        jnp.where(lane < half, -sine, 0.0),
        jnp.cos(turned),
        jnp.sin(turned),
    )


def attention_kernel(
    q_ref, k_ref, v_ref, cot_ref, w_ref, c_ref, sa_ref, sb_ref, ct_ref, st_ref,
    a_ref, dqkv_ref, da_ref, qt_ref, dat_ref, dq, dkt, dvt, *, rows,
):
    count = q_ref.shape[0]
    blocks = count // rows
    low = lax.broadcasted_iota(jnp.int32, (1, LANES), 1) < HEAD_DIM
    causal = lax.broadcasted_iota(jnp.int32, (rows, rows), 1) <= lax.broadcasted_iota(
        jnp.int32, (rows, rows), 0
    )
    da_ref[...] = nt(cot_ref[...], w_ref[...]).astype(bf16)
    qt_ref[...] = q_ref[...].T
    dat_ref[...] = da_ref[...].T

    def products(i, h):
        here, past = slice(i * rows, (i + 1) * rows), slice(0, i * rows)
        mine = low if h == 0 else jnp.logical_not(low)
        q, da = q_ref[here, :], da_ref[here, :]
        q = jnp.where(mine, q, jnp.zeros_like(q))
        da = jnp.where(mine, da, jnp.zeros_like(da))
        s_here, d_here = nt(q, k_ref[here, :]), nt(da, v_ref[here, :])
        if not i:
            return [s_here], [d_here]
        return [s_here, nt(q, k_ref[past, :])], [d_here, nt(da, v_ref[past, :])]

    def rest(i, h, scores, grads):
        here, past = slice(i * rows, (i + 1) * rows), slice(0, i * rows)
        head = slice(HEAD_DIM * h, HEAD_DIM * (h + 1))
        spans = (here, past)[: len(scores)]
        scores = [jnp.where(causal, scores[0], -1e30)] + scores[1:]
        highest = jnp.max(scores[0], -1, keepdims=True)
        for s in scores[1:]:
            highest = jnp.maximum(highest, jnp.max(s, -1, keepdims=True))
        raised = [jnp.exp(s - highest) for s in scores]
        inverse = 1.0 / sum(jnp.sum(e, -1, keepdims=True) for e in raised)
        probs = [e * inverse for e in raised]
        row_dot = sum(jnp.sum(p * d, -1, keepdims=True) for p, d in zip(probs, grads))
        out, grad = 0.0, 0.0
        for span, p, d in zip(spans, probs, grads):
            weights = p.astype(bf16)
            ds = (p * (d - row_dot)).astype(bf16)
            out = out + nn(weights, v_ref[span, :])
            grad = grad + nn(ds, k_ref[span, :])
            dk, dv = nn(qt_ref[head, here], ds), nn(dat_ref[head, here], weights)
            if i == blocks - 1:
                dkt[head, span], dvt[head, span] = dk, dv
            else:
                dkt[head, span] += dk
                dvt[head, span] += dv
        return out, grad

    units = [(i, h) for i in reversed(range(blocks)) for h in range(2)]
    ready = products(*units[0])
    results = {}
    for at, unit in enumerate(units):
        now = ready
        if at + 1 < len(units):
            ready = products(*units[at + 1])
        results[unit] = rest(*unit, *now)
        i, h = unit
        if h == 1:
            here = slice(i * rows, (i + 1) * rows)
            first, second = results.pop((i, 0)), results.pop((i, 1))
            a_ref[here, :] = jnp.where(low, first[0], second[0]).astype(bf16)
            y = jnp.where(low, first[1], second[1]) * (HEAD_DIM**-0.5)
            dq[here, :] = (
                y * c_ref[here, :]
                + pltpu.roll(y * sa_ref[here, :], LANES - 8, 1)
                + pltpu.roll(y * sb_ref[here, :], 8, 1)
            )
    cosine, sine = ct_ref[...], st_ref[...]
    for h in range(2):
        one = slice(HEAD_DIM * h, HEAD_DIM * h + 8)
        two = slice(HEAD_DIM * h + 8, HEAD_DIM * h + 16)
        first, second = dkt[one, :], dkt[two, :]
        dkt[one, :] = first * cosine + second * sine
        dkt[two, :] = second * cosine - first * sine
    gk = dkt[...].astype(bf16).T
    gv = dvt[...].astype(bf16).T
    gq = dq[...].astype(bf16)
    gk = jnp.concatenate([gk[:, HEAD_DIM:], gk[:, :HEAD_DIM]], 1)
    dqkv_ref[:, 0:LANES] = jnp.where(low, gq, gk)
    dqkv_ref[:, LANES : 2 * LANES] = jnp.where(low, gv, gq)
    dqkv_ref[:, 2 * LANES : 3 * LANES] = jnp.where(low, gk, gv)


def attention(qkv, cot, out_weight, tables, rows=256):
    count, width = cot.shape
    pairs = width // LANES
    column = lambda offset: pl.BlockSpec((count, LANES), lambda p: (0, offset + p))
    return pl.pallas_call(
        functools.partial(attention_kernel, rows=rows),
        grid=(pairs,),
        in_specs=[column(0), column(pairs), column(2 * pairs), fixed((count, width))]
        + [pl.BlockSpec((LANES, width), lambda p: (p, 0))]
        + [fixed((count, LANES))] * 3
        + [fixed((8, count))] * 2,
        out_specs=[column(0), pl.BlockSpec((count, 3 * LANES), lambda p: (0, p))],
        out_shape=[
            jax.ShapeDtypeStruct((count, width), bf16),
            jax.ShapeDtypeStruct((count, 3 * width), bf16),
        ],
        scratch_shapes=[
            pltpu.VMEM((count, LANES), bf16),
            pltpu.VMEM((LANES, count), bf16),
            pltpu.VMEM((LANES, count), bf16),
            pltpu.VMEM((count, LANES), f32),
            pltpu.VMEM((LANES, count), f32),
            pltpu.VMEM((LANES, count), f32),
        ],
        compiler_params=params(),
        cost_estimate=pl.CostEstimate(
            flops=30 * 10**9, bytes_accessed=20 * 2**20, transcendentals=8 * 10**6
        ),
        name="attention",
    )(qkv, qkv, qkv, cot, out_weight, *tables)


def feed_kernel(
    co_ref, h2_ref, h2t_ref, cot_ref, cott_ref, upb_ref, acc0_ref, before_ref,
    p0, p1, p2, p3, p4, r0, r1, r2, r3, r4, e0, e1, e2, e3, e4, f0, f1, f2, f3, f4,
    mix_ref, k0_ref, s0_ref, k1_ref, s1_ref, ubg_ref, dh2_ref, sq_ref, up_ref, down_ref, us, ds, g_ref, du_ref, *acc,
):
    j = pl.program_id(0)
    side, sub = j % 2, j // 2
    rows = up_ref.shape[0] // 16
    unit = LANES // 2
    x_here = side ^ co_ref[1]
    acc_ref = acc[0] if acc else mix_ref

    @pl.when(j == 0)
    def _():
        acc_ref[...] = acc0_ref[...]
        dh2_ref[...] = jnp.zeros_like(dh2_ref) if before_ref is None else before_ref[...]
        sq_ref[...] = jnp.zeros_like(sq_ref)

    def fill_up(x, k):
        for other, parts in enumerate(((p0, p1, p2, p3, p4), (r0, r1, r2, r3, r4))):
            for y in range(2):
                ref = piece_of(parts, 2 * y + x, k)
                shard = (k ^ co_ref[3]) * 2 + (other ^ co_ref[0])
                row = pl.multiple_of((2 * shard + (y ^ co_ref[2])) * rows, rows)
                for t in range(4):
                    up_ref[pl.ds(row, rows), t * LANES : (t + 1) * LANES] = ref[
                        0, t // 2, 0, (t % 2) * rows : (t % 2 + 1) * rows, :
                    ]

    for x in range(2):

        @pl.when(x_here == x)
        def _(x=x):
            fill_up(x, 0)
            pl.loop(1, 4)(lambda k: fill_up(x, k))


    def fill_down(k):
        z = k ^ co_ref[3]
        for other, parts in enumerate(((e0, e1, e2, e3, e4), (f0, f1, f2, f3, f4))):
            first = (2 * (z % 2) + (other ^ co_ref[0])) * LANES
            for q in range(4):
                ref = piece_of(parts, q, k)
                row = pl.multiple_of(first + ((q // 2) ^ co_ref[2]) * unit, unit)
                for t in range(3):
                    lane = pl.multiple_of((((q % 2) ^ co_ref[1]) * 3 + t) * LANES, LANES)
                    down_ref[pl.ds(row, unit), pl.ds(lane, LANES)] = ref[0, t * unit : (t + 1) * unit, :]

    pl.when(co_ref[3] // 2 == side)(lambda: fill_down(0))

    @pl.loop(1, 4)
    def _(k):
        pl.when((k ^ co_ref[3]) // 2 == side)(lambda: fill_down(k))


    part = g_ref.shape[0] // 2
    ubg_ref[...] = jnp.zeros_like(ubg_ref)

    @pl.loop(0, 2)
    def _(at):
        here = pl.ds(pl.multiple_of(at * part, part), part)
        u = nn(h2_ref[here, :], up_ref[...]) + upb_ref[...]
        act = nt(cot_ref[here, :], down_ref[...])
        cdf = 0.5 * (1.0 + lax.erf(u * math.sqrt(0.5)))
        pdf = jnp.exp(-0.5 * u * u) * (1.0 / math.sqrt(2.0 * math.pi))
        g = (u * cdf).astype(bf16)
        du = (act * (cdf + u * pdf)).astype(bf16)
        g_ref[here, :] = g
        du_ref[here, :] = du
        ubg_ref[...] += jnp.sum(du.astype(f32), 0, keepdims=True)
        acc_ref[here, :] += nn(g, down_ref[...])
        dh2_ref[here, :] += nt(du, up_ref[...])

    bias_grad = ubg_ref[...]
    up_grad = nn(h2t_ref[...], du_ref[...])
    us[...] = up_grad.astype(bf16)
    down_grad = nn(cott_ref[...], g_ref[...])
    ds[...] = down_grad.astype(bf16)
    refs = (k0_ref, s0_ref, k1_ref, s1_ref)
    for x in range(2):
        put_rows(us, x, (2 * sub + side) * 2 * rows, co_ref, refs, tiles=(2 * x, 2 * x + 1))
    first = pl.num_programs(0) * 2 * rows

    def put_down(c, pair):
        for z in range(2):
            tile = 2 * z + c
            for x in range(2):
                for y in range(2):
                    ref, s2 = (pair[x], y) if c == 0 else (pair[y], x)
                    for t in range(3):
                        start = ((x ^ co_ref[1]) * 3 + t) * LANES + (y ^ co_ref[2]) * unit
                        to = pl.ds(pl.multiple_of(first + (3 * sub + t) * unit, unit), unit)
                        ref[s2, z_at(2 * side + z, co_ref), to, :] = ds[
                            pl.ds(pl.multiple_of(start, unit), unit), tile * LANES : (tile + 1) * LANES
                        ]

    for c in range(2):
        pl.when(co_ref[0] == c)(functools.partial(put_down, c, refs[:2]))
        pl.when(co_ref[0] != c)(functools.partial(put_down, c, refs[2:]))
    sq_ref[0:1, :] += fold(
        jnp.sum(up_grad * up_grad + down_grad * down_grad, 0, keepdims=True)
        + bias_grad * bias_grad
    )
    if not acc:
        return

    @pl.when(j == pl.num_programs(0) - 1)
    def _():
        row = lax.broadcasted_iota(jnp.int32, (mix_ref.shape[0], 1), 0)
        mix_ref[...] = jnp.where(row < co_ref[4], acc_ref[...], 0.0).astype(bf16)


def feed(coords, h2, h2t, cot, cott, up_bias, acc, before, pieces, first, subs):
    count, width = h2.shape
    tile = 4 * LANES
    hidden = 2 * subs * tile
    rows = width // 16
    last = before is not None
    piece = jax.ShapeDtypeStruct((2, 4, subs * (4 * rows + 3 * LANES // 2), LANES), bf16)
    up_pieces = [
        [entry.reshape(*entry.shape[:2], 2, 3, 2 * rows, LANES) for entry in part] for part in pieces
    ]
    up_spec = lambda n: pl.BlockSpec(
        (n, 1, 2, 1, 2 * rows, LANES), lambda j, co: (0, 0, 0, first + j // 2, 0, 0)
    )
    down_spec = lambda n: pl.BlockSpec(
        (n, 1, 3 * LANES // 2, LANES), lambda j, co: (0, 1, first + j // 2, 0)
    )
    up_parts = [up_spec(4)] + [up_spec(3)] * 4
    down_parts = [down_spec(4)] + [down_spec(3)] * 4
    up_arrays = [entry for part in up_pieces for entry in part]
    arrays = [entry for part in pieces for entry in part]
    whole = lambda s: pl.BlockSpec(s, lambda j, co: (0,) * len(s))
    start = [before] if last else []
    kernel = feed_kernel
    if not last:
        kernel = lambda *refs: feed_kernel(*refs[:7], None, *refs[7:])
    return pl.pallas_call(
        kernel,
        grid_spec=pltpu.PrefetchScalarGridSpec(
            num_scalar_prefetch=1,
            grid=(2 * subs,),
            in_specs=[
                fixed((count, width)),
                fixed((width, count)),
                fixed((count, width)),
                fixed((width, count)),
                pl.BlockSpec((1, tile), lambda j, co: (0, 2 * first + j)),
                fixed((count, width)),
            ]
            + [fixed((count, width))] * len(start)
            + up_parts * 2
            + down_parts * 2,
            out_specs=[whole((count, width))]
            + [whole(piece.shape)] * 4
            + [
                pl.BlockSpec((1, tile), lambda j, co: (0, j)),
                whole((count, width)),
                whole((8, LANES)),
            ],
            scratch_shapes=[
                pltpu.VMEM((width, tile), bf16),
                pltpu.VMEM((tile, width), bf16),
                pltpu.VMEM((width, tile), bf16),
                pltpu.VMEM((width, tile), bf16),
                pltpu.VMEM((count, tile), bf16),
                pltpu.VMEM((count, tile), bf16),
            ]
            + [pltpu.VMEM((count, width), f32)] * len(start),
        ),
        out_shape=[jax.ShapeDtypeStruct((count, width), bf16 if last else f32)]
        + [piece] * 4
        + [
            jax.ShapeDtypeStruct((1, hidden), f32),
            jax.ShapeDtypeStruct((count, width), f32),
            jax.ShapeDtypeStruct((8, LANES), f32),
        ],
        compiler_params=params(),
        cost_estimate=pl.CostEstimate(
            flops=12 * count * width * hidden,
            bytes_accessed=12 * subs * 2**20,
            transcendentals=2 * count * hidden,
        ),
        name="feed",
    )(coords, h2, h2t, cot, cott, up_bias, acc, *start, *up_arrays, *arrays)


def inner_kernel(
    co_ref, h1t_ref, dqkv_ref, w_ref, heads_ref, cot_ref, x_ref, wo_ref, ob_ref,
    k0_ref, s0_ref, k1_ref, s1_ref, bias_ref, cotsum_ref, dh1_ref, acc_ref, sq_ref, scr,
):
    j = pl.program_id(0)
    inner = j < pl.num_programs(0) - 1

    @pl.when(j == 0)
    def _():
        sq_ref[...] = jnp.zeros_like(sq_ref)

    @pl.when(inner)
    def _():
        right = dqkv_ref[...]
        grad = nn(h1t_ref[...], right)
        scr[...] = grad.astype(bf16)
        bias_grad = jnp.sum(right.astype(f32), 0, keepdims=True)
        bias_ref[...] = bias_grad
        part = nt(right, w_ref[...])

        @pl.when(j == 0)
        def _():
            dh1_ref[...] = part

        @pl.when(j > 0)
        def _():
            dh1_ref[...] += part

        sq_ref[0:1, :] += fold(jnp.sum(grad * grad, 0, keepdims=True) + bias_grad * bias_grad)

    @pl.when(jnp.logical_not(inner))
    def _():
        right = cot_ref[...]
        grad = tn(heads_ref[...], right)
        scr[...] = grad.astype(bf16)
        bias_grad = jnp.sum(right.astype(f32), 0, keepdims=True)
        cotsum_ref[...] = bias_grad
        acc_ref[...] = x_ref[...].astype(f32) + nn(heads_ref[...], wo_ref[...]) + ob_ref[...]
        sq_ref[0:1, :] += fold(jnp.sum(grad * grad, 0, keepdims=True) + 2.0 * bias_grad * bias_grad)

    half = scr.shape[1] // LANES // 2
    for x in range(2):
        tiles = range(x * half, (x + 1) * half)
        put_rows(scr, x, 0, co_ref, (k0_ref, s0_ref, k1_ref, s1_ref), (0,), tiles)


def inner_grads(coords, h1t, dqkv, weight, heads, cot, x, out_weight, out_bias):
    count, width = heads.shape
    cols = dqkv.shape[1]
    tile = width
    steps = cols // tile + 1
    inner = lambda j: jnp.minimum(j, steps - 2)
    piece = jax.ShapeDtypeStruct((2, 4, steps, tile // LANES // 2 * width // 16, LANES), bf16)
    spec = pl.BlockSpec((2, 4, 1) + piece.shape[3:], lambda j, co: (0, 0, j, 0, 0))
    outer_block = lambda r: fixed((r, tile))
    outer_out = lambda r: pl.BlockSpec((r, tile), lambda j, co: (0, 0))
    return pl.pallas_call(
        inner_kernel,
        grid_spec=pltpu.PrefetchScalarGridSpec(
            num_scalar_prefetch=1,
            grid=(steps,),
            in_specs=[
                fixed((width, count)),
                pl.BlockSpec((count, tile), lambda j, co: (0, inner(j))),
                pl.BlockSpec((width, tile), lambda j, co: (0, inner(j))),
                fixed((count, width)),
                outer_block(count),
                outer_block(count),
                outer_block(width),
                outer_block(1),
            ],
            out_specs=[spec] * 4
            + [
                pl.BlockSpec((1, tile), lambda j, co: (0, inner(j))),
                outer_out(1),
                pl.BlockSpec((count, width), lambda j, co: (0, 0)),
                outer_out(count),
                pl.BlockSpec((8, LANES), lambda j, co: (0, 0)),
            ],
            scratch_shapes=[pltpu.VMEM((width, tile), bf16)],
        ),
        out_shape=[piece] * 4
        + [
            jax.ShapeDtypeStruct((1, cols), f32),
            jax.ShapeDtypeStruct((1, width), f32),
            jax.ShapeDtypeStruct((count, width), f32),
            jax.ShapeDtypeStruct((count, width), f32),
            jax.ShapeDtypeStruct((8, LANES), f32),
        ],
        compiler_params=params(),
        cost_estimate=pl.CostEstimate(
            flops=16 * count * width * width, bytes_accessed=24 * 2**20, transcendentals=0
        ),
        name="inner_grads",
    )(coords, h1t, dqkv, weight, heads, cot, x, out_weight, out_bias)


def combine_kernel(scale_ref, co_ref, *refs, vectors):
    pieces, out_ref = refs[:4], refs[-1]
    weigh = lambda parts: sum(scale_ref[at] * part.astype(f32) for at, part in enumerate(parts)).astype(bf16)
    rows = pieces[0].shape[2]
    out_ref[0, :rows] = weigh([ref[0, 0] for ref in pieces])
    if vectors:
        owner = 2 * z_of(pl.program_id(0), co_ref) + co_ref[0]
        out_ref[0, rows:] = weigh([ref[pl.ds(owner, 1)][0] for ref in refs[4:8]])


def combine(scales, coords, s2, arrays, vectors=()):
    rows = arrays[0].shape[2]
    extra = vectors[0].shape[1] if vectors else 0
    return pl.pallas_call(
        functools.partial(combine_kernel, vectors=bool(vectors)),
        grid_spec=pltpu.PrefetchScalarGridSpec(
            num_scalar_prefetch=2,
            grid=(4,),
            in_specs=[pl.BlockSpec((1, 1, rows, LANES), lambda i, s, co: (s2, i, 0, 0))] * 4
            + [fixed(entry.shape) for entry in vectors],
            out_specs=pl.BlockSpec((1, rows + extra, LANES), lambda i, s, co: (i, 0, 0)),
        ),
        out_shape=jax.ShapeDtypeStruct((4, rows + extra, LANES), bf16),
        compiler_params=params(12),
        cost_estimate=pl.CostEstimate(
            flops=10**7, bytes_accessed=40 * rows * LANES, transcendentals=0
        ),
        name="combine",
    )(scales, coords, *arrays, *vectors)


def pack_kernel(ln_ref, qkv_ref, cot_ref, ub1_ref, ub2_ref, out_ref, row_ref):
    out_ref[...] = jnp.zeros_like(out_ref)
    for f in range(8):
        to = 0
        sources = [ln_ref.at[i : i + 1] for i in range(4)] + [qkv_ref, cot_ref]
        for ref in sources:
            size = ref.shape[1] // 8
            row_ref[f : f + 1, to : to + size] = ref[:, f * size : (f + 1) * size]
            to += size
        for sub in range(3):
            ref, at = (ub1_ref, 8 * sub + f) if sub < 2 else (ub2_ref, f)
            row_ref[f : f + 1, to : to + LANES] = ref[:, at * LANES : (at + 1) * LANES]
            to += LANES
        for row in range(row_ref.shape[1] // LANES):
            out_ref[f, row : row + 1, :] = row_ref[f : f + 1, row * LANES : (row + 1) * LANES]


def pack(*arrays):
    whole = lambda s: pl.BlockSpec(s, lambda i: (0,) * len(s))
    width = (4 * arrays[0].shape[1] + sum(entry.shape[1] for entry in arrays[1:])) // 8
    rows = -(-width // LANES // 16) * 16
    return pl.pallas_call(
        pack_kernel,
        grid=(1,),
        in_specs=[whole(entry.shape) for entry in arrays],
        out_specs=whole((8, rows, LANES)),
        out_shape=jax.ShapeDtypeStruct((8, rows, LANES), f32),
        scratch_shapes=[pltpu.VMEM((8, width), f32)],
        compiler_params=params(),
        name="pack",
    )(*arrays)


def finish_kernel(co_ref, *refs):
    groups = refs[0:4], refs[4:8], refs[8:12]
    gq_ref, go_ref, gu_ref, gd_ref = refs[12:16]
    vector_refs, row_ref = refs[16:-4], refs[-1]
    half = gq_ref.shape[0] // 2
    unit = LANES // 2
    for group, parts, scr in zip(range(3), groups, refs[-4:-1]):
        for at, part in enumerate(parts):
            scr[((at // 2) ^ co_ref[2]) * 2 + ((at % 2) ^ co_ref[1])] = part[...]
        for y in range(2):
            rows = slice(y * half, (y + 1) * half)
            for x in range(2):
                owner = 2 * y + x
                if group == 0:
                    for window in range(4):
                        for t in range(3):
                            at = (window * 3 + t) * half
                            value = scr[owner, at : at + half, :].astype(f32)
                            ref, tile = gq_ref, (2 * window + x) * 3 + t
                            if window == 3:
                                ref, tile = go_ref, x * 3 + t
                            ref[rows, tile * LANES : (tile + 1) * LANES] = value
                    continue
                for i in range(2 // group):
                    sub = 2 * (group - 1) + i
                    for z in range(2):
                        for c in range(2):
                            at = ((2 * i + z) * 2 + c) * half
                            tile = (2 * (2 * z + x) + c) * 3 + sub
                            gu_ref[rows, tile * LANES : (tile + 1) * LANES] = scr[
                                owner, at : at + half, :
                            ].astype(f32)
        if group == 0:
            continue
        for i in range(2 // group):
            sub = 2 * (group - 1) + i
            for x in range(2):
                for t in range(3):
                    at = 4 * (2 // group) * half + (3 * i + t) * unit
                    block = jnp.concatenate([scr[2 * y + x, at : at + unit, :] for y in range(2)], 0)
                    lanes = slice((3 * x + t) * LANES, (3 * x + t + 1) * LANES)
                    gd_ref[sub * LANES : (sub + 1) * LANES, lanes] = block.astype(f32).T
    rows = -(-row_ref.shape[1] // LANES // 16) * 16
    sums = scr[0, scr.shape[1] - rows :, :].astype(f32)
    for at in range(row_ref.shape[1] // LANES):
        row_ref[:, at * LANES : (at + 1) * LANES] = sums[at : at + 1]
    start = 0
    for ref in vector_refs[:-1]:
        ref[...] = row_ref[:, start : start + ref.shape[1]]
        start += ref.shape[1]
    vector_refs[-1][...] = vector_refs[-3][...]


def finish(coords, groups, shapes):
    whole = lambda s: pl.BlockSpec(s, lambda i, co: (0,) * len(s))
    arrays = [entry for group in groups for entry in group]
    return pl.pallas_call(
        finish_kernel,
        grid_spec=pltpu.PrefetchScalarGridSpec(
            num_scalar_prefetch=1,
            grid=(1,),
            in_specs=[whole(entry.shape) for entry in arrays],
            out_specs=[whole(s) for s in shapes],
            scratch_shapes=[pltpu.VMEM((4,) + group[0].shape, bf16) for group in groups]
            + [pltpu.VMEM((1, sum(s[1] for s in shapes[4:-1])), f32)],
        ),
        out_shape=[jax.ShapeDtypeStruct(s, f32) for s in shapes],
        compiler_params=params(24),
        name="finish",
    )(coords, *arrays)


def norm_back_kernel(x_ref, cot_ref, dh1_ref, dh2_ref, ln_ref, dx_ref, sums_ref):
    x = x_ref[...].astype(f32)
    centred = x - jnp.mean(x, -1, keepdims=True)
    inverse = lax.rsqrt(jnp.mean(centred * centred, -1, keepdims=True) + 1e-05)
    normed = centred * inverse
    dh1, dh2 = dh1_ref[...], dh2_ref[...]
    scaled = dh1 * ln_ref[0:1, :] + dh2 * ln_ref[2:3, :]
    spread = (
        scaled
        - jnp.mean(scaled, -1, keepdims=True)
        - normed * jnp.mean(scaled * normed, -1, keepdims=True)
    )
    dx_ref[...] = cot_ref[...].astype(f32) + inverse * spread

    @pl.when(pl.program_id(0) == 0)
    def _():
        sums_ref[...] = jnp.zeros_like(sums_ref)

    for row, value in enumerate((dh1 * normed, dh1, dh2 * normed, dh2)):
        sums_ref[row : row + 1, :] += jnp.sum(value, 0, keepdims=True)


def norm_back(x, cot, dh1, dh2, ln, rows=256):
    count, width = x.shape
    block = pl.BlockSpec((rows, width), lambda i: (i, 0))
    return pl.pallas_call(
        norm_back_kernel,
        grid=(count // rows,),
        in_specs=[block] * 4 + [fixed(ln.shape)],
        out_specs=[block, pl.BlockSpec((8, width), lambda i: (0, 0))],
        out_shape=[
            jax.ShapeDtypeStruct((count, width), f32),
            jax.ShapeDtypeStruct((8, width), f32),
        ],
        compiler_params=params(),
        cost_estimate=pl.CostEstimate(
            flops=30 * count * width, bytes_accessed=12 * 2**20, transcendentals=0
        ),
        name="norm_back",
    )(x, cot, dh1, dh2, ln)


def body(
    tokens_in, ln1_gain, ln1_bias, ln2_gain, ln2_bias, qkv_weight, qkv_bias, out_weight, out_bias,
    up_weight, up_bias, down_weight, down_bias, cotangent, lengths, assignment, clip_bound,
):
    dp, fsdp = lax.axis_size("dp"), lax.axis_size("fsdp")
    both = ("dp", "fsdp")
    total = dp * fsdp
    fast = (dp, fsdp) == (4, 8)
    me = lax.axis_index("dp") * fsdp + lax.axis_index("fsdp")

    def swap(value, even, odd=None):
        pairs = [(i, i ^ (even if odd is None or i % 2 == 0 else odd)) for i in range(total)]
        return lax.ppermute(value, both, pairs)

    width = tokens_in.shape[2]
    smalls = (ln1_gain, ln1_bias, ln2_gain, ln2_bias, qkv_bias, out_bias, up_bias, down_bias)
    packed = jnp.concatenate(smalls)
    if fast:
        slot = lax.broadcasted_iota(jnp.int32, (fsdp, 1), 0) == lax.axis_index("fsdp")
        rows = jnp.where(slot, packed[None, :], jnp.zeros_like(packed)[None, :])
        for at in range(3):
            rows = rows + swap(rows, 2**at)
    else:
        rows = lax.all_gather(packed, "fsdp", axis=0)
    vectors, start = [], 0
    for entry in smalls:
        stop = start + entry.shape[0]
        vectors.append(rows[:, start:stop].reshape(1, -1).astype(f32))
        start = stop
    ln = jnp.concatenate(vectors[:4] + [jnp.zeros((4, vectors[0].shape[1]), f32)], 0)
    qkv_b, out_b, up_b, down_b = vectors[4:]

    spot = [me & 1, (me >> 3) & 1, (me >> 4) & 1, (me >> 1) & 3] if fast else [0 * me] * 4
    coords = jnp.stack(spot + [lengths[0]]).astype(jnp.int32)
    if fast:
        in_own, in_mine, ff_own, ff_mine = cut(coords, qkv_weight, out_weight, up_weight, down_weight)
        lines = []
        for piece in (in_mine, ff_mine):
            lines.append([swap(piece, 2 * k) for k in (1, 2, 3)])
        gathered = []
        for own, line in ((in_own, lines[0]), (ff_own, lines[1])):
            line = lax.optimization_barrier(jnp.stack(line))
            mine = [own, line] + [swap(line, 8 * way) for way in (1, 2, 3)]
            theirs = [swap(entry, 1) for entry in mine]
            gathered.append((mine, theirs))
    else:
        whole = [
            lax.all_gather(w, "fsdp", axis=0, tiled=True)
            for w in (qkv_weight, out_weight, up_weight, down_weight)
        ]
        flat = lambda w: w.reshape(4, 2, 2, w.shape[0] // 16, 2, -1, LANES).transpose(
            0, 1, 2, 4, 5, 3, 6
        ).reshape(4, 2, 4, -1, LANES)
        qkv_p, out_p, up_p = (flat(w) for w in whole[:3])
        down_p = whole[3].reshape(4, 2, 3, 2, LANES // 2, 2, 3, LANES).transpose(0, 1, 3, 5, 2, 6, 4, 7)
        down_p = down_p.reshape(up_p.shape)
        up_p = up_p.reshape(4, 2, 4, 2, 2, 3, width // 16, LANES).swapaxes(4, 5).reshape(up_p.shape)
        gathered = []
        for entry in (jnp.concatenate([qkv_p, out_p], 3), jnp.stack([up_p, down_p], 3)):
            gathered.append(
                tuple([entry[0, c]] + [entry[1:, c, q] for q in range(4)] for c in range(2))
            )

    tokens = tokens_in[0]
    count, width = tokens.shape
    tables = rotary_tables(count)
    h1, h2, h1t, h2t, cot, cott = prepare(lengths, tokens, cotangent[0], ln)
    qkv, w_qkv, w_out = qkv_forward(coords, h1, qkv_b, tables, gathered[0])
    heads, dqkv = attention(qkv, cot, w_out, tables)
    *in_pieces, qkv_bias_grad, cot_sum, dh1, acc, in_sq = inner_grads(
        coords, h1t, dqkv, w_qkv, heads, cot, tokens, w_out, out_b + down_b
    )
    up_b = up_b.reshape(8, 3, LANES).swapaxes(0, 1).reshape(1, -1)
    ff = (coords, h2, h2t, cot, cott, up_b)
    acc, *f1_pieces, ub_grad1, dh2, f1_sq = feed(*ff, acc, None, gathered[1], 0, 2)
    mixed, *f2_pieces, ub_grad2, dh2, f2_sq = feed(*ff, acc, dh2, gathered[1], 2, 1)
    groups = []
    for pieces in (in_pieces, f1_pieces, f2_pieces):
        kept, sent, kept_other, sent_other = (entry.reshape(2, 4, -1, LANES) for entry in pieces)
        if fast:
            sent, sent_other = swap(sent, 8, 16), swap(sent_other, 16, 8)
            kept_other, sent_other = swap(kept_other, 1), swap(sent_other, 1)
        groups.append((kept, sent, kept_other, sent_other))
    dx, ln_sums = norm_back(tokens, cot, dh1, dh2, ln)
    ln_grads = ln_sums[:4]

    squares = jnp.sum(in_sq + f1_sq + f2_sq) + jnp.sum(ln_grads * ln_grads)
    slots = jnp.arange(total, dtype=jnp.int32)
    facts = jnp.stack([squares, assignment[0].astype(f32)])[:, None]
    facts = jnp.where(slots[None, :] == me, facts, 0.0)
    if fast:
        facts = facts + swap(facts, 1)
        packed = pack(ln_sums, qkv_bias_grad, cot_sum, ub_grad1, ub_grad2)
        vectors = [packed, swap(packed, 8, 16)]
        facts = facts + swap(facts, 8) + swap(facts, 16) + swap(facts, 24)
        vectors += [swap(packed, 1), swap(packed, 17, 9)]
        facts = facts + swap(facts, 2) + swap(facts, 4) + swap(facts, 6)
    else:
        facts = lax.psum(facts, both)
    norms, numbers = jnp.sqrt(facts[0]), facts[1].astype(jnp.int32)
    ahead = (norms[None, :] < norms[:, None]) | (
        (norms[None, :] == norms[:, None]) & (slots[None, :] < slots[:, None])
    )
    rank = jnp.sum(ahead.astype(jnp.int32), 1)
    median = jnp.sum(jnp.where(rank == total // 2, norms, 0.0))
    bound = median * clip_bound[0].astype(f32) / 8.0
    slot_scale = jnp.minimum(1.0, bound / (norms + 1e-06))
    clip_scale = jnp.sum(jnp.where(numbers[None, :] == slots[:, None], slot_scale[None, :], 0.0), 1)
    if fast:
        next_slot = me ^ jnp.where(me % 2 == 0, 8, 16)
        sources = jnp.stack([me, next_slot, me ^ 1, next_slot ^ 1])
    else:
        sources = jnp.stack([me] * 4)
    own_scales = jnp.sum(jnp.where(slots[None, :] == sources[:, None], slot_scale[None, :], 0.0), 1)
    own = own_scales[0]
    scales = own_scales / total
    share = scales[0]
    sizes = [ln1_gain.shape[0]] * 4 + [qkv_bias.shape[0], out_bias.shape[0], up_bias.shape[0]]

    if fast:
        finals, kepts = [], []
        for arrays, more in zip(groups, ((), (), vectors)):
            sent = combine(scales, coords, 1, arrays, more)
            kepts.append(swap(sent, 16, 8))
        for name, arrays, came, more in zip("abc", groups, kepts, ((), (), vectors)):
            kept = combine(scales, coords, 0, arrays, more)
            add = lambda at, *more: sum((e.astype(f32) for e in more), kept[at].astype(f32) + came[at])
            near = swap(add(slice(2, 4)).astype(bf16), 2)
            sent = add(1, near[1]).astype(bf16)
            last = swap(sent, 4)
            line = add(0, near[0], last).astype(bf16)
            along_x, along_y = swap(line, 8), swap(line, 16)
            turn = (along_y, 8) if name == "b" else (along_x, 16)
            finals.append((line, along_x, along_y, swap(*turn)))
        own_rows = width // fsdp
        hidden = up_b.shape[1]
        shapes = [(own_rows, 3 * width), (own_rows, width), (own_rows, hidden)]
        shapes.append((hidden // fsdp, width))
        shapes += [(1, size) for size in sizes + sizes[5:6]]
        gq, go, gu, gd, *parts = finish(coords, finals, shapes)
        parts = [entry.reshape(-1) for entry in parts]
    else:
        up_bias_grad = jnp.concatenate([ub_grad1, ub_grad2], 1).reshape(3, 8, LANES).swapaxes(0, 1)
        vector_grads = [ln_grads[i] for i in range(4)] + [qkv_bias_grad, cot_sum, up_bias_grad]
        vector_grads = jnp.concatenate([entry.reshape(fsdp, -1) for entry in vector_grads], 1)
        vector_grads = lax.psum(vector_grads * share, both)
        own_row = lax.dynamic_index_in_dim(vector_grads, lax.axis_index("fsdp"), 0, keepdims=False)
        parts, start = [], 0
        for size in sizes:
            parts.append(own_row[start : start + size])
            start += size
        parts.append(parts[5])

        def plain(arrays):
            kept, sent, kept_other, sent_other = (
                entry.reshape(2, 2, 2, -1, LANES).swapaxes(1, 2).reshape(entry.shape)
                for entry in arrays
            )
            return jnp.stack([jnp.stack([kept, sent]), jnp.stack([kept_other, sent_other], 1)])

        half = width // 16
        inner = plain(groups[0]).reshape(2, 2, 2, 4, 4, 3, half, LANES)
        flat = lambda e: e.transpose(3, 0, 2, 6, 4, 1, 5, 7).reshape(width, -1)
        outs = [flat(inner[:, :, :, :, :3]), flat(inner[:, :, :, :, 3:])]
        ups, downs = [], []
        for entry in groups[1:]:
            up, down = jnp.split(plain(entry), 2, 4)
            ups.append(up.reshape(2, 2, 2, 4, -1, 2, 2, half, LANES))
            downs.append(down.reshape(2, 2, 2, 4, -1, 3, LANES // 2, LANES))
        up, down = jnp.concatenate(ups, 4), jnp.concatenate(downs, 4)
        outs.append(up.transpose(3, 0, 2, 7, 5, 1, 6, 4, 8).reshape(width, -1))
        outs.append(down.transpose(3, 0, 4, 7, 1, 5, 2, 6).reshape(-1, width))
        outs = [(entry.astype(f32) * share).astype(bf16) for entry in outs]
        gq, go, gu, gd = (
            lax.psum(
                lax.psum_scatter(w, "fsdp", scatter_dimension=0, tiled=True).astype(f32), "dp"
            )
            for w in outs
        )

    tokens_grad = (own * dx).astype(bf16)[None]
    g1, b1, g2, b2, gqb, gob, gub, gdb = parts
    return (mixed[None], tokens_grad, clip_scale, g1, b1, g2, b2, gq, gqb, go, gob, gu, gub, gd, gdb)


def solution(mesh):
    step = mapped(mesh)
    if dict(mesh.shape) != {"dp": 4, "fsdp": 8}:
        return step
    return step


def mapped(mesh):
    rows, cols, flat = P("fsdp", None), P("fsdp"), P(("dp", "fsdp"))
    slots = P(("dp", "fsdp"), None, None)
    return jax.shard_map(
        body,
        mesh=mesh,
        in_specs=(slots, cols, cols, cols, cols, rows, cols, rows, cols, rows, cols, rows, cols)
        + (slots, flat, flat, P()),
        out_specs=(slots, slots, P(), cols, cols, cols, cols, rows, cols, rows, cols, rows, cols)
        + (rows, cols),
        check_vma=False,
    )
```

```python
import functools
import math

import jax
import jax.numpy as jnp
from jax import lax
from jax.experimental import pallas as pl
from jax.experimental.pallas import tpu as pltpu
from jax.sharding import PartitionSpec as P


HEAD_DIM = 64
ROT_DIM = 16
LANES = 128
f32 = jnp.float32
bf16 = jnp.bfloat16


def nn(left, right):
    return lax.dot_general(left, right, (((1,), (0,)), ((), ())), preferred_element_type=f32)


def nt(left, right):
    return lax.dot_general(left, right, (((1,), (1,)), ((), ())), preferred_element_type=f32)


def tn(left, right):
    return lax.dot_general(left, right, (((0,), (0,)), ((), ())), preferred_element_type=f32)


def fold(row):
    total = row[:, 0:LANES]
    for start in range(LANES, row.shape[1], LANES):
        total = total + row[:, start : start + LANES]
    return total


def fixed(shape):
    return pl.BlockSpec(shape, lambda *_: (0,) * len(shape), pipeline_mode=pl.Buffered(1))


def params(mib=60):
    return pltpu.CompilerParams(vmem_limit_bytes=mib * 2**20)


def z_of(at, coords):
    return ((at % 2) * 2 + at // 2) ^ coords[3]


def z_at(z, coords):
    rel = z ^ coords[3]
    return (rel % 2) * 2 + rel // 2


def put_rows(scr, x, row, coords, refs, extra=(), tiles=None):
    half = scr.shape[0] // 16
    x_rel = x ^ coords[1]

    def put(c, near, pair):
        def one(z):
            shard = z_of(z, coords) * 2 + (c ^ coords[0])
            for y in range(2):
                start = pl.multiple_of((2 * shard + (y ^ coords[2])) * half, half)
                ref, s2 = (pair[0], y) if near else (pair[y], x_rel)
                for t, tile in enumerate(tiles or range(scr.shape[1] // LANES)):
                    to = pl.ds(pl.multiple_of(row + t * half, half), half)
                    ref[(s2, z) + extra + (to, slice(None))] = scr[
                        pl.ds(start, half), tile * LANES : (tile + 1) * LANES
                    ]

        if extra:
            for z in range(4):
                one(z)
        else:
            pl.loop(0, 4)(one)

    for c in range(2):
        kept, sent = refs[2 * c : 2 * c + 2]
        near = coords[0] == c
        pl.when(near & (x_rel == 0))(functools.partial(put, c, True, (kept,)))
        pl.when(near & (x_rel == 1))(functools.partial(put, c, True, (sent,)))
        pl.when(jnp.logical_not(near))(functools.partial(put, c, False, (kept, sent)))


def prepare_kernel(
    len_ref, x_ref, cot_ref, ln_ref, h1_ref, h2_ref, h1t_ref, h2t_ref, cotm_ref, cott_ref
):
    x = x_ref[...].astype(f32)
    centred = x - jnp.mean(x, -1, keepdims=True)
    normed = centred * lax.rsqrt(jnp.mean(centred * centred, -1, keepdims=True) + 1e-05)
    h1 = (normed * ln_ref[0:1, :] + ln_ref[1:2, :]).astype(bf16)
    h2 = (normed * ln_ref[2:3, :] + ln_ref[3:4, :]).astype(bf16)
    row = pl.program_id(0) * x.shape[0] + lax.broadcasted_iota(jnp.int32, (x.shape[0], 1), 0)
    cot = jnp.where(row < len_ref[0], cot_ref[...], jnp.zeros_like(cot_ref[...]))
    h1_ref[...] = h1
    h2_ref[...] = h2
    cotm_ref[...] = cot
    h1t_ref[...] = h1.T
    h2t_ref[...] = h2.T
    cott_ref[...] = cot.T


def prepare(lengths, x, cot, ln, rows=256):
    count, width = x.shape
    block = pl.BlockSpec((rows, width), lambda i, n: (i, 0))
    turned = pl.BlockSpec((width, rows), lambda i, n: (0, i))
    straight = jax.ShapeDtypeStruct((count, width), bf16)
    across = jax.ShapeDtypeStruct((width, count), bf16)
    return pl.pallas_call(
        prepare_kernel,
        grid_spec=pltpu.PrefetchScalarGridSpec(
            num_scalar_prefetch=1,
            grid=(count // rows,),
            in_specs=[block, block, fixed(ln.shape)],
            out_specs=[block, block, turned, turned, block, turned],
        ),
        out_shape=[straight, straight, across, across, straight, across],
        compiler_params=params(),
        cost_estimate=pl.CostEstimate(
            flops=20 * count * width, bytes_accessed=12 * 2**20, transcendentals=0
        ),
        name="prepare",
    )(lengths, x, cot, ln)


def cut_inner_kernel(co_ref, qkv_ref, out_ref, in_ref, in0_ref):
    half = qkv_ref.shape[0] // 2
    for y in range(2):
        for x in range(2):
            at = (y ^ co_ref[2]) * 2 + (x ^ co_ref[1])

            def fill(inner):
                row = 0
                for ref in (qkv_ref, out_ref):
                    tiles = ref.shape[1] // 2 // LANES
                    for t in range(tiles):
                        lanes = slice((x * tiles + t) * LANES, (x * tiles + t + 1) * LANES)
                        inner[row : row + half, :] = ref[y * half : (y + 1) * half, lanes]
                        row += half

            fill(in_ref.at[at])
            pl.when(at == 0)(lambda: fill(in0_ref))


def cut_feed_kernel(co_ref, up_ref, down_ref, ff_ref, ff0_ref):
    half = up_ref.shape[0] // 2
    unit = LANES // 2
    for y in range(2):
        for x in range(2):
            at = (y ^ co_ref[2]) * 2 + (x ^ co_ref[1])

            def fill(feeds):
                for sub in range(3):
                    for z in range(2):
                        for c in range(2):
                            tile = (2 * (2 * x + z) + c) * 3 + sub
                            row = ((3 * z + sub) * 2 + c) * half
                            feeds[0, row : row + half, :] = up_ref[
                                y * half : (y + 1) * half, tile * LANES : (tile + 1) * LANES
                            ]
                    for t in range(3):
                        row = (3 * sub + t) * unit
                        start = sub * LANES + y * unit
                        lanes = slice((3 * x + t) * LANES, (3 * x + t + 1) * LANES)
                        feeds[1, row : row + unit, :] = down_ref[start : start + unit, lanes]

            fill(ff_ref.at[at])
            pl.when(at == 0)(lambda: fill(ff0_ref))


def cut(kernel, coords, arrays, shape):
    whole = lambda s: pl.BlockSpec(s, lambda i, co: (0,) * len(s))
    shapes = [(4, *shape), shape]
    return pl.pallas_call(
        kernel,
        grid_spec=pltpu.PrefetchScalarGridSpec(
            num_scalar_prefetch=1,
            grid=(1,),
            in_specs=[whole(entry.shape) for entry in arrays],
            out_specs=[whole(entry) for entry in shapes],
        ),
        out_shape=[jax.ShapeDtypeStruct(entry, bf16) for entry in shapes],
        compiler_params=params(),
        name="cut",
    )(coords, *arrays)


def piece_of(parts, q, k):
    own, line, side, up, diagonal = parts
    if isinstance(k, int) and k == 0:
        return own.at[q]
    return (line, side, up, diagonal)[q].at[k - 1]


def qkv_kernel(
    co_ref, h1_ref, b_ref, c_ref, sa_ref, sb_ref,
    p0, p1, p2, p3, p4, r0, r1, r2, r3, r4, o_ref, w_ref, wo_ref,
):
    width = h1_ref.shape[1]
    half = width // 16

    @pl.when(pl.program_id(0) == 0)
    def _():
        for other, parts in enumerate(((p0, p1, p2, p3, p4), (r0, r1, r2, r3, r4))):


            def fill(k, other=other, parts=parts):
                for q in range(4):
                    ref = piece_of(parts, q, k)
                    shard = (k ^ co_ref[3]) * 2 + (other ^ co_ref[0])
                    row = pl.multiple_of(shard * 2 * half + ((q // 2) ^ co_ref[2]) * half, half)
                    x = (q % 2) ^ co_ref[1]
                    start = 0
                    for target in (w_ref, wo_ref):
                        tiles = target.shape[1] // 2 // LANES
                        for t in range(tiles):
                            lane = pl.multiple_of((x * tiles + t) * LANES, LANES)
                            target[pl.ds(row, half), pl.ds(lane, LANES)] = ref[start : start + half, :]
                            start += half

            fill(0)
            pl.loop(1, 4)(fill)

    h1 = h1_ref[...]
    cosine, ahead, behind = c_ref[...], sa_ref[...], sb_ref[...]
    low = lax.broadcasted_iota(jnp.int32, (1, LANES), 1) < HEAD_DIM

    def turn(y):
        return y * cosine - pltpu.roll(y * ahead, LANES - 8, 1) - pltpu.roll(y * behind, 8, 1)

    for part in range(3):
        cols = slice(part * width, (part + 1) * width)
        y = nn(h1, w_ref[:, cols]) + b_ref[:, cols]
        for pair in range(2):
            base = pair * 3 * LANES
            t0 = y[:, base : base + LANES]
            t1 = y[:, base + LANES : base + 2 * LANES]
            t2 = y[:, base + 2 * LANES : base + 3 * LANES]
            queries = turn(jnp.where(low, t0, t1)) * (HEAD_DIM**-0.5)
            keys = turn(pltpu.roll(jnp.where(low, t2, t0), HEAD_DIM, 1))
            at = (2 * part + pair) * LANES
            o_ref[:, at : at + LANES] = queries.astype(bf16)
            o_ref[:, width + at : width + at + LANES] = keys.astype(bf16)
            o_ref[:, 2 * width + at : 2 * width + at + LANES] = jnp.where(low, t1, t2).astype(bf16)


def qkv_forward(coords, h1, bias, tables, pieces, rows=256):
    count, width = h1.shape
    block = lambda n: pl.BlockSpec((rows, n), lambda i, co: (i, 0))
    whole = lambda s: pl.BlockSpec(s, lambda i, co: (0,) * len(s))
    arrays = [entry for part in pieces for entry in part]
    return pl.pallas_call(
        qkv_kernel,
        grid_spec=pltpu.PrefetchScalarGridSpec(
            num_scalar_prefetch=1,
            grid=(count // rows,),
            in_specs=[block(width), fixed(bias.shape)]
            + [block(LANES)] * 3
            + [fixed(entry.shape) for entry in arrays],
            out_specs=[block(3 * width), whole((width, 3 * width)), whole((width, width))],
        ),
        out_shape=[
            jax.ShapeDtypeStruct((count, 3 * width), bf16),
            jax.ShapeDtypeStruct((width, 3 * width), bf16),
            jax.ShapeDtypeStruct((width, width), bf16),
        ],
        compiler_params=params(),
        cost_estimate=pl.CostEstimate(
            flops=6 * count * width * width, bytes_accessed=18 * 2**20, transcendentals=0
        ),
        name="qkv_forward",
    )(coords, h1, bias, *tables[:3], *arrays)


def rotary_tables(count):
    half = ROT_DIM // 2
    lane = lax.broadcasted_iota(jnp.int32, (1, LANES), 1) % HEAD_DIM
    row = lax.broadcasted_iota(jnp.int32, (half, 1), 0)
    inverse = lambda at: 10000.0 ** (-(2 * (at % half)).astype(f32) / ROT_DIM)
    angles = lax.broadcasted_iota(jnp.int32, (count, 1), 0).astype(f32) * inverse(lane)
    turned = lax.broadcasted_iota(jnp.int32, (1, count), 1).astype(f32) * inverse(row)
    cosine, sine = jnp.cos(angles), jnp.sin(angles)
    return (
        jnp.where(lane < ROT_DIM, cosine, 1.0),
        jnp.where((lane >= half) & (lane < ROT_DIM), sine, 0.0),
        jnp.where(lane < half, -sine, 0.0),
        jnp.cos(turned),
        jnp.sin(turned),
    )


def attention_kernel(
    q_ref, k_ref, v_ref, cot_ref, w_ref, c_ref, sa_ref, sb_ref, ct_ref, st_ref,
    a_ref, dqkv_ref, da_ref, qt_ref, dat_ref, dq, dkt, dvt, *, rows,
):
    count = q_ref.shape[0]
    blocks = count // rows
    low = lax.broadcasted_iota(jnp.int32, (1, LANES), 1) < HEAD_DIM
    causal = lax.broadcasted_iota(jnp.int32, (rows, rows), 1) <= lax.broadcasted_iota(
        jnp.int32, (rows, rows), 0
    )
    da_ref[...] = nt(cot_ref[...], w_ref[...]).astype(bf16)
    qt_ref[...] = q_ref[...].T
    dat_ref[...] = da_ref[...].T

    def products(i, h):
        here, past = slice(i * rows, (i + 1) * rows), slice(0, i * rows)
        mine = low if h == 0 else jnp.logical_not(low)
        q, da = q_ref[here, :], da_ref[here, :]
        q = jnp.where(mine, q, jnp.zeros_like(q))
        da = jnp.where(mine, da, jnp.zeros_like(da))
        s_here, d_here = nt(q, k_ref[here, :]), nt(da, v_ref[here, :])
        if not i:
            return [s_here], [d_here]
        return [s_here, nt(q, k_ref[past, :])], [d_here, nt(da, v_ref[past, :])]

    def rest(i, h, scores, grads):
        here, past = slice(i * rows, (i + 1) * rows), slice(0, i * rows)
        head = slice(HEAD_DIM * h, HEAD_DIM * (h + 1))
        spans = (here, past)[: len(scores)]
        scores = [jnp.where(causal, scores[0], -1e30)] + scores[1:]
        highest = jnp.max(scores[0], -1, keepdims=True)
        for s in scores[1:]:
            highest = jnp.maximum(highest, jnp.max(s, -1, keepdims=True))
        raised = [jnp.exp(s - highest) for s in scores]
        inverse = 1.0 / sum(jnp.sum(e, -1, keepdims=True) for e in raised)
        probs = [e * inverse for e in raised]
        row_dot = sum(jnp.sum(p * d, -1, keepdims=True) for p, d in zip(probs, grads))
        out, grad = 0.0, 0.0
        for span, p, d in zip(spans, probs, grads):
            weights = p.astype(bf16)
            ds = (p * (d - row_dot)).astype(bf16)
            out = out + nn(weights, v_ref[span, :])
            grad = grad + nn(ds, k_ref[span, :])
            dk, dv = nn(qt_ref[head, here], ds), nn(dat_ref[head, here], weights)
            if i == blocks - 1:
                dkt[head, span], dvt[head, span] = dk, dv
            else:
                dkt[head, span] += dk
                dvt[head, span] += dv
        return out, grad

    units = [(i, h) for i in reversed(range(blocks)) for h in range(2)]
    ready = products(*units[0])
    results = {}
    for at, unit in enumerate(units):
        now = ready
        if at + 1 < len(units):
            ready = products(*units[at + 1])
        results[unit] = rest(*unit, *now)
        i, h = unit
        if h == 1:
            here = slice(i * rows, (i + 1) * rows)
            first, second = results.pop((i, 0)), results.pop((i, 1))
            a_ref[here, :] = jnp.where(low, first[0], second[0]).astype(bf16)
            y = jnp.where(low, first[1], second[1]) * (HEAD_DIM**-0.5)
            dq[here, :] = (
                y * c_ref[here, :]
                + pltpu.roll(y * sa_ref[here, :], LANES - 8, 1)
                + pltpu.roll(y * sb_ref[here, :], 8, 1)
            )
    cosine, sine = ct_ref[...], st_ref[...]
    for h in range(2):
        one = slice(HEAD_DIM * h, HEAD_DIM * h + 8)
        two = slice(HEAD_DIM * h + 8, HEAD_DIM * h + 16)
        first, second = dkt[one, :], dkt[two, :]
        dkt[one, :] = first * cosine + second * sine
        dkt[two, :] = second * cosine - first * sine
    gk = dkt[...].astype(bf16).T
    gv = dvt[...].astype(bf16).T
    gq = dq[...].astype(bf16)
    gk = jnp.concatenate([gk[:, HEAD_DIM:], gk[:, :HEAD_DIM]], 1)
    dqkv_ref[:, 0:LANES] = jnp.where(low, gq, gk)
    dqkv_ref[:, LANES : 2 * LANES] = jnp.where(low, gv, gq)
    dqkv_ref[:, 2 * LANES : 3 * LANES] = jnp.where(low, gk, gv)


def attention(qkv, cot, out_weight, tables, rows=256):
    count, width = cot.shape
    pairs = width // LANES
    column = lambda offset: pl.BlockSpec((count, LANES), lambda p: (0, offset + p))
    return pl.pallas_call(
        functools.partial(attention_kernel, rows=rows),
        grid=(pairs,),
        in_specs=[column(0), column(pairs), column(2 * pairs), fixed((count, width))]
        + [pl.BlockSpec((LANES, width), lambda p: (p, 0))]
        + [fixed((count, LANES))] * 3
        + [fixed((8, count))] * 2,
        out_specs=[column(0), pl.BlockSpec((count, 3 * LANES), lambda p: (0, p))],
        out_shape=[
            jax.ShapeDtypeStruct((count, width), bf16),
            jax.ShapeDtypeStruct((count, 3 * width), bf16),
        ],
        scratch_shapes=[
            pltpu.VMEM((count, LANES), bf16),
            pltpu.VMEM((LANES, count), bf16),
            pltpu.VMEM((LANES, count), bf16),
            pltpu.VMEM((count, LANES), f32),
            pltpu.VMEM((LANES, count), f32),
            pltpu.VMEM((LANES, count), f32),
        ],
        compiler_params=params(),
        cost_estimate=pl.CostEstimate(
            flops=30 * 10**9, bytes_accessed=20 * 2**20, transcendentals=8 * 10**6
        ),
        name="attention",
    )(qkv, qkv, qkv, cot, out_weight, *tables)


def feed_kernel(
    co_ref, h2_ref, h2t_ref, cot_ref, cott_ref, upb_ref, acc0_ref, before_ref,
    p0, p1, p2, p3, p4, r0, r1, r2, r3, r4, e0, e1, e2, e3, e4, f0, f1, f2, f3, f4,
    mix_ref, k0_ref, s0_ref, k1_ref, s1_ref, ubg_ref, dh2_ref, sq_ref, up_ref, down_ref, us, ds, g_ref, du_ref, *acc,
):
    j = pl.program_id(0)
    side, sub = j % 2, j // 2
    rows = up_ref.shape[0] // 16
    unit = LANES // 2
    x_here = side ^ co_ref[1]
    acc_ref = acc[0] if acc else mix_ref

    @pl.when(j == 0)
    def _():
        acc_ref[...] = acc0_ref[...]
        dh2_ref[...] = jnp.zeros_like(dh2_ref) if before_ref is None else before_ref[...]
        sq_ref[...] = jnp.zeros_like(sq_ref)

    def fill_up(x, k):
        for other, parts in enumerate(((p0, p1, p2, p3, p4), (r0, r1, r2, r3, r4))):
            for y in range(2):
                ref = piece_of(parts, 2 * y + x, k)
                shard = (k ^ co_ref[3]) * 2 + (other ^ co_ref[0])
                row = pl.multiple_of((2 * shard + (y ^ co_ref[2])) * rows, rows)
                for t in range(4):
                    up_ref[pl.ds(row, rows), t * LANES : (t + 1) * LANES] = ref[
                        0, t // 2, 0, (t % 2) * rows : (t % 2 + 1) * rows, :
                    ]

    for x in range(2):

        @pl.when(x_here == x)
        def _(x=x):
            fill_up(x, 0)
            pl.loop(1, 4)(lambda k: fill_up(x, k))


    def fill_down(k):
        z = k ^ co_ref[3]
        for other, parts in enumerate(((e0, e1, e2, e3, e4), (f0, f1, f2, f3, f4))):
            first = (2 * (z % 2) + (other ^ co_ref[0])) * LANES
            for q in range(4):
                ref = piece_of(parts, q, k)
                row = pl.multiple_of(first + ((q // 2) ^ co_ref[2]) * unit, unit)
                for t in range(3):
                    lane = pl.multiple_of((((q % 2) ^ co_ref[1]) * 3 + t) * LANES, LANES)
                    down_ref[pl.ds(row, unit), pl.ds(lane, LANES)] = ref[0, t * unit : (t + 1) * unit, :]

    pl.when(co_ref[3] // 2 == side)(lambda: fill_down(0))

    @pl.loop(1, 4)
    def _(k):
        pl.when((k ^ co_ref[3]) // 2 == side)(lambda: fill_down(k))


    part = g_ref.shape[0] // 2
    ubg_ref[...] = jnp.zeros_like(ubg_ref)

    @pl.loop(0, 2)
    def _(at):
        here = pl.ds(pl.multiple_of(at * part, part), part)
        u = nn(h2_ref[here, :], up_ref[...]) + upb_ref[...]
        act = nt(cot_ref[here, :], down_ref[...])
        cdf = 0.5 * (1.0 + lax.erf(u * math.sqrt(0.5)))
        pdf = jnp.exp(-0.5 * u * u) * (1.0 / math.sqrt(2.0 * math.pi))
        g = (u * cdf).astype(bf16)
        du = (act * (cdf + u * pdf)).astype(bf16)
        g_ref[here, :] = g
        du_ref[here, :] = du
        ubg_ref[...] += jnp.sum(du.astype(f32), 0, keepdims=True)
        acc_ref[here, :] += nn(g, down_ref[...])
        dh2_ref[here, :] += nt(du, up_ref[...])

    bias_grad = ubg_ref[...]
    up_grad = nn(h2t_ref[...], du_ref[...])
    us[...] = up_grad.astype(bf16)
    down_grad = nn(cott_ref[...], g_ref[...])
    ds[...] = down_grad.astype(bf16)
    refs = (k0_ref, s0_ref, k1_ref, s1_ref)
    for x in range(2):
        put_rows(us, x, (2 * sub + side) * 2 * rows, co_ref, refs, tiles=(2 * x, 2 * x + 1))
    first = pl.num_programs(0) * 2 * rows

    def put_down(c, pair):
        for z in range(2):
            tile = 2 * z + c
            for x in range(2):
                for y in range(2):
                    ref, s2 = (pair[x], y) if c == 0 else (pair[y], x)
                    for t in range(3):
                        start = ((x ^ co_ref[1]) * 3 + t) * LANES + (y ^ co_ref[2]) * unit
                        to = pl.ds(pl.multiple_of(first + (3 * sub + t) * unit, unit), unit)
                        ref[s2, z_at(2 * side + z, co_ref), to, :] = ds[
                            pl.ds(pl.multiple_of(start, unit), unit), tile * LANES : (tile + 1) * LANES
                        ]

    for c in range(2):
        pl.when(co_ref[0] == c)(functools.partial(put_down, c, refs[:2]))
        pl.when(co_ref[0] != c)(functools.partial(put_down, c, refs[2:]))
    sq_ref[0:1, :] += fold(
        jnp.sum(up_grad * up_grad + down_grad * down_grad, 0, keepdims=True)
        + bias_grad * bias_grad
    )
    if not acc:
        return

    @pl.when(j == pl.num_programs(0) - 1)
    def _():
        row = lax.broadcasted_iota(jnp.int32, (mix_ref.shape[0], 1), 0)
        mix_ref[...] = jnp.where(row < co_ref[4], acc_ref[...], 0.0).astype(bf16)


def feed(coords, h2, h2t, cot, cott, up_bias, acc, before, pieces, first, subs):
    count, width = h2.shape
    tile = 4 * LANES
    hidden = 2 * subs * tile
    rows = width // 16
    last = before is not None
    piece = jax.ShapeDtypeStruct((2, 4, subs * (4 * rows + 3 * LANES // 2), LANES), bf16)
    up_pieces = [
        [entry.reshape(*entry.shape[:2], 2, 3, 2 * rows, LANES) for entry in part] for part in pieces
    ]
    up_spec = lambda n: pl.BlockSpec(
        (n, 1, 2, 1, 2 * rows, LANES), lambda j, co: (0, 0, 0, first + j // 2, 0, 0)
    )
    down_spec = lambda n: pl.BlockSpec(
        (n, 1, 3 * LANES // 2, LANES), lambda j, co: (0, 1, first + j // 2, 0)
    )
    up_parts = [up_spec(4)] + [up_spec(3)] * 4
    down_parts = [down_spec(4)] + [down_spec(3)] * 4
    up_arrays = [entry for part in up_pieces for entry in part]
    arrays = [entry for part in pieces for entry in part]
    whole = lambda s: pl.BlockSpec(s, lambda j, co: (0,) * len(s))
    start = [before] if last else []
    kernel = feed_kernel
    if not last:
        kernel = lambda *refs: feed_kernel(*refs[:7], None, *refs[7:])
    return pl.pallas_call(
        kernel,
        grid_spec=pltpu.PrefetchScalarGridSpec(
            num_scalar_prefetch=1,
            grid=(2 * subs,),
            in_specs=[
                fixed((count, width)),
                fixed((width, count)),
                fixed((count, width)),
                fixed((width, count)),
                pl.BlockSpec((1, tile), lambda j, co: (0, 2 * first + j)),
                fixed((count, width)),
            ]
            + [fixed((count, width))] * len(start)
            + up_parts * 2
            + down_parts * 2,
            out_specs=[whole((count, width))]
            + [whole(piece.shape)] * 4
            + [
                pl.BlockSpec((1, tile), lambda j, co: (0, j)),
                whole((count, width)),
                whole((8, LANES)),
            ],
            scratch_shapes=[
                pltpu.VMEM((width, tile), bf16),
                pltpu.VMEM((tile, width), bf16),
                pltpu.VMEM((width, tile), bf16),
                pltpu.VMEM((width, tile), bf16),
                pltpu.VMEM((count, tile), bf16),
                pltpu.VMEM((count, tile), bf16),
            ]
            + [pltpu.VMEM((count, width), f32)] * len(start),
        ),
        out_shape=[jax.ShapeDtypeStruct((count, width), bf16 if last else f32)]
        + [piece] * 4
        + [
            jax.ShapeDtypeStruct((1, hidden), f32),
            jax.ShapeDtypeStruct((count, width), f32),
            jax.ShapeDtypeStruct((8, LANES), f32),
        ],
        compiler_params=params(),
        cost_estimate=pl.CostEstimate(
            flops=12 * count * width * hidden,
            bytes_accessed=12 * subs * 2**20,
            transcendentals=2 * count * hidden,
        ),
        name="feed",
    )(coords, h2, h2t, cot, cott, up_bias, acc, *start, *up_arrays, *arrays)


def inner_kernel(
    co_ref, h1t_ref, dqkv_ref, w_ref, heads_ref, cot_ref, x_ref, wo_ref, ob_ref,
    k0_ref, s0_ref, k1_ref, s1_ref, bias_ref, cotsum_ref, dh1_ref, acc_ref, sq_ref, scr,
):
    j = pl.program_id(0)
    inner = j < pl.num_programs(0) - 1

    @pl.when(j == 0)
    def _():
        sq_ref[...] = jnp.zeros_like(sq_ref)

    @pl.when(inner)
    def _():
        right = dqkv_ref[...]
        grad = nn(h1t_ref[...], right)
        scr[...] = grad.astype(bf16)
        bias_grad = jnp.sum(right.astype(f32), 0, keepdims=True)
        bias_ref[...] = bias_grad
        part = nt(right, w_ref[...])

        @pl.when(j == 0)
        def _():
            dh1_ref[...] = part

        @pl.when(j > 0)
        def _():
            dh1_ref[...] += part

        sq_ref[0:1, :] += fold(jnp.sum(grad * grad, 0, keepdims=True) + bias_grad * bias_grad)

    @pl.when(jnp.logical_not(inner))
    def _():
        right = cot_ref[...]
        grad = tn(heads_ref[...], right)
        scr[...] = grad.astype(bf16)
        bias_grad = jnp.sum(right.astype(f32), 0, keepdims=True)
        cotsum_ref[...] = bias_grad
        acc_ref[...] = x_ref[...].astype(f32) + nn(heads_ref[...], wo_ref[...]) + ob_ref[...]
        sq_ref[0:1, :] += fold(jnp.sum(grad * grad, 0, keepdims=True) + 2.0 * bias_grad * bias_grad)

    half = scr.shape[1] // LANES // 2
    for x in range(2):
        tiles = range(x * half, (x + 1) * half)
        put_rows(scr, x, 0, co_ref, (k0_ref, s0_ref, k1_ref, s1_ref), (0,), tiles)


def inner_grads(coords, h1t, dqkv, weight, heads, cot, x, out_weight, out_bias):
    count, width = heads.shape
    cols = dqkv.shape[1]
    tile = width
    steps = cols // tile + 1
    inner = lambda j: jnp.minimum(j, steps - 2)
    piece = jax.ShapeDtypeStruct((2, 4, steps, tile // LANES // 2 * width // 16, LANES), bf16)
    spec = pl.BlockSpec((2, 4, 1) + piece.shape[3:], lambda j, co: (0, 0, j, 0, 0))
    outer_block = lambda r: fixed((r, tile))
    outer_out = lambda r: pl.BlockSpec((r, tile), lambda j, co: (0, 0))
    return pl.pallas_call(
        inner_kernel,
        grid_spec=pltpu.PrefetchScalarGridSpec(
            num_scalar_prefetch=1,
            grid=(steps,),
            in_specs=[
                fixed((width, count)),
                pl.BlockSpec((count, tile), lambda j, co: (0, inner(j))),
                pl.BlockSpec((width, tile), lambda j, co: (0, inner(j))),
                fixed((count, width)),
                outer_block(count),
                outer_block(count),
                outer_block(width),
                outer_block(1),
            ],
            out_specs=[spec] * 4
            + [
                pl.BlockSpec((1, tile), lambda j, co: (0, inner(j))),
                outer_out(1),
                pl.BlockSpec((count, width), lambda j, co: (0, 0)),
                outer_out(count),
                pl.BlockSpec((8, LANES), lambda j, co: (0, 0)),
            ],
            scratch_shapes=[pltpu.VMEM((width, tile), bf16)],
        ),
        out_shape=[piece] * 4
        + [
            jax.ShapeDtypeStruct((1, cols), f32),
            jax.ShapeDtypeStruct((1, width), f32),
            jax.ShapeDtypeStruct((count, width), f32),
            jax.ShapeDtypeStruct((count, width), f32),
            jax.ShapeDtypeStruct((8, LANES), f32),
        ],
        compiler_params=params(),
        cost_estimate=pl.CostEstimate(
            flops=16 * count * width * width, bytes_accessed=24 * 2**20, transcendentals=0
        ),
        name="inner_grads",
    )(coords, h1t, dqkv, weight, heads, cot, x, out_weight, out_bias)


def combine_kernel(scale_ref, co_ref, *refs, vectors):
    pieces, out_ref = refs[:4], refs[-1]
    weigh = lambda parts: sum(scale_ref[at] * part.astype(f32) for at, part in enumerate(parts)).astype(bf16)
    rows = pieces[0].shape[2]
    out_ref[0, :rows] = weigh([ref[0, 0] for ref in pieces])
    if vectors:
        owner = 2 * z_of(pl.program_id(0), co_ref) + co_ref[0]
        out_ref[0, rows:] = weigh([ref[pl.ds(owner, 1)][0] for ref in refs[4:8]])


def combine(scales, coords, s2, arrays, vectors=()):
    rows = arrays[0].shape[2]
    extra = vectors[0].shape[1] if vectors else 0
    return pl.pallas_call(
        functools.partial(combine_kernel, vectors=bool(vectors)),
        grid_spec=pltpu.PrefetchScalarGridSpec(
            num_scalar_prefetch=2,
            grid=(4,),
            in_specs=[pl.BlockSpec((1, 1, rows, LANES), lambda i, s, co: (s2, i, 0, 0))] * 4
            + [fixed(entry.shape) for entry in vectors],
            out_specs=pl.BlockSpec((1, rows + extra, LANES), lambda i, s, co: (i, 0, 0)),
        ),
        out_shape=jax.ShapeDtypeStruct((4, rows + extra, LANES), bf16),
        compiler_params=params(12),
        cost_estimate=pl.CostEstimate(
            flops=10**7, bytes_accessed=40 * rows * LANES, transcendentals=0
        ),
        name="combine",
    )(scales, coords, *arrays, *vectors)


def pack_kernel(ln_ref, qkv_ref, cot_ref, ub1_ref, ub2_ref, out_ref, row_ref):
    out_ref[...] = jnp.zeros_like(out_ref)
    for f in range(8):
        to = 0
        sources = [ln_ref.at[i : i + 1] for i in range(4)] + [qkv_ref, cot_ref]
        for ref in sources:
            size = ref.shape[1] // 8
            row_ref[f : f + 1, to : to + size] = ref[:, f * size : (f + 1) * size]
            to += size
        for sub in range(3):
            ref, at = (ub1_ref, 8 * sub + f) if sub < 2 else (ub2_ref, f)
            row_ref[f : f + 1, to : to + LANES] = ref[:, at * LANES : (at + 1) * LANES]
            to += LANES
        for row in range(row_ref.shape[1] // LANES):
            out_ref[f, row : row + 1, :] = row_ref[f : f + 1, row * LANES : (row + 1) * LANES]


def pack(*arrays):
    whole = lambda s: pl.BlockSpec(s, lambda i: (0,) * len(s))
    width = (4 * arrays[0].shape[1] + sum(entry.shape[1] for entry in arrays[1:])) // 8
    rows = -(-width // LANES // 16) * 16
    return pl.pallas_call(
        pack_kernel,
        grid=(1,),
        in_specs=[whole(entry.shape) for entry in arrays],
        out_specs=whole((8, rows, LANES)),
        out_shape=jax.ShapeDtypeStruct((8, rows, LANES), f32),
        scratch_shapes=[pltpu.VMEM((8, width), f32)],
        compiler_params=params(),
        name="pack",
    )(*arrays)


def finish_kernel(co_ref, *refs):
    groups = refs[0:4], refs[4:8], refs[8:12]
    gq_ref, go_ref, gu_ref, gd_ref = refs[12:16]
    vector_refs, row_ref = refs[16:-4], refs[-1]
    half = gq_ref.shape[0] // 2
    unit = LANES // 2
    for group, parts, scr in zip(range(3), groups, refs[-4:-1]):
        for at, part in enumerate(parts):
            scr[((at // 2) ^ co_ref[2]) * 2 + ((at % 2) ^ co_ref[1])] = part[...]
        for y in range(2):
            rows = slice(y * half, (y + 1) * half)
            for x in range(2):
                owner = 2 * y + x
                if group == 0:
                    for window in range(4):
                        for t in range(3):
                            at = (window * 3 + t) * half
                            value = scr[owner, at : at + half, :].astype(f32)
                            ref, tile = gq_ref, (2 * window + x) * 3 + t
                            if window == 3:
                                ref, tile = go_ref, x * 3 + t
                            ref[rows, tile * LANES : (tile + 1) * LANES] = value
                    continue
                for i in range(2 // group):
                    sub = 2 * (group - 1) + i
                    for z in range(2):
                        for c in range(2):
                            at = ((2 * i + z) * 2 + c) * half
                            tile = (2 * (2 * z + x) + c) * 3 + sub
                            gu_ref[rows, tile * LANES : (tile + 1) * LANES] = scr[
                                owner, at : at + half, :
                            ].astype(f32)
        if group == 0:
            continue
        for i in range(2 // group):
            sub = 2 * (group - 1) + i
            for x in range(2):
                for t in range(3):
                    at = 4 * (2 // group) * half + (3 * i + t) * unit
                    block = jnp.concatenate([scr[2 * y + x, at : at + unit, :] for y in range(2)], 0)
                    lanes = slice((3 * x + t) * LANES, (3 * x + t + 1) * LANES)
                    gd_ref[sub * LANES : (sub + 1) * LANES, lanes] = block.astype(f32).T
    rows = -(-row_ref.shape[1] // LANES // 16) * 16
    sums = scr[0, scr.shape[1] - rows :, :].astype(f32)
    for at in range(row_ref.shape[1] // LANES):
        row_ref[:, at * LANES : (at + 1) * LANES] = sums[at : at + 1]
    start = 0
    for ref in vector_refs[:-1]:
        ref[...] = row_ref[:, start : start + ref.shape[1]]
        start += ref.shape[1]
    vector_refs[-1][...] = vector_refs[-3][...]


def finish(coords, groups, shapes):
    whole = lambda s: pl.BlockSpec(s, lambda i, co: (0,) * len(s))
    arrays = [entry for group in groups for entry in group]
    return pl.pallas_call(
        finish_kernel,
        grid_spec=pltpu.PrefetchScalarGridSpec(
            num_scalar_prefetch=1,
            grid=(1,),
            in_specs=[whole(entry.shape) for entry in arrays],
            out_specs=[whole(s) for s in shapes],
            scratch_shapes=[pltpu.VMEM((4,) + group[0].shape, bf16) for group in groups]
            + [pltpu.VMEM((1, sum(s[1] for s in shapes[4:-1])), f32)],
        ),
        out_shape=[jax.ShapeDtypeStruct(s, f32) for s in shapes],
        compiler_params=params(24),
        name="finish",
    )(coords, *arrays)


def norm_back_kernel(x_ref, cot_ref, dh1_ref, dh2_ref, ln_ref, dx_ref, sums_ref):
    x = x_ref[...].astype(f32)
    centred = x - jnp.mean(x, -1, keepdims=True)
    inverse = lax.rsqrt(jnp.mean(centred * centred, -1, keepdims=True) + 1e-05)
    normed = centred * inverse
    dh1, dh2 = dh1_ref[...], dh2_ref[...]
    scaled = dh1 * ln_ref[0:1, :] + dh2 * ln_ref[2:3, :]
    spread = (
        scaled
        - jnp.mean(scaled, -1, keepdims=True)
        - normed * jnp.mean(scaled * normed, -1, keepdims=True)
    )
    dx_ref[...] = cot_ref[...].astype(f32) + inverse * spread

    @pl.when(pl.program_id(0) == 0)
    def _():
        sums_ref[...] = jnp.zeros_like(sums_ref)

    for row, value in enumerate((dh1 * normed, dh1, dh2 * normed, dh2)):
        sums_ref[row : row + 1, :] += jnp.sum(value, 0, keepdims=True)


def norm_back(x, cot, dh1, dh2, ln, rows=256):
    count, width = x.shape
    block = pl.BlockSpec((rows, width), lambda i: (i, 0))
    return pl.pallas_call(
        norm_back_kernel,
        grid=(count // rows,),
        in_specs=[block] * 4 + [fixed(ln.shape)],
        out_specs=[block, pl.BlockSpec((8, width), lambda i: (0, 0))],
        out_shape=[
            jax.ShapeDtypeStruct((count, width), f32),
            jax.ShapeDtypeStruct((8, width), f32),
        ],
        compiler_params=params(),
        cost_estimate=pl.CostEstimate(
            flops=30 * count * width, bytes_accessed=12 * 2**20, transcendentals=0
        ),
        name="norm_back",
    )(x, cot, dh1, dh2, ln)


def body(
    tokens_in, ln1_gain, ln1_bias, ln2_gain, ln2_bias, qkv_weight, qkv_bias, out_weight, out_bias,
    up_weight, up_bias, down_weight, down_bias, cotangent, lengths, assignment, clip_bound,
):
    dp, fsdp = lax.axis_size("dp"), lax.axis_size("fsdp")
    both = ("dp", "fsdp")
    total = dp * fsdp
    fast = (dp, fsdp) == (4, 8)
    me = lax.axis_index("dp") * fsdp + lax.axis_index("fsdp")

    def swap(value, even, odd=None):
        pairs = [(i, i ^ (even if odd is None or i % 2 == 0 else odd)) for i in range(total)]
        return lax.ppermute(value, both, pairs)

    width = tokens_in.shape[2]
    smalls = (ln1_gain, ln1_bias, ln2_gain, ln2_bias, qkv_bias, out_bias, up_bias, down_bias)
    packed = jnp.concatenate(smalls)
    if fast:
        slot = lax.broadcasted_iota(jnp.int32, (fsdp, 1), 0) == lax.axis_index("fsdp")
        rows = jnp.where(slot, packed[None, :], jnp.zeros_like(packed)[None, :])
        for at in range(3):
            rows = rows + swap(rows, 2**at)
    else:
        rows = lax.all_gather(packed, "fsdp", axis=0)
    vectors, start = [], 0
    for entry in smalls:
        stop = start + entry.shape[0]
        vectors.append(rows[:, start:stop].reshape(1, -1).astype(f32))
        start = stop
    ln = jnp.concatenate(vectors[:4] + [jnp.zeros((4, vectors[0].shape[1]), f32)], 0)
    qkv_b, out_b, up_b, down_b = vectors[4:]

    spot = [me & 1, (me >> 3) & 1, (me >> 4) & 1, (me >> 1) & 3] if fast else [0 * me] * 4
    coords = jnp.stack(spot + [lengths[0]]).astype(jnp.int32)
    if fast:
        rows = qkv_weight.shape[0] // 2 * ((qkv_weight.shape[1] + out_weight.shape[1]) // 2 // LANES)
        in_own, in_mine = cut(cut_inner_kernel, coords, (qkv_weight, out_weight), (rows, LANES))
        ff_own, ff_mine = cut(cut_feed_kernel, coords, (up_weight, down_weight), (2, rows, LANES))
        lines = []
        for piece in (in_mine, ff_mine):
            lines.append([swap(piece, 2 * k) for k in (1, 2, 3)])
        gathered = []
        for own, line in ((in_own, lines[0]), (ff_own, lines[1])):
            line = lax.optimization_barrier(jnp.stack(line))
            mine = [own, line] + [swap(line, 8 * way) for way in (1, 2, 3)]
            theirs = [swap(entry, 1) for entry in mine]
            gathered.append((mine, theirs))
    else:
        whole = [
            lax.all_gather(w, "fsdp", axis=0, tiled=True)
            for w in (qkv_weight, out_weight, up_weight, down_weight)
        ]
        flat = lambda w: w.reshape(4, 2, 2, w.shape[0] // 16, 2, -1, LANES).transpose(
            0, 1, 2, 4, 5, 3, 6
        ).reshape(4, 2, 4, -1, LANES)
        qkv_p, out_p, up_p = (flat(w) for w in whole[:3])
        down_p = whole[3].reshape(4, 2, 3, 2, LANES // 2, 2, 3, LANES).transpose(0, 1, 3, 5, 2, 6, 4, 7)
        down_p = down_p.reshape(up_p.shape)
        up_p = up_p.reshape(4, 2, 4, 2, 2, 3, width // 16, LANES).swapaxes(4, 5).reshape(up_p.shape)
        gathered = []
        for entry in (jnp.concatenate([qkv_p, out_p], 3), jnp.stack([up_p, down_p], 3)):
            gathered.append(
                tuple([entry[0, c]] + [entry[1:, c, q] for q in range(4)] for c in range(2))
            )

    tokens = tokens_in[0]
    count, width = tokens.shape
    tables = rotary_tables(count)
    h1, h2, h1t, h2t, cot, cott = prepare(lengths, tokens, cotangent[0], ln)
    qkv, w_qkv, w_out = qkv_forward(coords, h1, qkv_b, tables, gathered[0])
    heads, dqkv = attention(qkv, cot, w_out, tables)
    *in_pieces, qkv_bias_grad, cot_sum, dh1, acc, in_sq = inner_grads(
        coords, h1t, dqkv, w_qkv, heads, cot, tokens, w_out, out_b + down_b
    )
    up_b = up_b.reshape(8, 3, LANES).swapaxes(0, 1).reshape(1, -1)
    ff = (coords, h2, h2t, cot, cott, up_b)
    acc, *f1_pieces, ub_grad1, dh2, f1_sq = feed(*ff, acc, None, gathered[1], 0, 2)
    mixed, *f2_pieces, ub_grad2, dh2, f2_sq = feed(*ff, acc, dh2, gathered[1], 2, 1)
    groups = []
    for pieces in (in_pieces, f1_pieces, f2_pieces):
        kept, sent, kept_other, sent_other = (entry.reshape(2, 4, -1, LANES) for entry in pieces)
        if fast:
            sent, sent_other = swap(sent, 8, 16), swap(sent_other, 16, 8)
            kept_other, sent_other = swap(kept_other, 1), swap(sent_other, 1)
        groups.append((kept, sent, kept_other, sent_other))
    dx, ln_sums = norm_back(tokens, cot, dh1, dh2, ln)
    ln_grads = ln_sums[:4]

    squares = jnp.sum(in_sq + f1_sq + f2_sq) + jnp.sum(ln_grads * ln_grads)
    slots = jnp.arange(total, dtype=jnp.int32)
    facts = jnp.stack([squares, assignment[0].astype(f32)])[:, None]
    facts = jnp.where(slots[None, :] == me, facts, 0.0)
    if fast:
        facts = facts + swap(facts, 1)
        packed = pack(ln_sums, qkv_bias_grad, cot_sum, ub_grad1, ub_grad2)
        vectors = [packed, swap(packed, 8, 16)]
        facts = facts + swap(facts, 2) + swap(facts, 4) + swap(facts, 6)
        vectors += [swap(packed, 1), swap(packed, 17, 9)]
        facts = facts + swap(facts, 8) + swap(facts, 16) + swap(facts, 24)
    else:
        facts = lax.psum(facts, both)
    norms, numbers = jnp.sqrt(facts[0]), facts[1].astype(jnp.int32)
    ahead = (norms[None, :] < norms[:, None]) | (
        (norms[None, :] == norms[:, None]) & (slots[None, :] < slots[:, None])
    )
    rank = jnp.sum(ahead.astype(jnp.int32), 1)
    median = jnp.sum(jnp.where(rank == total // 2, norms, 0.0))
    bound = median * clip_bound[0].astype(f32) / 8.0
    slot_scale = jnp.minimum(1.0, bound / (norms + 1e-06))
    clip_scale = jnp.sum(jnp.where(numbers[None, :] == slots[:, None], slot_scale[None, :], 0.0), 1)
    if fast:
        next_slot = me ^ jnp.where(me % 2 == 0, 8, 16)
        sources = jnp.stack([me, next_slot, me ^ 1, next_slot ^ 1])
    else:
        sources = jnp.stack([me] * 4)
    own_scales = jnp.sum(jnp.where(slots[None, :] == sources[:, None], slot_scale[None, :], 0.0), 1)
    own = own_scales[0]
    scales = own_scales / total
    share = scales[0]
    sizes = [ln1_gain.shape[0]] * 4 + [qkv_bias.shape[0], out_bias.shape[0], up_bias.shape[0]]

    if fast:
        finals, kepts = [], []
        for arrays, more in zip(groups, ((), (), vectors)):
            sent = combine(scales, coords, 1, arrays, more)
            kepts.append(swap(sent, 16, 8))
        for name, arrays, came, more in zip("abc", groups, kepts, ((), (), vectors)):
            kept = combine(scales, coords, 0, arrays, more)
            add = lambda at, *more: sum((e.astype(f32) for e in more), kept[at].astype(f32) + came[at])
            near = swap(add(slice(2, 4)).astype(bf16), 2)
            sent = add(1, near[1]).astype(bf16)
            last = swap(sent, 4)
            line = add(0, near[0], last).astype(bf16)
            along_x, along_y = swap(line, 8), swap(line, 16)
            turn = (along_y, 8) if name == "b" else (along_x, 16)
            finals.append((line, along_x, along_y, swap(*turn)))
        own_rows = width // fsdp
        hidden = up_b.shape[1]
        shapes = [(own_rows, 3 * width), (own_rows, width), (own_rows, hidden)]
        shapes.append((hidden // fsdp, width))
        shapes += [(1, size) for size in sizes + sizes[5:6]]
        gq, go, gu, gd, *parts = finish(coords, finals, shapes)
        parts = [entry.reshape(-1) for entry in parts]
    else:
        up_bias_grad = jnp.concatenate([ub_grad1, ub_grad2], 1).reshape(3, 8, LANES).swapaxes(0, 1)
        vector_grads = [ln_grads[i] for i in range(4)] + [qkv_bias_grad, cot_sum, up_bias_grad]
        vector_grads = jnp.concatenate([entry.reshape(fsdp, -1) for entry in vector_grads], 1)
        vector_grads = lax.psum(vector_grads * share, both)
        own_row = lax.dynamic_index_in_dim(vector_grads, lax.axis_index("fsdp"), 0, keepdims=False)
        parts, start = [], 0
        for size in sizes:
            parts.append(own_row[start : start + size])
            start += size
        parts.append(parts[5])

        def plain(arrays):
            kept, sent, kept_other, sent_other = (
                entry.reshape(2, 2, 2, -1, LANES).swapaxes(1, 2).reshape(entry.shape)
                for entry in arrays
            )
            return jnp.stack([jnp.stack([kept, sent]), jnp.stack([kept_other, sent_other], 1)])

        half = width // 16
        inner = plain(groups[0]).reshape(2, 2, 2, 4, 4, 3, half, LANES)
        flat = lambda e: e.transpose(3, 0, 2, 6, 4, 1, 5, 7).reshape(width, -1)
        outs = [flat(inner[:, :, :, :, :3]), flat(inner[:, :, :, :, 3:])]
        ups, downs = [], []
        for entry in groups[1:]:
            up, down = jnp.split(plain(entry), 2, 4)
            ups.append(up.reshape(2, 2, 2, 4, -1, 2, 2, half, LANES))
            downs.append(down.reshape(2, 2, 2, 4, -1, 3, LANES // 2, LANES))
        up, down = jnp.concatenate(ups, 4), jnp.concatenate(downs, 4)
        outs.append(up.transpose(3, 0, 2, 7, 5, 1, 6, 4, 8).reshape(width, -1))
        outs.append(down.transpose(3, 0, 4, 7, 1, 5, 2, 6).reshape(-1, width))
        outs = [(entry.astype(f32) * share).astype(bf16) for entry in outs]
        gq, go, gu, gd = (
            lax.psum(
                lax.psum_scatter(w, "fsdp", scatter_dimension=0, tiled=True).astype(f32), "dp"
            )
            for w in outs
        )

    tokens_grad = (own * dx).astype(bf16)[None]
    g1, b1, g2, b2, gqb, gob, gub, gdb = parts
    return (mixed[None], tokens_grad, clip_scale, g1, b1, g2, b2, gq, gqb, go, gob, gu, gub, gd, gdb)


def solution(mesh):
    step = mapped(mesh)
    if dict(mesh.shape) != {"dp": 4, "fsdp": 8}:
        return step
    return step


def mapped(mesh):
    rows, cols, flat = P("fsdp", None), P("fsdp"), P(("dp", "fsdp"))
    slots = P(("dp", "fsdp"), None, None)
    return jax.shard_map(
        body,
        mesh=mesh,
        in_specs=(slots, cols, cols, cols, cols, rows, cols, rows, cols, rows, cols, rows, cols)
        + (slots, flat, flat, P()),
        out_specs=(slots, slots, P(), cols, cols, cols, cols, rows, cols, rows, cols, rows, cols)
        + (rows, cols),
        check_vma=False,
    )
```
